32 devices in a mesh: gx: 4 (over y, x), gy: 4 (over z), gz: 2 (over core).
Axes of the slice: x: 2, y: 2, z: 4, core: 2. Of those that a mesh axis runs over, the one named last changes fastest.
Arguments:
- adjoint: float32 [1024, 5, 512], P(('gx', 'gy', 'gz')), may hold values from -6 to 6
- saved: bfloat16 [3, 1024, 5, 512], P(None, ('gx', 'gy', 'gz')), as said below
- inv_jac: float32 [1024], P(('gx', 'gy', 'gz')), may hold values from 0.5 to 2
- stiffness: bfloat16 [3, 512, 512], replicated, may hold values from -0.25 to 0.25
- send_face: int32 [32, 128], P(('gx', 'gy', 'gz')), may hold values from -1 to 191, as said below
- mortar_table: int32 [32, 5, 64], P(('gx', 'gy', 'gz')), may hold values from 0 to 127, as said below
- conf_faces: int32 [32, 2, 16], P(('gx', 'gy', 'gz')), may hold values from 0 to 190, as said below
Outputs:
- adjoint_out: float32 [1024, 5, 512], P(('gx', 'gy', 'gz'))
The draws below stay inside these ranges and needn't reach their ends.
Inputs may be any that keep to these rules, and one draw needn't show every extreme that they name: `saved`: density is 1.0 to 1.4 at every node, each momentum component within 0.6 in magnitude, total energy 2 to 3. `send_face`: row d lists, owner-major, for each of the 8 owners of d's group and each of 16 slots, the local face id (6 times element plus face) sent there, or -1 for an empty slot. Live ids of a device are distinct and differ from its conforming faces. The filled slots toward one owner are its first ones, an even number of them. `mortar_table`: row d holds for each of 64 owned mortars: left received slot, right received slot (slot = source position times 16 plus slot), child position of the left side (0 whole face, 1 to 4 quadrant), normal axis (0 to 2), 1 if live else 0. The left and right slots of all mortars name each received slot once; a mortar is live exactly when both its slots are filled, and then its child is drawn from 0 to 4; dead mortars have child 0. In every group some owner receives all 16 slots filled from every source. `conf_faces`: row d holds 16 local face ids of d's lower side and 16 of its upper side along gz, all distinct; face j of the upper side meets face j of the next device's lower side, cyclically along gz.
All inputs are finite; a program needn't handle non-finite values.
Results may differ from the reference program's by a relative error of at most 0.0014.
Values may be sent and summed in bfloat16 or wider, within the bound.
No kernel may reach another device: no remote copies, remote signals or barrier semaphores. Data moves between devices by JAX's collectives and lax.ppermute only.
A program may use at most 64 MiB of HBM per device.

```python
import math
import jax
import jax.numpy as jnp
from jax import lax

ORDER = 7
SECTIONS = 3
E_DEV = 32
CF = 16
NODES = 512
CAP = 16
ELEMS = 1024
N_GX = 4
N_GY = 4
N_GZ = 2
DEVICES = 32


def connectivity(key):
    owners = N_GY * N_GZ
    slot_count = owners * CAP
    face_total = 6 * E_DEV
    key_heavy, key_forced, key_light, key_faces, key_pairs, key_child, key_axis = jax.random.split(jax.random.fold_in(key, 7771), 7)
    heavy_owner = jax.random.randint(key_heavy, (N_GX, owners), 0, 4) == 0
    forced = jax.random.randint(key_forced, (N_GX, 1), 0, owners)
    owner_ids = jnp.arange(owners)[None, :]
    heavy_owner = heavy_owner | (owner_ids == forced)
    heavy_owner = heavy_owner & (owner_ids != (forced + 1) % owners)
    light_half = jax.random.randint(key_light, (N_GX, owners, owners), 1, max(1, CAP // 4) + 1)
    half_count = jnp.where(heavy_owner[:, :, None], CAP // 2, light_half)
    live_slot = jnp.arange(CAP)[None, None, None, :] < (2 * half_count)[..., None]

    def face_order(sub_key):
        rest = (jax.random.permutation(sub_key, face_total - 3) + 1).astype(jnp.int32)
        return jnp.concatenate([jnp.array([0, face_total - 1, face_total - 2], jnp.int32), rest])
    orders = jax.vmap(face_order)(jax.random.split(key_faces, DEVICES))
    shared = jnp.concatenate([orders[:, 0:1], orders[:, 2:2 * CF + 1]], axis=1).reshape(DEVICES, 2, CF)
    slot_face = jnp.concatenate([orders[:, 1:2], orders[:, 2 * CF + 1:2 * CF + slot_count]], axis=1)
    send_live = jnp.transpose(live_slot, (0, 2, 1, 3)).reshape(DEVICES, slot_count)
    send_face = jnp.where(send_live, slot_face, -1).astype(jnp.int32)
    owner_live = live_slot.reshape(DEVICES, slot_count)
    shuffles = jax.vmap(lambda sub_key: jax.random.permutation(sub_key, slot_count))(jax.random.split(key_pairs, DEVICES)).astype(jnp.int32)
    sort_score = jnp.where(owner_live, shuffles, shuffles + slot_count)
    ranking = jnp.argsort(sort_score, axis=1, stable=True).astype(jnp.int32)
    left_slot = ranking[:, 0::2]
    right_slot = ranking[:, 1::2]
    mortar_live = jnp.take_along_axis(owner_live, left_slot, axis=1).astype(jnp.int32)
    child_pos = jax.random.randint(key_child, left_slot.shape, 0, 5) * mortar_live
    axis_id = jax.random.randint(key_axis, left_slot.shape, 0, 3)
    table = jnp.stack([left_slot, right_slot, child_pos, axis_id, mortar_live], axis=1).astype(jnp.int32)
    return (send_face, table, shared.astype(jnp.int32))


def draw_send_face(key, part):
    return connectivity(key)[0]


def draw_mortar_table(key, part):
    return connectivity(key)[1]


def draw_conf_faces(key, part):
    return connectivity(key)[2]


def draw_saved(key, part):
    key_density, key_momentum, key_energy = jax.random.split(jax.random.fold_in(key, 4099), 3)
    elem_nodes = (ORDER + 1) ** 3
    first = jax.random.uniform(key_density, (SECTIONS, ELEMS, 1, elem_nodes), jnp.float32)
    middle = jax.random.uniform(key_momentum, (SECTIONS, ELEMS, 3, elem_nodes), jnp.float32, -1.0, 1.0)
    last = jax.random.uniform(key_energy, (SECTIONS, ELEMS, 1, elem_nodes), jnp.float32)
    density = 1.0 + 0.4 * first
    momentum = 0.6 * middle
    energy = 2.0 + last
    return jnp.concatenate([density, momentum, energy], axis=2).astype(jnp.bfloat16)


def levels(own_key, dims, cuts, smallest, high):
    def one(dim, parts):
        steps = jax.random.uniform(jax.random.fold_in(jax.random.fold_in(own_key, 6), dim), (parts,), jnp.float32, smallest / len(cuts), high / len(cuts))
        return jnp.repeat(jnp.exp(steps), dims[dim] // parts).reshape((-1,) + (1,) * (len(dims) - dim - 1))

    factor_of = one(*cuts[0])
    for cut in cuts[1:]:
        factor_of = factor_of * one(*cut)
    return factor_of


def gaussian(key, extent, scale, limit, pieces=(), held_as=jnp.bfloat16):
    loudness = levels(key, extent, pieces, -0.22, 0.18) if pieces else 1.0
    drawn = jax.random.normal(key, extent, jnp.float32) * scale * loudness
    return jnp.minimum(jnp.maximum(drawn, -limit), limit).astype(held_as)


def setup_inputs(seed: int = 0) -> dict:
    arg_keys = jax.random.split(jax.random.key(seed), 8)
    return {
        "adjoint": gaussian(arg_keys[0], (ELEMS, 5, NODES), 1.0, 6.0, ((0, 32),), jnp.float32),
        "saved": draw_saved(jax.random.fold_in(arg_keys[7], 71), 0),
        "inv_jac": jnp.clip(jnp.exp(math.log(2.0) - 1.3862944 * jax.random.uniform(arg_keys[2], (ELEMS,), jnp.float32) ** levels(arg_keys[2], (ELEMS,), ((0, 32),), -0.2, 0.2)), 0.5, 2.0),
        "stiffness": gaussian(arg_keys[3], (3, NODES, NODES), NODES ** -0.5, 0.25),
        "send_face": draw_send_face(jax.random.fold_in(arg_keys[7], 71), 0),
        "mortar_table": draw_mortar_table(jax.random.fold_in(arg_keys[7], 71), 0),
        "conf_faces": draw_conf_faces(jax.random.fold_in(arg_keys[7], 71), 0),
    }


gamma_gas = 1.4
penalty = 1.5
viscosity = 0.5
step_size = 0.2
section_weights = (0.25, 0.25, 0.5)

def lagrange_matrix(points, abscissa, line_nodes):
    columns = []
    for target in range(line_nodes):
        column = jnp.ones_like(points)
        for other in range(line_nodes):
            if other != target:
                column = column * (points - abscissa[other]) / (abscissa[target] - abscissa[other])
        columns.append(column)
    return jnp.stack(columns, axis=1)

def projection_tables(line_nodes):
    indices = jnp.arange(line_nodes, dtype=jnp.float32)
    abscissa = -jnp.cos(jnp.pi * indices / (line_nodes - 1))
    halves = [lagrange_matrix((abscissa + 2.0 * half_id - 1.0) * 0.5, abscissa, line_nodes) for half_id in range(2)]
    blocks = [jnp.eye(line_nodes * line_nodes, dtype=jnp.float32)]
    for child_id in range(4):
        blocks.append(jnp.kron(halves[child_id // 2], halves[child_id % 2]))
    forward = jnp.concatenate([matrix.T for matrix in blocks], axis=1)
    backward = jnp.concatenate(blocks, axis=1)
    return (forward, backward)

def restriction_table(line_nodes):
    face_nodes = line_nodes * line_nodes
    column_id = jnp.arange(6 * face_nodes, dtype=jnp.int32)
    face_id = column_id // face_nodes
    local_id = column_id % face_nodes
    first_coord = local_id // line_nodes
    second = local_id % line_nodes
    axis_id = face_id // 2
    fixed_coord = face_id % 2 * (line_nodes - 1)
    coord_x = jnp.where(axis_id == 0, fixed_coord, first_coord)
    coord_y = jnp.where(axis_id == 0, first_coord, jnp.where(axis_id == 1, fixed_coord, second))
    coord_z = jnp.where(axis_id == 2, fixed_coord, second)
    node_id = coord_x * face_nodes + coord_y * line_nodes + coord_z
    elem_nodes = face_nodes * line_nodes
    return (jnp.arange(elem_nodes, dtype=jnp.int32)[:, None] == node_id[None, :]).astype(jnp.float32)

def euler_flux(conserved):
    density = conserved[..., 0:1, :]
    momentum = conserved[..., 1:4, :]
    energy = conserved[..., 4:5, :]
    velocity = momentum / density
    pressure = (gamma_gas - 1.0) * (energy - 0.5 * lax.optimization_barrier(jnp.sum(momentum * velocity, axis=-2, keepdims=True)))
    identity = jnp.eye(3, dtype=conserved.dtype)
    mass_flux = momentum[..., None, :, :]
    moment_flux = momentum[..., :, None, :] * velocity[..., None, :, :] + pressure[..., None, :, :] * identity[:, :, None]
    energy_flux = ((energy + pressure) * velocity)[..., None, :, :]
    return jnp.concatenate([mass_flux, moment_flux, energy_flux], axis=-3)

def normal_adjoint(conserved, weight, normal_pick):

    def normal_flux(values):
        return lax.optimization_barrier(jnp.sum(euler_flux(values) * normal_pick[:, None, :, None], axis=2))
    return jax.vjp(normal_flux, conserved)[1](weight)[0]

def rest_value():
    return jnp.array([1.0, 0.0, 0.0, 0.0, 2.5], jnp.float32)

def face_traces(values, restrict, exact_high):
    element_count = values.shape[0]
    face_nodes = restrict.shape[1] // 6
    flattened = values.reshape(element_count * 5, values.shape[2])
    if exact_high:
        traced = jnp.dot(flattened, restrict, precision=lax.Precision.HIGHEST, preferred_element_type=jnp.float32)
    else:
        traced = jnp.dot(flattened, restrict, preferred_element_type=jnp.float32)
    arranged = jnp.transpose(traced.reshape(element_count, 5, 6, face_nodes), (0, 2, 1, 3))
    return arranged.reshape(element_count * 6, 5 * face_nodes)

def lift_faces(face_grad, lift_table, element_count):
    face_nodes = lift_table.shape[0] // 6
    arranged = jnp.transpose(face_grad.reshape(element_count, 6, 5, face_nodes), (0, 2, 1, 3))
    arranged = arranged.reshape(element_count * 5, 6 * face_nodes)
    lifted = jnp.dot(arranged, lift_table, precision=lax.Precision.HIGHEST, preferred_element_type=jnp.float32)
    return lifted.reshape(element_count, 5, lift_table.shape[1])

def volume_adjoint(lam_block, forward, stiff_rows, stiff_cols):
    element_count = lam_block.shape[0]
    elem_nodes = lam_block.shape[2]
    lam_low = lam_block.astype(jnp.bfloat16).reshape(element_count * 5, elem_nodes)
    slopes = jnp.dot(lam_low, stiff_rows, preferred_element_type=jnp.float32)
    smooth = jnp.dot(slopes.astype(jnp.bfloat16), stiff_cols, preferred_element_type=jnp.float32)
    cotangent = slopes.reshape(element_count, 5, 3, elem_nodes)
    pulled = jax.vjp(euler_flux, forward.astype(jnp.float32))[1](cotangent)[0]
    return pulled - viscosity * smooth.reshape(element_count, 5, elem_nodes)

def mortar_adjoint(lam_recv, state_recv, mortar_rows, project_out, project_in):
    left_slot = mortar_rows[0]
    right_slot = mortar_rows[1]
    child_pos = mortar_rows[2]
    axis_id = mortar_rows[3]
    live_flag = mortar_rows[4]
    mortars = left_slot.shape[0]
    trace_width = lam_recv.shape[1]
    face_nodes = trace_width // 5
    slot_count = lam_recv.shape[0]
    child_pick = (child_pos[:, None] == jnp.arange(5, dtype=jnp.int32)[None, :]).astype(jnp.float32)
    left_side = jnp.stack([lam_recv[left_slot], state_recv[left_slot]], axis=1).astype(jnp.float32)
    left_side = left_side.reshape(mortars * 10, face_nodes)
    spread = jnp.dot(left_side, project_out, precision=lax.Precision.HIGHEST, preferred_element_type=jnp.float32)
    chosen = lax.optimization_barrier(jnp.sum(spread.reshape(mortars, 10, 5, face_nodes) * child_pick[:, None, :, None], axis=2))
    lam_left = chosen[:, :5]
    state_left = chosen[:, 5:]
    lam_right = lam_recv[right_slot].astype(jnp.float32).reshape(mortars, 5, face_nodes)
    state_right = state_recv[right_slot].astype(jnp.float32).reshape(mortars, 5, face_nodes)
    keep_live = (live_flag == 1)[:, None, None]
    rest_state = rest_value()[None, :, None]
    state_left = jnp.where(keep_live, state_left, rest_state)
    state_right = jnp.where(keep_live, state_right, rest_state)
    weight = (lam_right - lam_left) * live_flag.astype(jnp.float32)[:, None, None]
    normal_pick = (axis_id[:, None] == jnp.arange(3, dtype=jnp.int32)[None, :]).astype(jnp.float32)
    pull_left = 0.5 * normal_adjoint(state_left, weight, normal_pick) + 0.5 * penalty * weight
    pull_right = 0.5 * normal_adjoint(state_right, weight, normal_pick) - 0.5 * penalty * weight
    pulled_back = jnp.dot(pull_left.reshape(mortars * 5, face_nodes), project_in, precision=lax.Precision.HIGHEST, preferred_element_type=jnp.float32)
    pulled_back = lax.optimization_barrier(jnp.sum(pulled_back.reshape(mortars, 5, 5, face_nodes) * child_pick[:, None, :, None], axis=2))
    result = jnp.zeros((slot_count, trace_width), jnp.float32)
    result = result.at[left_slot].set(pulled_back.reshape(mortars, trace_width))
    return result.at[right_slot].set(pull_right.reshape(mortars, trace_width))

def conforming_adjoint(payload, own_state, neighbour):
    face_count = payload.shape[1]
    trace_width = payload.shape[2]
    face_nodes = trace_width // 5
    orient = jnp.array([-1.0, 1.0], jnp.float32)[:, None, None, None]
    lam_own = payload.astype(jnp.float32).reshape(2, face_count, 5, face_nodes)
    lam_neighbour = neighbour.astype(jnp.float32).reshape(2, face_count, 5, face_nodes)
    state_own = own_state.astype(jnp.float32).reshape(2 * face_count, 5, face_nodes)
    weight = orient * (lam_neighbour - lam_own)
    normal_pick = jnp.broadcast_to(jnp.array([[0.0, 0.0, 1.0]], jnp.float32), (2 * face_count, 3))
    pulled = normal_adjoint(state_own, weight.reshape(2 * face_count, 5, face_nodes), normal_pick)
    result = 0.5 * pulled.reshape(2, face_count, 5, face_nodes) + 0.5 * penalty * orient * weight
    return result.reshape(2, face_count, trace_width)

def reference(adjoint, saved, inv_jac, stiffness, send_face, mortar_table, conf_faces):
    line_nodes = ORDER + 1
    elem_nodes = line_nodes ** 3
    face_nodes = line_nodes * line_nodes
    trace_width = 5 * face_nodes
    element_count = adjoint.shape[0]
    per_device = element_count // DEVICES
    owners = N_GY * N_GZ
    slot_count = send_face.shape[1]
    capacity = slot_count // owners
    face_count = conf_faces.shape[2]
    restrict = restriction_table(line_nodes)
    restrict_low = restrict.astype(jnp.bfloat16)
    lift_table = restrict.T
    project_out, project_in = projection_tables(line_nodes)
    stiff_rows = jnp.transpose(stiffness, (1, 0, 2)).reshape(elem_nodes, 3 * elem_nodes)
    stiff_cols = jnp.transpose(stiffness, (0, 2, 1)).reshape(3 * elem_nodes, elem_nodes)
    is_live = (send_face >= 0).reshape(-1)
    offsets = (jnp.arange(DEVICES, dtype=jnp.int32) * (per_device * 6)).astype(jnp.int32)
    global_face = (jnp.maximum(send_face, 0) + offsets[:, None]).reshape(-1).astype(jnp.int32)
    global_shared = (conf_faces + offsets[:, None, None]).astype(jnp.int32)
    jacobian = inv_jac[:, None, None]
    lam = adjoint
    for section_id in (2, 1, 0):
        forward = saved[section_id]
        lam_faces = face_traces(lam, restrict, True).astype(jnp.bfloat16)
        state_faces = face_traces(forward, restrict_low, False).astype(jnp.bfloat16)
        face_rows = jnp.concatenate([lam_faces, state_faces], axis=1)
        outgoing = jnp.where(is_live[:, None], face_rows[global_face], jnp.zeros((), jnp.bfloat16))
        outgoing = outgoing.reshape(N_GX, owners, owners, capacity, 2 * trace_width)
        incoming = jnp.transpose(outgoing, (0, 2, 1, 3, 4)).reshape(DEVICES, slot_count, 2 * trace_width)

        def owner_work(item_pair):
            received, owner_rows = item_pair
            return mortar_adjoint(received[:, :trace_width], received[:, trace_width:], owner_rows, project_out, project_in)
        mortar_grads = lax.map(owner_work, (incoming, mortar_table))
        returned = mortar_grads.reshape(N_GX, owners, owners, capacity, trace_width)
        returned = jnp.transpose(returned, (0, 2, 1, 3, 4)).reshape(DEVICES * slot_count, trace_width)
        payload = lam_faces[global_shared]
        own_state = state_faces[global_shared]
        device_grid = payload.reshape(N_GX, N_GY, N_GZ, 2, face_count, trace_width)
        from_below = jnp.roll(device_grid[:, :, :, 1], 1, axis=2)
        from_above = jnp.roll(device_grid[:, :, :, 0], -1, axis=2)
        neighbour = jnp.stack([from_below, from_above], axis=3).reshape(DEVICES, 2, face_count, trace_width)
        shared_grads = jax.vmap(conforming_adjoint)(payload, own_state, neighbour)
        face_grad = jnp.zeros((element_count * 6, trace_width), jnp.float32)
        face_grad = face_grad.at[global_shared.reshape(-1)].add(shared_grads.reshape(-1, trace_width))
        face_grad = face_grad.at[global_face].add(jnp.where(is_live[:, None], returned, 0.0))
        lifted = lift_faces(face_grad, lift_table, element_count)

        def block_work(item_pair):
            return volume_adjoint(item_pair[0], item_pair[1], stiff_rows, stiff_cols)
        volume = lax.map(block_work, (lam.reshape(DEVICES, per_device, 5, elem_nodes), forward.reshape(DEVICES, per_device, 5, elem_nodes)))
        volume = volume.reshape(element_count, 5, elem_nodes)
        lam = lam + step_size * section_weights[section_id] * jacobian * (volume + lifted)
    return lam
```

```python
import functools

import jax
import jax.numpy as jnp
import numpy as np
from jax import lax
from jax.experimental import pallas as pl
from jax.experimental.pallas import tpu as pltpu
from jax.sharding import PartitionSpec as P

ORDER = 7
LINE = ORDER + 1
FACE = LINE * LINE
ELEM = FACE * LINE
PAIRS = 3
TILE = 2 * FACE
WIDTH = PAIRS * TILE

gamma_gas = 1.4
penalty = 1.5
viscosity = 0.5
step_size = 0.2
section_weights = (0.25, 0.25, 0.5)
GM1 = gamma_gas - 1.0
REST = (1.0, 0.0, 0.0, 0.0, 2.5)
F32 = jnp.float32
BF16 = jnp.bfloat16


def lagrange_matrix(points, abscissa):
    out = np.ones((LINE, LINE))
    for target in range(LINE):
        for other in range(LINE):
            if other != target:
                out[:, target] *= (points - abscissa[other]) / (abscissa[target] - abscissa[other])
    return out


def split_low(matrix):
    high = matrix.astype(np.float32).astype(BF16)
    low = (matrix - high.astype(np.float64)).astype(np.float32).astype(BF16)
    return high, low


def projection_tables():
    abscissa = -np.cos(np.pi * np.arange(LINE) / ORDER)
    halves = [lagrange_matrix((abscissa + 2.0 * h - 1.0) * 0.5, abscissa) for h in range(2)]
    children = [np.kron(halves[c // 2], halves[c % 2]) for c in range(4)]
    eye2 = np.eye(2)
    forward = np.concatenate([np.kron(eye2, m.T) for m in children], axis=1)
    backward = np.concatenate([np.kron(eye2, m) for m in children], axis=1)
    fh, fl = split_low(forward)
    bh, bl = split_low(backward)
    return np.concatenate([fh, fl], axis=0), np.concatenate([bh, bh, bl], axis=0)


def restriction_table():
    column = np.arange(6 * FACE)
    face, local = column // FACE, column % FACE
    first, second = local // LINE, local % LINE
    axis, fixed = face // 2, face % 2 * (LINE - 1)
    x = np.where(axis == 0, fixed, first)
    y = np.where(axis == 0, first, np.where(axis == 1, fixed, second))
    z = np.where(axis == 2, fixed, second)
    node = x * FACE + y * LINE + z
    return (np.arange(ELEM)[:, None] == node[None, :]).astype(np.float32).astype(BF16)


def dot(a, b, ca=1, cb=0):
    return lax.dot_general(a, b, (((ca,), (cb,)), ((), ())), preferred_element_type=F32)


def low_lanes(rows):
    return lax.broadcasted_iota(jnp.int32, (rows, TILE), 1) < FACE


def swap(x):
    return pltpu.roll(x, FACE, 1)


def exchange(a, b, low):
    return jnp.where(low, a, swap(b)), jnp.where(low, swap(a), b)


def tiles(x):
    return [x[:, j * TILE : (j + 1) * TILE] for j in range(PAIRS)]


def flux_pull(u, w, picks):
    inv = 1.0 / u[0]
    vel = [u[i] * inv for i in (1, 2, 3)]
    kin = 0.5 * (vel[0] * vel[0] + vel[1] * vel[1] + vel[2] * vel[2])
    enth = gamma_gas * (u[4] * inv) - GM1 * kin
    q = w[1] * vel[0] + w[2] * vel[1] + w[3] * vel[2]
    if picks is None:
        vn, wn = vel[2], w[3]
    else:
        vn = jnp.where(picks[0], vel[0], jnp.where(picks[1], vel[1], vel[2]))
        wn = jnp.where(picks[0], w[1], jnp.where(picks[1], w[2], w[3]))
    r = vn * w[4]
    a = w[0] + q + enth * w[4]
    g = [GM1 * kin * wn - vn * q + (GM1 * kin - enth) * r]
    t = GM1 * (wn + r)
    for i in range(3):
        gi = w[1 + i] * vn - vel[i] * t
        if picks is None:
            gi = gi + a if i == 2 else gi
        else:
            gi = gi + jnp.where(picks[i], a, 0.0)
        g.append(gi)
    g.append(GM1 * wn + gamma_gas * r)
    return g


def face_rows_of(ids_row, elements):
    shape = (6 * elements, ids_row.shape[1])
    row = lax.broadcasted_iota(jnp.int32, shape, 0)
    face = row // elements
    ident = 6 * (row - face * elements) + face
    return jnp.where(ident == ids_row, 1.0, 0.0).astype(BF16)


def trace_faces(field_low, table, elements):
    traced = dot(field_low, table)
    low = low_lanes(elements)
    zero = jnp.zeros((elements, TILE), F32)
    rows = [[None] * PAIRS for _ in range(6)]

    def piece(v, k):
        if v >= 5:
            return zero
        return traced[v * elements : (v + 1) * elements, k * TILE : (k + 1) * TILE]

    for j in range(PAIRS):
        for k in range(3):
            rows[2 * k][j], rows[2 * k + 1][j] = exchange(piece(2 * j, k), piece(2 * j + 1, k), low)
    return jnp.concatenate([jnp.concatenate(r, axis=1) for r in rows], axis=0).astype(BF16)


def lift_faces(face_grad, table, elements):
    low = low_lanes(elements)
    rows = [[None] * 3 for _ in range(6)]

    def piece(f, j):
        return face_grad[f * elements : (f + 1) * elements, j * TILE : (j + 1) * TILE]

    for j in range(PAIRS):
        for k in range(3):
            rows[2 * j][k], rows[2 * j + 1][k] = exchange(piece(2 * k, j), piece(2 * k + 1, j), low)
    arranged = jnp.concatenate([jnp.concatenate(r, axis=1) for r in rows[:5]], axis=0).astype(BF16)
    return dot(arranged, table, 1, 1)


def column_of(row):
    n = row.shape[1]
    same = lax.broadcasted_iota(jnp.int32, (n, n), 0) == lax.broadcasted_iota(jnp.int32, (n, n), 1)
    return jnp.sum(jnp.where(same, jnp.broadcast_to(row, (n, n)), jnp.zeros((), row.dtype)), axis=1, keepdims=True)


def gather_outputs(faces, send_ref, conf_ref, elements):
    out = dot(face_rows_of(send_ref[...], elements), faces, 0, 0).astype(BF16)
    conf = conf_ref[0]
    lower = dot(face_rows_of(conf[0:1], elements), faces, 0, 0).astype(BF16)
    upper = dot(face_rows_of(conf[1:2], elements), faces, 0, 0).astype(BF16)
    return out, lower, upper


def start_kernel(lam_ref, saved_ref, send_ref, conf_ref, table_ref, out_ref, conf_lam_ref, conf_state_ref):
    elements = lam_ref.shape[1]
    sections = saved_ref.shape[0]
    table = table_ref[...]
    owners, rows = out_ref.shape[0], out_ref.shape[1]
    cap = rows // (sections + 1)

    def put(k, value):
        out_ref[:, k * cap : (k + 1) * cap, :] = value.reshape(owners, cap, WIDTH)

    lam_low = lam_ref[...].astype(BF16).reshape(5 * elements, ELEM)
    out, lower, upper = gather_outputs(trace_faces(lam_low, table, elements), send_ref, conf_ref, elements)
    put(0, out)
    conf_lam_ref[0] = lower
    conf_lam_ref[1] = upper
    for s in range(sections):
        state = saved_ref[s].reshape(5 * elements, ELEM)
        out, lower, upper = gather_outputs(trace_faces(state, table, elements), send_ref, conf_ref, elements)
        put(1 + s, out)
        conf_state_ref[s, 0] = lower
        conf_state_ref[s, 1] = upper


def volume_kernel(section, lam_ref, saved_ref, stiff_ref, jac_ref, own_ref, near_ref, state_ref, base_ref, grad_ref, slope_ref, smooth_ref):
    elements = lam_ref.shape[1]
    coef = step_size * section_weights[section]
    lam_low = lam_ref[...].astype(BF16).reshape(5 * elements, ELEM)
    smooth = None
    for d in range(3):
        slopes = dot(lam_low, stiff_ref[d])
        slope_ref[d] = slopes
        part = dot(slopes.astype(BF16), stiff_ref[d], 1, 1)
        smooth = part if smooth is None else smooth + part
    smooth_ref[...] = smooth
    jac = column_of(jac_ref[...]) * coef
    step = 16
    for r in range(0, elements, step):
        scale = jnp.broadcast_to(jac[r : r + step], (step, 128))
        for c in range(0, ELEM, 128):
            u = [saved_ref[section, v, r : r + step, c : c + 128].astype(F32) for v in range(5)]
            inv = 1.0 / u[0]
            vel = [u[i] * inv for i in (1, 2, 3)]
            kin = 0.5 * (vel[0] * vel[0] + vel[1] * vel[1] + vel[2] * vel[2])
            enth = gamma_gas * (u[4] * inv) - GM1 * kin
            trace = run = first = None
            g = [None, None, None, None]
            for d in range(3):
                w = [slope_ref[d, v * elements + r : v * elements + r + step, c : c + 128] for v in range(5)]
                q = w[1] * vel[0] + w[2] * vel[1] + w[3] * vel[2]
                term = vel[d] * q
                first = term if first is None else first + term
                trace = w[1 + d] if trace is None else trace + w[1 + d]
                part = vel[d] * w[4]
                run = part if run is None else run + part
                for i in range(3):
                    gi = w[1 + i] * vel[d]
                    if i == d:
                        gi = gi + (w[0] + q + enth * w[4])
                    g[1 + i] = gi if g[1 + i] is None else g[1 + i] + gi
            t = GM1 * (trace + run)
            pulled = [GM1 * kin * trace - first + (GM1 * kin - enth) * run]
            pulled += [g[1 + i] - vel[i] * t for i in range(3)]
            pulled.append(GM1 * trace + gamma_gas * run)
            for v in range(5):
                rows = slice(v * elements + r, v * elements + r + step)
                vol = pulled[v] - viscosity * smooth_ref[rows, c : c + 128]
                base_ref[v, r : r + step, c : c + 128] = lam_ref[v, r : r + step, c : c + 128] + scale * vol

    faces = own_ref.shape[1]
    low = low_lanes(faces)
    sign = jnp.where(low, -1.0, 1.0)

    def by_variable(ref, index=(), order=(0, 1)):
        lower, upper = (tiles(ref[index + (side,)].astype(F32)) for side in order)
        out = []
        for j in range(PAIRS):
            out += exchange(lower[j], upper[j], low)
        return out[:5]

    own, near, u = by_variable(own_ref), by_variable(near_ref, (), (1, 0)), by_variable(state_ref, (section,))
    w = [sign * (near[v] - own[v]) for v in range(5)]
    g = flux_pull(u, w, None)
    pull = [0.5 * g[v] + (0.5 * penalty) * sign * w[v] for v in range(5)]
    pull.append(jnp.zeros_like(pull[0]))
    for j in range(PAIRS):
        lower, upper = exchange(pull[2 * j], pull[2 * j + 1], low)
        grad_ref[0, :, j * TILE : (j + 1) * TILE] = lower.astype(BF16)
        grad_ref[1, :, j * TILE : (j + 1) * TILE] = upper.astype(BF16)


def mortar_kernel(section, lam_ref, first_ref, map_ref, forward_ref, backward_ref, out_ref):
    owners, cap = out_ref.shape[0], out_ref.shape[1]
    slots = owners * cap
    lam = lam_ref[:, 0:cap, :].reshape(slots, WIDTH)
    state = first_ref[:, (1 + section) * cap : (2 + section) * cap, :].reshape(slots, WIDTH)
    rows = map_ref[0]
    mortars = rows.shape[1]
    slot = lax.broadcasted_iota(jnp.int32, (slots, mortars), 0)
    pick_left = jnp.where(slot == rows[0:1], 1.0, 0.0).astype(BF16)
    pick_right = jnp.where(slot == rows[1:2], 1.0, 0.0).astype(BF16)
    column = [jnp.broadcast_to(column_of(rows[k : k + 1].astype(F32)), (mortars, TILE)) for k in (2, 3, 4)]
    child = [column[0] == float(c) for c in range(5)]
    picks = [column[1] == float(n) for n in range(3)]
    live = column[2]
    alive = live == 1.0
    low = low_lanes(mortars)

    left = tiles(dot(pick_left, lam, 0, 0)) + tiles(dot(pick_left, state, 0, 0))
    right = tiles(dot(pick_right, lam, 0, 0)) + tiles(dot(pick_right, state, 0, 0))

    def choose(raw, spread, j):
        out = raw
        for c in range(4):
            out = jnp.where(child[c + 1], spread[j * mortars : (j + 1) * mortars, c * TILE : (c + 1) * TILE], out)
        return out

    stacked = jnp.concatenate(left, axis=0).astype(BF16)
    spread = dot(jnp.concatenate([stacked, stacked], axis=1), forward_ref[...])
    left = [choose(left[j], spread, j) for j in range(2 * PAIRS)]

    w, u = [], []
    for j in range(PAIRS):
        jump = (right[j] - left[j]) * live
        turned = swap(jump)
        w += [jnp.where(low, jump, turned), jnp.where(low, turned, jump)]
        u += exchange(left[PAIRS + j], right[PAIRS + j], low)
    u = [jnp.where(alive, u[v], REST[v]) for v in range(5)]
    g = flux_pull(u, w[:5], picks)
    side = jnp.where(low, 0.5 * penalty, -0.5 * penalty)
    pull = [0.5 * g[v] + side * w[v] for v in range(5)]
    pull.append(jnp.zeros_like(pull[0]))
    back_left, back_right = [], []
    for j in range(PAIRS):
        a, b = exchange(pull[2 * j], pull[2 * j + 1], low)
        back_left.append(a)
        back_right.append(b)
    stacked = jnp.concatenate(back_left, axis=0)
    high = stacked.astype(BF16)
    rest = (stacked - high.astype(F32)).astype(BF16)
    spread = dot(jnp.concatenate([high, rest, high], axis=1), backward_ref[...])
    back_left = [choose(back_left[j], spread, j) for j in range(PAIRS)]
    grads = dot(pick_left, jnp.concatenate(back_left, axis=1).astype(BF16))
    grads = grads + dot(pick_right, jnp.concatenate(back_right, axis=1).astype(BF16))
    out_ref[...] = grads.astype(BF16).reshape(owners, cap, WIDTH)


def update_of(section, base_ref, back_ref, grad_ref, jac_ref, send_ref, conf_ref, table_ref):
    elements = base_ref.shape[1]
    coef = step_size * section_weights[section]
    slots = send_ref.shape[1]
    conf = conf_ref[0]
    face_grad = dot(face_rows_of(send_ref[...], elements), back_ref[...].reshape(slots, WIDTH))
    face_grad = face_grad + dot(face_rows_of(conf[0:1], elements), grad_ref[0])
    face_grad = face_grad + dot(face_rows_of(conf[1:2], elements), grad_ref[1])
    lifted = lift_faces(face_grad, table_ref[...], elements)
    jac = column_of(jac_ref[...]) * coef
    return [base_ref[v] + jac * lifted[v * elements : (v + 1) * elements] for v in range(5)]


def update_kernel(section, base_ref, back_ref, grad_ref, jac_ref, send_ref, conf_ref, table_ref, lam_ref, out_ref, conf_lam_ref):
    elements = base_ref.shape[1]
    lam = update_of(section, base_ref, back_ref, grad_ref, jac_ref, send_ref, conf_ref, table_ref)
    for v in range(5):
        lam_ref[v] = lam[v]
    lam_low = jnp.concatenate([x.astype(BF16) for x in lam], axis=0)
    out, lower, upper = gather_outputs(trace_faces(lam_low, table_ref[...], elements), send_ref, conf_ref, elements)
    out_ref[...] = out.reshape(out_ref.shape)
    conf_lam_ref[0] = lower
    conf_lam_ref[1] = upper


def final_kernel(section, base_ref, back_ref, grad_ref, jac_ref, send_ref, conf_ref, table_ref, lam_ref):
    lam = update_of(section, base_ref, back_ref, grad_ref, jac_ref, send_ref, conf_ref, table_ref)
    for v in range(5):
        lam_ref[v] = lam[v]


def call(kernel, outs, *args, scratch=()):
    single = not isinstance(outs, (list, tuple))
    shapes = outs if single else [jax.ShapeDtypeStruct(s, t) for s, t in outs]
    return pl.pallas_call(
        kernel,
        out_shape=shapes,
        in_specs=[pl.BlockSpec(memory_space=pltpu.VMEM)] * len(args),
        out_specs=jax.tree.map(lambda _: pl.BlockSpec(memory_space=pltpu.VMEM), shapes),
        scratch_shapes=list(scratch),
    )(*args)


def trade(x):
    return lax.all_to_all(x, ("gy", "gz"), split_axis=0, concat_axis=0, tiled=True)


def neighbours(payload):
    peers = lax.axis_size("gz")
    up = [(i, (i + 1) % peers) for i in range(peers)]
    down = [(j, i) for i, j in up]
    if peers == 2:
        return lax.ppermute(payload, "gz", up)
    below = lax.ppermute(payload[1], "gz", up)
    above = lax.ppermute(payload[0], "gz", down)
    return jnp.stack([above, below], axis=0)


def per_device(adjoint, saved, inv_jac, stiffness, send_face, mortar_table, conf_faces):
    elements = adjoint.shape[0]
    sections = saved.shape[0]
    owners = lax.axis_size("gy") * lax.axis_size("gz")
    cap = send_face.shape[1] // owners
    faces = conf_faces.shape[2]
    table = jnp.asarray(restriction_table())
    forward, backward = (jnp.asarray(t) for t in projection_tables())
    jac = inv_jac.reshape(1, elements)
    S = jax.ShapeDtypeStruct
    lam = jnp.transpose(adjoint, (1, 0, 2))
    states = jnp.transpose(saved, (0, 2, 1, 3))
    rows = S((5, elements, ELEM), F32)
    slots = S((owners, cap, WIDTH), BF16)
    pair = S((2, faces, WIDTH), BF16)

    outgoing, conf_lam, conf_state = call(
        start_kernel,
        [((owners, (sections + 1) * cap, WIDTH), BF16), ((2, faces, WIDTH), BF16), ((sections, 2, faces, WIDTH), BF16)],
        lam, states, send_face, conf_faces, table,
    )
    first = incoming = trade(outgoing)
    for section in (2, 1, 0):
        near = neighbours(conf_lam)
        base, grad = call(
            functools.partial(volume_kernel, section),
            [(rows.shape, F32), (pair.shape, BF16)],
            lam, states, stiffness, jac, conf_lam, near, conf_state,
            scratch=(pltpu.VMEM((3, 5 * elements, ELEM), F32), pltpu.VMEM((5 * elements, ELEM), F32)),
        )
        out = call(functools.partial(mortar_kernel, section), slots, incoming, first, mortar_table, forward, backward)
        back = trade(out)
        shared = (base, back, grad, jac, send_face, conf_faces, table)
        if section:
            lam, outgoing, conf_lam = call(
                functools.partial(update_kernel, section),
                [(rows.shape, F32), (slots.shape, BF16), (pair.shape, BF16)],
                *shared,
            )
            incoming = trade(outgoing)
        else:
            lam = call(functools.partial(final_kernel, section), rows, *shared)
    return jnp.transpose(lam, (1, 0, 2))


def solution(mesh):
    return jax.shard_map(
        per_device,
        mesh=mesh,
        in_specs=(
            P(("gx", "gy", "gz"), None, None),
            P(None, ("gx", "gy", "gz"), None, None),
            P(("gx", "gy", "gz")),
            P(),
            P(("gx", "gy", "gz"), None),
            P(("gx", "gy", "gz"), None, None),
            P(("gx", "gy", "gz"), None, None),
        ),
        out_specs=P(("gx", "gy", "gz"), None, None),
        check_vma=False,
    )
```

```python
import functools

import jax
import jax.numpy as jnp
import numpy as np
from jax import lax
from jax.experimental import pallas as pl
from jax.experimental.pallas import tpu as pltpu
from jax.sharding import PartitionSpec as P

ORDER = 7
LINE = ORDER + 1
FACE = LINE * LINE
ELEM = FACE * LINE
PAIRS = 3
TILE = 2 * FACE
ROWS = 5 * FACE
EXTRA = 16

gamma_gas = 1.4
penalty = 1.5
viscosity = 0.5
step_size = 0.2
section_weights = (0.25, 0.25, 0.5)
GM1 = gamma_gas - 1.0
REST = (1.0, 0.0, 0.0, 0.0, 2.5)
F32 = jnp.float32
VMEM_GRANT = 24 << 20
BF16 = jnp.bfloat16


def lagrange_matrix(points, abscissa):
    out = np.ones((LINE, LINE))
    for target in range(LINE):
        for other in range(LINE):
            if other != target:
                out[:, target] *= (points - abscissa[other]) / (abscissa[target] - abscissa[other])
    return out


def split_low(matrix):
    high = matrix.astype(np.float32).astype(BF16)
    low = (matrix - high.astype(np.float64)).astype(np.float32).astype(BF16)
    return high, low


def projection_tables():
    abscissa = -np.cos(np.pi * np.arange(LINE) / ORDER)
    halves = [lagrange_matrix((abscissa + 2.0 * h - 1.0) * 0.5, abscissa) for h in range(2)]
    children = [np.kron(halves[c // 2], halves[c % 2]) for c in range(4)]
    fh, fl = split_low(np.concatenate(children, axis=0))
    bh, bl = split_low(np.concatenate([m.T for m in children], axis=0))
    return np.concatenate([fh, fl], axis=1), np.concatenate([bh, bh, bl], axis=1)


def restriction_table():
    column = np.arange(6 * FACE)
    face, local = column // FACE, column % FACE
    first, second = local // LINE, local % LINE
    axis, fixed = face // 2, face % 2 * (LINE - 1)
    x = np.where(axis == 0, fixed, first)
    y = np.where(axis == 0, first, np.where(axis == 1, fixed, second))
    z = np.where(axis == 2, fixed, second)
    node = x * FACE + y * LINE + z
    return (np.arange(ELEM)[:, None] == node[None, :]).astype(np.float32).astype(BF16)


def dot(a, b, ca=1, cb=0):
    return lax.dot_general(a, b, (((ca,), (cb,)), ((), ())), preferred_element_type=F32)


def low_lanes(rows):
    return lax.broadcasted_iota(jnp.int32, (rows, TILE), 1) < FACE


def swap(x):
    return pltpu.roll(x, FACE, 1)


def exchange(a, b, low):
    return jnp.where(low, a, swap(b)), jnp.where(low, swap(a), b)


def flux_pull(u, w, picks):
    inv = 1.0 / u[0]
    vel = [u[i] * inv for i in (1, 2, 3)]
    kin = 0.5 * (vel[0] * vel[0] + vel[1] * vel[1] + vel[2] * vel[2])
    enth = gamma_gas * (u[4] * inv) - GM1 * kin
    q = w[1] * vel[0] + w[2] * vel[1] + w[3] * vel[2]
    if picks is None:
        vn, wn = vel[2], w[3]
    else:
        vn = jnp.where(picks[0], vel[0], jnp.where(picks[1], vel[1], vel[2]))
        wn = jnp.where(picks[0], w[1], jnp.where(picks[1], w[2], w[3]))
    r = vn * w[4]
    a = w[0] + q + enth * w[4]
    g = [GM1 * kin * wn - vn * q + (GM1 * kin - enth) * r]
    t = GM1 * (wn + r)
    for i in range(3):
        gi = w[1 + i] * vn - vel[i] * t
        if picks is None:
            gi = gi + a if i == 2 else gi
        else:
            gi = gi + jnp.where(picks[i], a, 0.0)
        g.append(gi)
    g.append(GM1 * wn + gamma_gas * r)
    return g


def trace_faces(field_low, table, elements):
    traced = dot(field_low, table)
    low = low_lanes(elements)
    zero = jnp.zeros((elements, TILE), F32)
    rows = [[None] * PAIRS for _ in range(6)]

    def piece(v, k):
        if v >= 5:
            return zero
        return traced[v * elements : (v + 1) * elements, k * TILE : (k + 1) * TILE]

    for j in range(PAIRS):
        for k in range(3):
            rows[2 * k][j], rows[2 * k + 1][j] = exchange(piece(2 * j, k), piece(2 * j + 1, k), low)
    return jnp.concatenate([jnp.concatenate(r, axis=1) for r in rows], axis=0).astype(BF16)


def lift_slots(grads, hot, table, elements):
    padded = jnp.concatenate([g.astype(BF16) for g in grads] + [jnp.zeros(grads[0].shape, BF16)], axis=0)
    face_grad = dot(hot, padded, 1, 1)
    low = low_lanes(elements)
    rows = [[None] * 3 for _ in range(6)]

    def piece(f, j):
        return face_grad[f * elements : (f + 1) * elements, j * TILE : (j + 1) * TILE]

    for j in range(PAIRS):
        for k in range(3):
            rows[2 * j][k], rows[2 * j + 1][k] = exchange(piece(2 * k, j), piece(2 * k + 1, j), low)
    arranged = jnp.concatenate([jnp.concatenate(r, axis=1) for r in rows[:5]], axis=0).astype(BF16)
    return dot(arranged, table, 1, 1)


def column_of(row):
    n = row.shape[1]
    same = lax.broadcasted_iota(jnp.int32, (n, n), 0) == lax.broadcasted_iota(jnp.int32, (n, n), 1)
    return jnp.sum(jnp.where(same, jnp.broadcast_to(row, (n, n)), 0.0), axis=1, keepdims=True)


def slot_values(field_low, hot, table, elements):
    faces = trace_faces(field_low, table, elements)
    return dot(faces, hot, 0, 0).astype(BF16)[:ROWS]


def start_kernel(lam_ref, send_ref, conf_ref, map_ref, table_ref, out_ref, shared_ref, hot_ref, ids_ref):
    elements = lam_ref.shape[1]
    slots = send_ref.shape[1]
    faces = conf_ref.shape[2]
    ids_ref[...] = jnp.full(ids_ref.shape, -1, jnp.int32)
    ids_ref[0:1, 0:slots] = send_ref[...]
    ids_ref[0:1, slots : slots + faces] = conf_ref[0, 0:1]
    ids_ref[0:1, slots + faces : slots + 2 * faces] = conf_ref[0, 1:2]
    shape = hot_ref.shape
    row = lax.broadcasted_iota(jnp.int32, shape, 0)
    face = row // elements
    ident = 6 * (row - face * elements) + face
    hot = jnp.where(ident == ids_ref[0:1], 1.0, 0.0).astype(BF16)
    hot_ref[...] = hot
    lam_low = lam_ref[...].astype(BF16).reshape(5 * elements, ELEM)
    values = slot_values(lam_low, hot, table_ref[...], elements)
    out_ref[0:ROWS] = values[:, :slots]
    shared_ref[...] = values[:, slots:]
    rows = map_ref[0]
    mortars = rows.shape[1]
    slot = lax.broadcasted_iota(jnp.int32, (slots, mortars), 0)
    field = lax.broadcasted_iota(jnp.int32, (EXTRA, mortars), 0)
    known = jnp.where(field == 1, rows[2:3], jnp.where(field == 2, rows[3:4], jnp.where(field == 3, rows[4:5], 0)))
    info = None
    for mine, other, left in ((0, 1, 1), (1, 0, 0)):
        hits = jnp.where(slot == rows[mine : mine + 1], 1.0, 0.0).astype(BF16)
        fields = jnp.where(field == 0, rows[other : other + 1], jnp.where(field == 4, left, known))
        part = dot(fields.astype(F32).astype(BF16), hits, 1, 1)
        info = part if info is None else info + part
    out_ref[ROWS:] = info.astype(BF16)


def state_kernel(saved_ref, hot_ref, table_ref, out_ref):
    elements = saved_ref.shape[2]
    for s in range(saved_ref.shape[0]):
        out_ref[s] = slot_values(saved_ref[s].reshape(5 * elements, ELEM), hot_ref[...], table_ref[...], elements)


def volume_kernel(section, faces, lam_ref, saved_ref, stiff_ref, jac_ref, own_ref, near_ref, state_ref, hot_ref, table_ref, base_ref, slope_ref, smooth_ref):
    elements = lam_ref.shape[1]
    coef = step_size * section_weights[section]
    lam_low = lam_ref[...].astype(BF16).reshape(5 * elements, ELEM)

    slots = state_ref.shape[2] - own_ref.shape[1]
    width = own_ref.shape[1]
    lane = lax.broadcasted_iota(jnp.int32, (FACE, width), 1)
    used = lane < 2 * faces
    lower = lane < faces
    sign = jnp.where(lower, -1.0, 1.0)
    w, u = [], []
    for v in range(5):
        rows = slice(v * FACE, (v + 1) * FACE)
        near = near_ref[rows].astype(F32)
        near = jnp.where(lower, pltpu.roll(near, width - faces, 1), pltpu.roll(near, faces, 1))
        w.append(jnp.where(used, sign * (near - own_ref[rows].astype(F32)), 0.0))
        u.append(jnp.where(used, state_ref[section, rows, slots:].astype(F32), REST[v]))
    g = flux_pull(u, w, None)
    grads = [0.5 * g[v] + (0.5 * penalty) * sign * w[v] for v in range(5)]
    total = viscosity * -1.0
    smooth = lift_slots(grads, hot_ref[:, slots:], table_ref[...], elements)
    for d in range(3):
        slopes = dot(lam_low, stiff_ref[d])
        slope_ref[d] = slopes
        smooth = smooth + total * dot(slopes.astype(BF16), stiff_ref[d], 1, 1)
    smooth_ref[...] = smooth
    jac = column_of(jac_ref[...]) * coef
    step = 16
    for r in range(0, elements, step):
        scale = jnp.broadcast_to(jac[r : r + step], (step, 128))
        for c in range(0, ELEM, 128):
            u = [saved_ref[section, v, r : r + step, c : c + 128].astype(F32) for v in range(5)]
            inv = 1.0 / u[0]
            vel = [u[i] * inv for i in (1, 2, 3)]
            kin = 0.5 * (vel[0] * vel[0] + vel[1] * vel[1] + vel[2] * vel[2])
            enth = gamma_gas * (u[4] * inv) - GM1 * kin
            trace = run = first = None
            g = [None, None, None, None]
            for d in range(3):
                w = [slope_ref[d, v * elements + r : v * elements + r + step, c : c + 128] for v in range(5)]
                q = w[1] * vel[0] + w[2] * vel[1] + w[3] * vel[2]
                term = vel[d] * q
                first = term if first is None else first + term
                trace = w[1 + d] if trace is None else trace + w[1 + d]
                part = vel[d] * w[4]
                run = part if run is None else run + part
                for i in range(3):
                    gi = w[1 + i] * vel[d]
                    if i == d:
                        gi = gi + (w[0] + q + enth * w[4])
                    g[1 + i] = gi if g[1 + i] is None else g[1 + i] + gi
            t = GM1 * (trace + run)
            pulled = [GM1 * kin * trace - first + (GM1 * kin - enth) * run]
            pulled += [g[1 + i] - vel[i] * t for i in range(3)]
            pulled.append(GM1 * trace + gamma_gas * run)
            for v in range(5):
                rows = slice(v * elements + r, v * elements + r + step)
                vol = pulled[v] + smooth_ref[rows, c : c + 128]
                base_ref[v, r : r + step, c : c + 128] = lam_ref[v, r : r + step, c : c + 128] + scale * vol

def spread_children(matrix, stacked):
    return dot(matrix, jnp.concatenate(stacked, axis=0))


def choose(raw, spread, child, keep=None):
    out = []
    for v, value in enumerate(raw):
        width = value.shape[1]
        picked = value
        for c in range(4):
            hit = child[c] if keep is None else child[c] & keep
            picked = jnp.where(hit, spread[c * FACE : (c + 1) * FACE, v * width : (v + 1) * width], picked)
        out.append(picked)
    return out


def read_table(pieces, me_ref, cap, relative):
    slots = pieces[0].shape[1]
    me = me_ref[0]
    lane = lax.broadcasted_iota(jnp.int32, (EXTRA, slots), 1)
    owner_of = lane // cap
    info = jnp.zeros((EXTRA, slots), F32)
    for p, piece in enumerate(pieces):
        owner = me ^ p if relative else p
        shift = lax.rem((owner - me) * cap + slots, slots)
        moved = pltpu.roll(piece[ROWS:].astype(F32), shift, 1)
        info = jnp.where(owner_of == owner, moved, info)
    info = info.astype(jnp.int32)
    source = info[0:1] // cap
    rank = info[0:1] - source * cap
    if relative:
        source = source ^ me
    code = source * slots + owner_of[0:1] * cap + rank
    field = lax.broadcasted_iota(jnp.int32, (EXTRA, slots), 0)
    return jnp.where(field == 0, code, info)


def mortar_update(section, relative, first, last, count, *refs):
    refs = list(refs)
    pieces = [r[...] for r in refs[:count]]
    own_ref = refs[count]
    base_ref, state_ref, hot_ref, table_ref, jac_ref, forward_ref, backward_ref, me_ref, info_ref = refs[count + 1 : count + 10]
    outs = refs[count + 10 :]
    elements = base_ref.shape[1]
    if len(pieces) == 1 and pieces[0].ndim == 3:
        pieces = [pieces[0][p] for p in range(pieces[0].shape[0])]
    slots = pieces[0].shape[1]
    cap = slots // len(pieces)
    if first:
        info = read_table(pieces, me_ref, cap, relative)
        outs[0][...] = info
        outs = outs[1:]
    else:
        info = info_ref[...]
    code, child, axis, live, left = (jnp.broadcast_to(info[k : k + 1], (FACE, slots)) for k in range(5))
    row = lax.broadcasted_iota(jnp.int32, (slots, slots), 0)
    partner = None
    for p in range(0, len(pieces), 2):
        both = jnp.concatenate([pieces[p][:ROWS], pieces[p + 1][:ROWS]], axis=1)
        hits = [jnp.where(row + (p + i) * slots == info[0:1], 1.0, 0.0).astype(BF16) for i in range(2)]
        part = dot(both, jnp.concatenate(hits, axis=0))
        partner = part if partner is None else partner + part
    is_left = left == 1
    alive = live == 1
    child = [child == c + 1 for c in range(4)]
    picks = [axis == n for n in range(3)]

    def variables(x):
        return [x[v * FACE : (v + 1) * FACE].astype(F32) for v in range(5)]

    own, partner, state = variables(own_ref[:ROWS]), variables(partner), variables(state_ref[section][:, :slots])
    left_lam = [jnp.where(is_left, a, b) for a, b in zip(own, partner)]
    right_lam = [jnp.where(is_left, b, a) for a, b in zip(own, partner)]
    stacked = jnp.concatenate([x.astype(BF16) for x in left_lam + state], axis=1)
    spread = spread_children(forward_ref[...], [stacked, stacked])
    left_lam = choose(left_lam, spread, child)
    u = choose(state, spread[:, 5 * slots :], child, is_left)
    w = [jnp.where(alive, b - a, 0.0) for a, b in zip(left_lam, right_lam)]
    u = [jnp.where(alive, u[v], REST[v]) for v in range(5)]
    g = flux_pull(u, w, picks)
    side = jnp.where(is_left, 0.5 * penalty, -0.5 * penalty)
    pull = [0.5 * g[v] + side * w[v] for v in range(5)]
    stacked = jnp.concatenate(pull, axis=1)
    high = stacked.astype(BF16)
    rest = (stacked - high.astype(F32)).astype(BF16)
    spread = spread_children(backward_ref[...], [high, rest, high])
    grads = choose(pull, spread, child, is_left)

    table = table_ref[...]
    lifted = lift_slots(grads, hot_ref[:, :slots], table, elements)
    jac = column_of(jac_ref[...]) * (step_size * section_weights[section])
    lam = [base_ref[v] + jac * lifted[v * elements : (v + 1) * elements] for v in range(5)]
    for v in range(5):
        outs[0][v] = lam[v]
    if not last:
        lam_low = jnp.concatenate([x.astype(BF16) for x in lam], axis=0)
        values = slot_values(lam_low, hot_ref[...], table, elements)
        outs[1][...] = values[:, :slots]
        outs[2][...] = values[:, slots:]


def call(kernel, outs, args, scratch=(), scalars=(), last=False):
    specs = [pl.BlockSpec(memory_space=pltpu.SMEM if i in scalars else pltpu.VMEM) for i in range(len(args))]
    args = [a if i in scalars else pltpu.with_memory_space_constraint(a, pltpu.VMEM) for i, a in enumerate(args)]
    shapes = [jax.ShapeDtypeStruct(o, t) if last else pltpu.VMEM(o, t) for o, t in outs]
    return pl.pallas_call(
        kernel,
        out_shape=shapes,
        in_specs=specs,
        out_specs=[pl.BlockSpec(memory_space=pltpu.VMEM)] * len(outs),
        scratch_shapes=list(scratch),
        compiler_params=pltpu.CompilerParams(vmem_limit_bytes=VMEM_GRANT),
    )(*args)


def power_of_two(n):
    return n & (n - 1) == 0


def gather_group(x):
    ny, nz = lax.axis_size("gy"), lax.axis_size("gz")
    if nz != 2 or not power_of_two(ny) or ny > 8:
        return [lax.all_gather(x, ("gy", "gz"), axis=0, tiled=False)], False
    pieces = []
    for k in range(ny):
        here = x if k == 0 else lax.ppermute(x, "gy", [(i, i ^ k) for i in range(ny)])
        pieces += [here, lax.ppermute(here, "gz", [(0, 1), (1, 0)])]
    return pieces, True


def neighbours(payload, faces):
    peers = lax.axis_size("gz")
    up = [(i, (i + 1) % peers) for i in range(peers)]
    down = [(j, i) for i, j in up]
    if peers == 2:
        return lax.ppermute(payload, "gz", up)
    below = lax.ppermute(payload, "gz", up)
    above = lax.ppermute(payload, "gz", down)
    lane = lax.broadcasted_iota(jnp.int32, payload.shape, 1)
    return jnp.where(lane < faces, above, below)


def per_device(adjoint, saved, inv_jac, stiffness, send_face, mortar_table, conf_faces):
    elements = adjoint.shape[0]
    sections = saved.shape[0]
    slots = send_face.shape[1]
    faces = conf_faces.shape[2]
    shared = -(-2 * faces // 128) * 128
    table = jnp.asarray(restriction_table())
    forward, backward = (jnp.asarray(t) for t in projection_tables())
    jac = inv_jac.reshape(1, elements)
    lam = jnp.transpose(adjoint, (1, 0, 2))
    states = jnp.transpose(saved, (0, 2, 1, 3))
    me = lax.axis_index(("gy", "gz")).astype(jnp.int32).reshape(1)
    rows = ((5, elements, ELEM), F32)
    sent = ((ROWS, slots), BF16)
    conforming = ((ROWS, shared), BF16)
    info_shape = ((EXTRA, slots), jnp.int32)

    outgoing, own_shared, hot = call(
        start_kernel,
        [((ROWS + EXTRA, slots), BF16), conforming, ((6 * elements, slots + shared), BF16)],
        [lam, send_face, conf_faces, mortar_table, table],
        scratch=(pltpu.VMEM((8, slots + shared), jnp.int32),),
    )
    (values,) = call(state_kernel, [((sections, ROWS, slots + shared), BF16)], [states, hot, table])
    info = jnp.zeros(info_shape[0], jnp.int32)
    for section in (2, 1, 0):
        pieces, relative = gather_group(outgoing)
        near = neighbours(own_shared, faces)
        (base,) = call(
            functools.partial(volume_kernel, section, faces),
            [rows],
            [lam, states, stiffness, jac, own_shared, near, values, hot, table],
            scratch=(pltpu.VMEM((3, 5 * elements, ELEM), F32), pltpu.VMEM((5 * elements, ELEM), F32)),
        )
        first, last = section == sections - 1, section == 0
        outs = ([info_shape] if first else []) + [rows] + ([] if last else [sent, conforming])
        args = pieces + [outgoing, base, values, hot, table, jac, forward, backward, me, info]
        out = call(
            functools.partial(mortar_update, section, relative, first, last, len(pieces)),
            outs, args, scalars=(len(args) - 2,), last=last,
        )
        if first:
            info, out = out[0], out[1:]
        lam = out[0]
        if not last:
            outgoing, own_shared = out[1:]
    return jnp.transpose(lam, (1, 0, 2))


def solution(mesh):
    return jax.shard_map(
        per_device,
        mesh=mesh,
        in_specs=(
            P(("gx", "gy", "gz"), None, None),
            P(None, ("gx", "gy", "gz"), None, None),
            P(("gx", "gy", "gz")),
            P(),
            P(("gx", "gy", "gz"), None),
            P(("gx", "gy", "gz"), None, None),
            P(("gx", "gy", "gz"), None, None),
        ),
        out_specs=P(("gx", "gy", "gz"), None, None),
        check_vma=False,
    )
```

```python
import functools

import jax
import jax.numpy as jnp
import numpy as np
from jax import lax
from jax.experimental import pallas as pl
from jax.experimental.pallas import tpu as pltpu
from jax.sharding import PartitionSpec as P

ORDER = 7
LINE = ORDER + 1
FACE = LINE * LINE
ELEM = FACE * LINE
PAIRS = 3
TILE = 2 * FACE
ROWS = 5 * FACE
EXTRA = 16

gamma_gas = 1.4
penalty = 1.5
viscosity = 0.5
step_size = 0.2
section_weights = (0.25, 0.25, 0.5)
GM1 = gamma_gas - 1.0
REST = (1.0, 0.0, 0.0, 0.0, 2.5)
F32 = jnp.float32
VMEM_GRANT = 24 << 20
BF16 = jnp.bfloat16


def lagrange_matrix(points, abscissa):
    out = np.ones((LINE, LINE))
    for target in range(LINE):
        for other in range(LINE):
            if other != target:
                out[:, target] *= (points - abscissa[other]) / (abscissa[target] - abscissa[other])
    return out


def split_low(matrix):
    high = matrix.astype(np.float32).astype(BF16)
    low = (matrix - high.astype(np.float64)).astype(np.float32).astype(BF16)
    return high, low


def projection_tables():
    abscissa = -np.cos(np.pi * np.arange(LINE) / ORDER)
    halves = [lagrange_matrix((abscissa + 2.0 * h - 1.0) * 0.5, abscissa) for h in range(2)]
    children = [np.kron(halves[c // 2], halves[c % 2]) for c in range(4)]
    fh, fl = split_low(np.concatenate(children, axis=0))
    bh, bl = split_low(np.concatenate([m.T for m in children], axis=0))
    return np.concatenate([fh, fl], axis=1), np.concatenate([bh, bh, bl], axis=1)


def restriction_table():
    column = np.arange(6 * FACE)
    face, local = column // FACE, column % FACE
    first, second = local // LINE, local % LINE
    axis, fixed = face // 2, face % 2 * (LINE - 1)
    x = np.where(axis == 0, fixed, first)
    y = np.where(axis == 0, first, np.where(axis == 1, fixed, second))
    z = np.where(axis == 2, fixed, second)
    node = x * FACE + y * LINE + z
    return (np.arange(ELEM)[:, None] == node[None, :]).astype(np.float32).astype(BF16)


def dot(a, b, ca=1, cb=0):
    return lax.dot_general(a, b, (((ca,), (cb,)), ((), ())), preferred_element_type=F32)


def low_lanes(rows):
    return lax.broadcasted_iota(jnp.int32, (rows, TILE), 1) < FACE


def swap(x):
    return pltpu.roll(x, FACE, 1)


def exchange(a, b, low):
    return jnp.where(low, a, swap(b)), jnp.where(low, swap(a), b)


def flux_pull(u, w, picks):
    inv = 1.0 / u[0]
    vel = [u[i] * inv for i in (1, 2, 3)]
    kin = 0.5 * (vel[0] * vel[0] + vel[1] * vel[1] + vel[2] * vel[2])
    enth = gamma_gas * (u[4] * inv) - GM1 * kin
    q = w[1] * vel[0] + w[2] * vel[1] + w[3] * vel[2]
    if picks is None:
        vn, wn = vel[2], w[3]
    else:
        vn = jnp.where(picks[0], vel[0], jnp.where(picks[1], vel[1], vel[2]))
        wn = jnp.where(picks[0], w[1], jnp.where(picks[1], w[2], w[3]))
    r = vn * w[4]
    a = w[0] + q + enth * w[4]
    g = [GM1 * kin * wn - vn * q + (GM1 * kin - enth) * r]
    t = GM1 * (wn + r)
    for i in range(3):
        gi = w[1 + i] * vn - vel[i] * t
        if picks is None:
            gi = gi + a if i == 2 else gi
        else:
            gi = gi + jnp.where(picks[i], a, 0.0)
        g.append(gi)
    g.append(GM1 * wn + gamma_gas * r)
    return g


def trace_faces(field_low, table, elements):
    traced = dot(field_low, table)
    low = low_lanes(elements)
    zero = jnp.zeros((elements, TILE), F32)
    rows = [[None] * PAIRS for _ in range(6)]

    def piece(v, k):
        if v >= 5:
            return zero
        return traced[v * elements : (v + 1) * elements, k * TILE : (k + 1) * TILE]

    for j in range(PAIRS):
        for k in range(3):
            rows[2 * k][j], rows[2 * k + 1][j] = exchange(piece(2 * j, k), piece(2 * j + 1, k), low)
    return jnp.concatenate([jnp.concatenate(r, axis=1) for r in rows], axis=0).astype(BF16)


def lift_slots(grads, hot, table, elements):
    padded = jnp.concatenate([g.astype(BF16) for g in grads] + [jnp.zeros(grads[0].shape, BF16)], axis=0)
    face_grad = dot(hot, padded, 1, 1)
    low = low_lanes(elements)
    rows = [[None] * 3 for _ in range(6)]

    def piece(f, j):
        return face_grad[f * elements : (f + 1) * elements, j * TILE : (j + 1) * TILE]

    for j in range(PAIRS):
        for k in range(3):
            rows[2 * j][k], rows[2 * j + 1][k] = exchange(piece(2 * k, j), piece(2 * k + 1, j), low)
    arranged = jnp.concatenate([jnp.concatenate(r, axis=1) for r in rows[:5]], axis=0).astype(BF16)
    return dot(arranged, table, 1, 1)


def column_of(row):
    n = row.shape[1]
    same = lax.broadcasted_iota(jnp.int32, (n, n), 0) == lax.broadcasted_iota(jnp.int32, (n, n), 1)
    return jnp.sum(jnp.where(same, jnp.broadcast_to(row, (n, n)), 0.0), axis=1, keepdims=True)


def slot_values(field_low, hot, table, elements):
    faces = trace_faces(field_low, table, elements)
    return dot(faces, hot, 0, 0).astype(BF16)[:ROWS]


def fetch(pairs, sems):
    copies = [pltpu.make_async_copy(a, b, sems.at[i]) for i, (a, b) in enumerate(pairs)]
    for copy in copies:
        copy.start()
    return copies


def start_kernel(lam_hbm, send_hbm, conf_hbm, map_hbm, table_hbm, out_ref, shared_ref, hot_ref, lam_ref, table_ref, send_ref, conf_ref, map_ref, ids_ref, sems):
    pairs = ((send_hbm, send_ref), (conf_hbm, conf_ref), (map_hbm, map_ref), (lam_hbm, lam_ref), (table_hbm, table_ref))
    copies = fetch(pairs, sems)
    elements = lam_ref.shape[1]
    slots = send_ref.shape[1]
    faces = conf_ref.shape[2]
    ids_ref[...] = jnp.full(ids_ref.shape, -1, jnp.int32)
    for copy in copies[:3]:
        copy.wait()
    ids_ref[0:1, 0:slots] = send_ref[...]
    ids_ref[0:1, slots : slots + faces] = conf_ref[0, 0:1]
    ids_ref[0:1, slots + faces : slots + 2 * faces] = conf_ref[0, 1:2]
    shape = hot_ref.shape
    row = lax.broadcasted_iota(jnp.int32, shape, 0)
    face = row // elements
    ident = 6 * (row - face * elements) + face
    hot = jnp.where(ident == ids_ref[0:1], 1.0, 0.0).astype(BF16)
    hot_ref[...] = hot
    rows = [map_ref[k] for k in range(5)]
    mortars = rows[0].shape[1]
    slot = lax.broadcasted_iota(jnp.int32, (slots, mortars), 0)
    field = lax.broadcasted_iota(jnp.int32, (EXTRA, mortars), 0)
    known = jnp.where(field == 1, rows[2], jnp.where(field == 2, rows[3], jnp.where(field == 3, rows[4], 0)))
    info = None
    for mine, other, left in ((0, 1, 1), (1, 0, 0)):
        hits = jnp.where(slot == rows[mine], 1.0, 0.0).astype(BF16)
        fields = jnp.where(field == 0, rows[other], jnp.where(field == 4, left, known))
        part = dot(fields.astype(F32).astype(BF16), hits, 1, 1)
        info = part if info is None else info + part
    out_ref[ROWS:] = info.astype(BF16)
    for copy in copies[3:]:
        copy.wait()
    lam_low = lam_ref[...].astype(BF16).reshape(5 * elements, ELEM)
    values = slot_values(lam_low, hot, table_ref[...], elements)
    out_ref[0:ROWS] = values[:, :slots]
    shared_ref[...] = values[:, slots:]


def state_kernel(saved_hbm, stiff_hbm, forward_hbm, backward_hbm, hot_ref, table_ref, out_ref, saved_ref, stiff_ref, forward_ref, backward_ref, sems):
    pairs = ((saved_hbm, saved_ref), (stiff_hbm, stiff_ref), (forward_hbm, forward_ref), (backward_hbm, backward_ref))
    copies = fetch(pairs, sems)
    copies[0].wait()
    elements = saved_ref.shape[2]
    for s in range(saved_ref.shape[0]):
        out_ref[s] = slot_values(saved_ref[s].reshape(5 * elements, ELEM), hot_ref[...], table_ref[...], elements)
    for copy in copies[1:]:
        copy.wait()


def volume_kernel(section, faces, lam_ref, saved_ref, stiff_ref, jac_ref, own_ref, near_ref, state_ref, hot_ref, table_ref, base_ref, slope_ref, smooth_ref):
    elements = lam_ref.shape[1]
    coef = step_size * section_weights[section]
    lam_low = lam_ref[...].astype(BF16).reshape(5 * elements, ELEM)

    slots = state_ref.shape[2] - own_ref.shape[1]
    width = own_ref.shape[1]
    lane = lax.broadcasted_iota(jnp.int32, (FACE, width), 1)
    used = lane < 2 * faces
    lower = lane < faces
    sign = jnp.where(lower, -1.0, 1.0)
    w, u = [], []
    for v in range(5):
        rows = slice(v * FACE, (v + 1) * FACE)
        near = near_ref[rows].astype(F32)
        near = jnp.where(lower, pltpu.roll(near, width - faces, 1), pltpu.roll(near, faces, 1))
        w.append(jnp.where(used, sign * (near - own_ref[rows].astype(F32)), 0.0))
        u.append(jnp.where(used, state_ref[section, rows, slots:].astype(F32), REST[v]))
    g = flux_pull(u, w, None)
    grads = [0.5 * g[v] + (0.5 * penalty) * sign * w[v] for v in range(5)]
    total = viscosity * -1.0
    smooth = lift_slots(grads, hot_ref[:, slots:], table_ref[...], elements)
    for d in range(3):
        slopes = dot(lam_low, stiff_ref[d])
        slope_ref[d] = slopes
        smooth = smooth + total * dot(slopes.astype(BF16), stiff_ref[d], 1, 1)
    smooth_ref[...] = smooth
    jac = column_of(jac_ref[...]) * coef
    step = 16
    for r in range(0, elements, step):
        scale = jnp.broadcast_to(jac[r : r + step], (step, 128))
        for c in range(0, ELEM, 128):
            u = [saved_ref[section, v, r : r + step, c : c + 128].astype(F32) for v in range(5)]
            inv = 1.0 / u[0]
            vel = [u[i] * inv for i in (1, 2, 3)]
            kin = 0.5 * (vel[0] * vel[0] + vel[1] * vel[1] + vel[2] * vel[2])
            enth = gamma_gas * (u[4] * inv) - GM1 * kin
            trace = run = first = None
            g = [None, None, None, None]
            for d in range(3):
                w = [slope_ref[d, v * elements + r : v * elements + r + step, c : c + 128] for v in range(5)]
                q = w[1] * vel[0] + w[2] * vel[1] + w[3] * vel[2]
                term = vel[d] * q
                first = term if first is None else first + term
                trace = w[1 + d] if trace is None else trace + w[1 + d]
                part = vel[d] * w[4]
                run = part if run is None else run + part
                for i in range(3):
                    gi = w[1 + i] * vel[d]
                    if i == d:
                        gi = gi + (w[0] + q + enth * w[4])
                    g[1 + i] = gi if g[1 + i] is None else g[1 + i] + gi
            t = GM1 * (trace + run)
            pulled = [GM1 * kin * trace - first + (GM1 * kin - enth) * run]
            pulled += [g[1 + i] - vel[i] * t for i in range(3)]
            pulled.append(GM1 * trace + gamma_gas * run)
            for v in range(5):
                rows = slice(v * elements + r, v * elements + r + step)
                vol = pulled[v] + smooth_ref[rows, c : c + 128]
                base_ref[v, r : r + step, c : c + 128] = lam_ref[v, r : r + step, c : c + 128] + scale * vol

def spread_children(matrix, stacked):
    return dot(matrix, jnp.concatenate(stacked, axis=0))


def choose(raw, spread, child, keep=None):
    out = []
    for v, value in enumerate(raw):
        width = value.shape[1]
        picked = value
        for c in range(4):
            hit = child[c] if keep is None else child[c] & keep
            picked = jnp.where(hit, spread[c * FACE : (c + 1) * FACE, v * width : (v + 1) * width], picked)
        out.append(picked)
    return out


def read_table(pieces, me_ref, cap, relative):
    slots = pieces[0].shape[1]
    me = me_ref[0]
    lane = lax.broadcasted_iota(jnp.int32, (EXTRA, slots), 1)
    owner_of = lane // cap
    info = jnp.zeros((EXTRA, slots), F32)
    for p, piece in enumerate(pieces):
        owner = me ^ p if relative else p
        shift = lax.rem((owner - me) * cap + slots, slots)
        moved = pltpu.roll(piece[ROWS:].astype(F32), shift, 1)
        info = jnp.where(owner_of == owner, moved, info)
    info = info.astype(jnp.int32)
    source = info[0:1] // cap
    rank = info[0:1] - source * cap
    if relative:
        source = source ^ me
    code = source * slots + owner_of[0:1] * cap + rank
    field = lax.broadcasted_iota(jnp.int32, (EXTRA, slots), 0)
    return jnp.where(field == 0, code, info)


def mortar_update(section, relative, first, last, count, *refs):
    refs = list(refs)
    pieces = [r[...] for r in refs[:count]]
    own_ref = refs[count]
    base_ref, state_ref, hot_ref, table_ref, jac_ref, forward_ref, backward_ref, me_ref = refs[count + 1 : count + 9]
    outs = refs[count + 9 :]
    elements = base_ref.shape[1]
    if len(pieces) == 1 and pieces[0].ndim == 3:
        pieces = [pieces[0][p] for p in range(pieces[0].shape[0])]
    slots = pieces[0].shape[1]
    cap = slots // len(pieces)
    if first:
        info = read_table(pieces, me_ref, cap, relative)
        outs[0][...] = info
        outs = outs[1:]
    else:
        info = outs[0][...]
        outs = outs[1:]
    code, child, axis, live, left = (jnp.broadcast_to(info[k : k + 1], (FACE, slots)) for k in range(5))
    row = lax.broadcasted_iota(jnp.int32, (slots, slots), 0)
    partner = None
    for p in range(0, len(pieces), 2):
        both = jnp.concatenate([pieces[p][:ROWS], pieces[p + 1][:ROWS]], axis=1)
        hits = [jnp.where(row + (p + i) * slots == info[0:1], 1.0, 0.0).astype(BF16) for i in range(2)]
        part = dot(both, jnp.concatenate(hits, axis=0))
        partner = part if partner is None else partner + part
    is_left = left == 1
    alive = live == 1
    child = [child == c + 1 for c in range(4)]
    picks = [axis == n for n in range(3)]

    def variables(x):
        return [x[v * FACE : (v + 1) * FACE].astype(F32) for v in range(5)]

    own, partner, state = variables(own_ref[:ROWS]), variables(partner), variables(state_ref[section][:, :slots])
    left_lam = [jnp.where(is_left, a, b) for a, b in zip(own, partner)]
    right_lam = [jnp.where(is_left, b, a) for a, b in zip(own, partner)]
    stacked = jnp.concatenate([x.astype(BF16) for x in left_lam + state], axis=1)
    spread = spread_children(forward_ref[...], [stacked, stacked])
    left_lam = choose(left_lam, spread, child)
    u = choose(state, spread[:, 5 * slots :], child, is_left)
    w = [jnp.where(alive, b - a, 0.0) for a, b in zip(left_lam, right_lam)]
    u = [jnp.where(alive, u[v], REST[v]) for v in range(5)]
    g = flux_pull(u, w, picks)
    side = jnp.where(is_left, 0.5 * penalty, -0.5 * penalty)
    pull = [0.5 * g[v] + side * w[v] for v in range(5)]
    stacked = jnp.concatenate(pull, axis=1)
    high = stacked.astype(BF16)
    rest = (stacked - high.astype(F32)).astype(BF16)
    spread = spread_children(backward_ref[...], [high, rest, high])
    grads = choose(pull, spread, child, is_left)

    table = table_ref[...]
    lifted = lift_slots(grads, hot_ref[:, :slots], table, elements)
    jac = column_of(jac_ref[...]) * (step_size * section_weights[section])
    lam = [base_ref[v] + jac * lifted[v * elements : (v + 1) * elements] for v in range(5)]
    for v in range(5):
        outs[0][v] = lam[v]
    if not last:
        lam_low = jnp.concatenate([x.astype(BF16) for x in lam], axis=0)
        values = slot_values(lam_low, hot_ref[...], table, elements)
        outs[1][...] = values[:, :slots]
        outs[2][...] = values[:, slots:]


def call(kernel, outs, args, scratch=(), scalars=(), far=0, last=False):
    def space(i):
        return pl.ANY if i < far else pltpu.SMEM if i in scalars else pltpu.VMEM

    args = [pltpu.with_memory_space_constraint(a, pltpu.VMEM) if space(i) is pltpu.VMEM else a for i, a in enumerate(args)]
    shapes = [jax.ShapeDtypeStruct(o, t) if last else pltpu.VMEM(o, t) for o, t in outs]
    return pl.pallas_call(
        kernel,
        out_shape=shapes,
        in_specs=[pl.BlockSpec(memory_space=space(i)) for i in range(len(args))],
        out_specs=[pl.BlockSpec(memory_space=pltpu.VMEM)] * len(outs),
        scratch_shapes=list(scratch),
        compiler_params=pltpu.CompilerParams(vmem_limit_bytes=VMEM_GRANT),
    )(*args)


def power_of_two(n):
    return n & (n - 1) == 0


def gather_group(x):
    ny, nz = lax.axis_size("gy"), lax.axis_size("gz")
    if nz != 2 or not power_of_two(ny) or ny > 8:
        return [lax.all_gather(x, ("gy", "gz"), axis=0, tiled=False)], False
    pieces = []
    for k in range(ny):
        here = x if k == 0 else lax.ppermute(x, "gy", [(i, i ^ k) for i in range(ny)])
        pieces += [here, lax.ppermute(here, "gz", [(0, 1), (1, 0)])]
    return pieces, True


def neighbours(payload, faces):
    peers = lax.axis_size("gz")
    up = [(i, (i + 1) % peers) for i in range(peers)]
    down = [(j, i) for i, j in up]
    if peers == 2:
        return lax.ppermute(payload, "gz", up)
    below = lax.ppermute(payload, "gz", up)
    above = lax.ppermute(payload, "gz", down)
    lane = lax.broadcasted_iota(jnp.int32, payload.shape, 1)
    return jnp.where(lane < faces, above, below)


def per_device(adjoint, saved, inv_jac, stiffness, send_face, mortar_table, conf_faces):
    elements = adjoint.shape[0]
    sections = saved.shape[0]
    slots = send_face.shape[1]
    faces = conf_faces.shape[2]
    shared = -(-2 * faces // 128) * 128
    table = jnp.asarray(restriction_table())
    forward, backward = (jnp.asarray(t) for t in projection_tables())
    jac = inv_jac.reshape(1, elements)
    lam = jnp.transpose(adjoint, (1, 0, 2))
    states = jnp.transpose(saved, (0, 2, 1, 3))
    me = lax.axis_index(("gy", "gz")).astype(jnp.int32).reshape(1)
    rows = ((5, elements, ELEM), F32)
    sent = ((ROWS, slots), BF16)
    conforming = ((ROWS, shared), BF16)
    info_shape = ((EXTRA, slots), jnp.int32)

    mortars = jnp.transpose(mortar_table, (1, 0, 2))
    held = lambda x: (x.shape, x.dtype)
    outgoing, own_shared, hot, lam, table = call(
        start_kernel,
        [((ROWS + EXTRA, slots), BF16), conforming, ((6 * elements, slots + shared), BF16), held(lam), held(table)],
        [lam, send_face, conf_faces, mortars, table],
        scratch=(
            pltpu.VMEM(send_face.shape, jnp.int32),
            pltpu.VMEM(conf_faces.shape, jnp.int32),
            pltpu.VMEM(mortars.shape, jnp.int32),
            pltpu.VMEM((8, slots + shared), jnp.int32),
            pltpu.SemaphoreType.DMA((5,)),
        ),
        far=5,
    )
    values, states, stiffness, forward, backward = call(
        state_kernel,
        [((sections, ROWS, slots + shared), BF16), held(states), held(stiffness), held(forward), held(backward)],
        [states, stiffness, forward, backward, hot, table],
        scratch=(pltpu.SemaphoreType.DMA((4,)),),
        far=4,
    )
    info = None
    for section in (2, 1, 0):
        pieces, relative = gather_group(outgoing)
        near = neighbours(own_shared, faces)
        (base,) = call(
            functools.partial(volume_kernel, section, faces),
            [rows],
            [lam, states, stiffness, jac, own_shared, near, values, hot, table],
            scratch=(pltpu.VMEM((3, 5 * elements, ELEM), F32), pltpu.VMEM((5 * elements, ELEM), F32)),
        )
        first, last = section == sections - 1, section == 0
        outs = ([info_shape] if first else []) + [rows] + ([] if last else [sent, conforming])
        args = pieces + [outgoing, base, values, hot, table, jac, forward, backward, me] + ([] if first else [info])
        out = call(
            functools.partial(mortar_update, section, relative, first, last, len(pieces)),
            outs, args, scalars=(len(pieces) + 8,), last=last,
        )
        if first:
            info, out = out[0], out[1:]
        lam = out[0]
        if not last:
            outgoing, own_shared = out[1:]
    return jnp.transpose(lam, (1, 0, 2))


def solution(mesh):
    return jax.shard_map(
        per_device,
        mesh=mesh,
        in_specs=(
            P(("gx", "gy", "gz"), None, None),
            P(None, ("gx", "gy", "gz"), None, None),
            P(("gx", "gy", "gz")),
            P(),
            P(("gx", "gy", "gz"), None),
            P(("gx", "gy", "gz"), None, None),
            P(("gx", "gy", "gz"), None, None),
        ),
        out_specs=P(("gx", "gy", "gz"), None, None),
        check_vma=False,
    )
```

```python
import functools

import jax
import jax.numpy as jnp
import numpy as np
from jax import lax
from jax.experimental import pallas as pl
from jax.experimental.pallas import tpu as pltpu
from jax.sharding import PartitionSpec as P


ORDER = 7
LINE = ORDER + 1
FACE = LINE * LINE
ELEM = FACE * LINE
PAIRS = 3
TILE = 2 * FACE
ROWS = 5 * FACE
EXTRA = 16

gamma_gas = 1.4
penalty = 1.5
viscosity = 0.5
step_size = 0.2
section_weights = (0.25, 0.25, 0.5)
GM1 = gamma_gas - 1.0
REST = (1.0, 0.0, 0.0, 0.0, 2.5)
F32 = jnp.float32
VMEM_GRANT = 24 << 20
BF16 = jnp.bfloat16


def lagrange_matrix(points, abscissa):
    out = np.ones((LINE, LINE))
    for target in range(LINE):
        for other in range(LINE):
            if other != target:
                out[:, target] *= (points - abscissa[other]) / (abscissa[target] - abscissa[other])
    return out


def split_low(matrix):
    high = matrix.astype(np.float32).astype(BF16)
    low = (matrix - high.astype(np.float64)).astype(np.float32).astype(BF16)
    return high, low


def projection_tables():
    abscissa = -np.cos(np.pi * np.arange(LINE) / ORDER)
    halves = [lagrange_matrix((abscissa + 2.0 * h - 1.0) * 0.5, abscissa) for h in range(2)]
    children = [np.kron(halves[c // 2], halves[c % 2]) for c in range(4)]
    fh, fl = split_low(np.concatenate(children, axis=0))
    bh, bl = split_low(np.concatenate([m.T for m in children], axis=0))
    return np.concatenate([fh, fl], axis=1), np.concatenate([bh, bh, bl], axis=1)


def restriction_table():
    column = np.arange(6 * FACE)
    face, local = column // FACE, column % FACE
    first, second = local // LINE, local % LINE
    axis, fixed = face // 2, face % 2 * (LINE - 1)
    x = np.where(axis == 0, fixed, first)
    y = np.where(axis == 0, first, np.where(axis == 1, fixed, second))
    z = np.where(axis == 2, fixed, second)
    node = x * FACE + y * LINE + z
    return (np.arange(ELEM)[:, None] == node[None, :]).astype(np.float32).astype(BF16)


def dot(a, b, ca=1, cb=0):
    return lax.dot_general(a, b, (((ca,), (cb,)), ((), ())), preferred_element_type=F32)


def low_lanes(rows):
    return lax.broadcasted_iota(jnp.int32, (rows, TILE), 1) < FACE


def swap(x):
    return pltpu.roll(x, FACE, 1)


def exchange(a, b, low):
    return jnp.where(low, a, swap(b)), jnp.where(low, swap(a), b)


def flux_pull(u, w, picks):
    inv = 1.0 / u[0]
    vel = [u[i] * inv for i in (1, 2, 3)]
    kin = 0.5 * (vel[0] * vel[0] + vel[1] * vel[1] + vel[2] * vel[2])
    enth = gamma_gas * (u[4] * inv) - GM1 * kin
    q = w[1] * vel[0] + w[2] * vel[1] + w[3] * vel[2]
    if picks is None:
        vn, wn = vel[2], w[3]
    else:
        vn = jnp.where(picks[0], vel[0], jnp.where(picks[1], vel[1], vel[2]))
        wn = jnp.where(picks[0], w[1], jnp.where(picks[1], w[2], w[3]))
    r = vn * w[4]
    a = w[0] + q + enth * w[4]
    g = [GM1 * kin * wn - vn * q + (GM1 * kin - enth) * r]
    t = GM1 * (wn + r)
    for i in range(3):
        gi = w[1 + i] * vn - vel[i] * t
        if picks is None:
            gi = gi + a if i == 2 else gi
        else:
            gi = gi + jnp.where(picks[i], a, 0.0)
        g.append(gi)
    g.append(GM1 * wn + gamma_gas * r)
    return g


def trace_faces(field_low, table, elements):
    traced = dot(field_low, table)
    low = low_lanes(elements)
    zero = jnp.zeros((elements, TILE), F32)
    rows = [[None] * PAIRS for _ in range(6)]

    def piece(v, k):
        if v >= 5:
            return zero
        return traced[v * elements : (v + 1) * elements, k * TILE : (k + 1) * TILE]

    for j in range(PAIRS):
        for k in range(3):
            rows[2 * k][j], rows[2 * k + 1][j] = exchange(piece(2 * j, k), piece(2 * j + 1, k), low)
    return jnp.concatenate([jnp.concatenate(r, axis=1) for r in rows], axis=0).astype(BF16)


def lift_slots(grads, hot, table, elements):
    padded = jnp.concatenate([g.astype(BF16) for g in grads] + [jnp.zeros(grads[0].shape, BF16)], axis=0)
    face_grad = dot(hot, padded, 1, 1)
    low = low_lanes(elements)
    rows = [[None] * 3 for _ in range(6)]

    def piece(f, j):
        return face_grad[f * elements : (f + 1) * elements, j * TILE : (j + 1) * TILE]

    for j in range(PAIRS):
        for k in range(3):
            rows[2 * j][k], rows[2 * j + 1][k] = exchange(piece(2 * k, j), piece(2 * k + 1, j), low)
    arranged = jnp.concatenate([jnp.concatenate(r, axis=1) for r in rows[:5]], axis=0).astype(BF16)
    return dot(arranged, table, 1, 1)


def column_of(row):
    n = row.shape[1]
    same = lax.broadcasted_iota(jnp.int32, (n, n), 0) == lax.broadcasted_iota(jnp.int32, (n, n), 1)
    return jnp.sum(jnp.where(same, jnp.broadcast_to(row, (n, n)), 0.0), axis=1, keepdims=True)


def slot_values(field_low, hot, table, elements):
    faces = trace_faces(field_low, table, elements)
    return dot(faces, hot, 0, 0).astype(BF16)[:ROWS]


def fetch(pairs, sems):
    copies = [pltpu.make_async_copy(a, b, sems.at[i]) for i, (a, b) in enumerate(pairs)]
    for copy in copies:
        copy.start()
    return copies


def start_kernel(lam_hbm, send_hbm, conf_hbm, map_hbm, table_hbm, me_ref, out_ref, pair_ref, hot_ref, lam_ref, table_ref, send_ref, conf_ref, map_ref, ids_ref, sems):
    pairs = ((send_hbm, send_ref), (conf_hbm, conf_ref), (map_hbm, map_ref), (lam_hbm, lam_ref), (table_hbm, table_ref))
    copies = fetch(pairs, sems)
    elements = lam_ref.shape[1]
    slots = send_ref.shape[1]
    faces = conf_ref.shape[2]
    ids_ref[...] = jnp.full(ids_ref.shape, -1, jnp.int32)
    for copy in copies[:3]:
        copy.wait()
    ids_ref[0:1, 0:slots] = send_ref[...]
    ids_ref[0:1, slots : slots + faces] = conf_ref[0, 0:1]
    ids_ref[0:1, slots + faces : slots + 2 * faces] = conf_ref[0, 1:2]
    shape = hot_ref.shape
    row = lax.broadcasted_iota(jnp.int32, shape, 0)
    face = row // elements
    ident = 6 * (row - face * elements) + face
    hot = jnp.where(ident == ids_ref[0:1], 1.0, 0.0).astype(BF16)
    hot_ref[...] = hot
    rows = [map_ref[k] for k in range(5)]
    mortars = rows[0].shape[1]
    slot = lax.broadcasted_iota(jnp.int32, (slots, mortars), 0)
    field = lax.broadcasted_iota(jnp.int32, (EXTRA, mortars), 0)
    known = jnp.where(field == 1, rows[2], jnp.where(field == 2, rows[3], jnp.where(field == 3, rows[4], 0)))
    info = None
    for mine, other, left in ((0, 1, 1), (1, 0, 0)):
        hits = jnp.where(slot == rows[mine], 1.0, 0.0).astype(BF16)
        fields = jnp.where(field == 0, rows[other], jnp.where(field == 4, left, known))
        part = dot(fields.astype(F32).astype(BF16), hits, 1, 1)
        info = part if info is None else info + part
    out_ref[ROWS:] = info.astype(BF16)
    pair_ref[ROWS:, :slots] = info.astype(BF16)
    pair_ref[ROWS:, slots:] = jnp.zeros((EXTRA, pair_ref.shape[1] - slots), BF16)
    for copy in copies[3:]:
        copy.wait()
    lam_low = lam_ref[...].astype(BF16).reshape(5 * elements, ELEM)
    values = slot_values(lam_low, hot, table_ref[...], elements)
    out_ref[0:ROWS] = values[:, :slots]
    pair_ref[0:ROWS] = values


def state_kernel(saved_hbm, stiff_hbm, forward_hbm, backward_hbm, hot_ref, table_ref, out_ref, saved_ref, stiff_ref, forward_ref, backward_ref, sems):
    pairs = ((saved_hbm, saved_ref), (stiff_hbm, stiff_ref), (forward_hbm, forward_ref), (backward_hbm, backward_ref))
    copies = fetch(pairs, sems)
    copies[0].wait()
    elements = saved_ref.shape[2]
    for s in range(saved_ref.shape[0]):
        out_ref[s] = slot_values(saved_ref[s].reshape(5 * elements, ELEM), hot_ref[...], table_ref[...], elements)
    for copy in copies[1:]:
        copy.wait()


def volume_kernel(section, slots, faces, lam_ref, saved_ref, stiff_ref, jac_ref, own_ref, near_ref, state_ref, hot_ref, table_ref, base_ref, slope_ref, smooth_ref):
    elements = lam_ref.shape[1]
    coef = step_size * section_weights[section]
    lam_low = lam_ref[...].astype(BF16).reshape(5 * elements, ELEM)

    width = own_ref.shape[1] - slots
    lane = lax.broadcasted_iota(jnp.int32, (FACE, width), 1)
    used = lane < 2 * faces
    lower = lane < faces
    sign = jnp.where(lower, -1.0, 1.0)
    w, u = [], []
    for v in range(5):
        rows = slice(v * FACE, (v + 1) * FACE)
        near = near_ref[rows, slots:].astype(F32)
        near = jnp.where(lower, pltpu.roll(near, width - faces, 1), pltpu.roll(near, faces, 1))
        w.append(jnp.where(used, sign * (near - own_ref[rows, slots:].astype(F32)), 0.0))
        u.append(jnp.where(used, state_ref[section, rows, slots:].astype(F32), REST[v]))
    g = flux_pull(u, w, None)
    grads = [0.5 * g[v] + (0.5 * penalty) * sign * w[v] for v in range(5)]
    total = viscosity * -1.0
    smooth = lift_slots(grads, hot_ref[:, slots:], table_ref[...], elements)
    for d in range(3):
        slopes = dot(lam_low, stiff_ref[d])
        slope_ref[d] = slopes
        smooth = smooth + total * dot(slopes.astype(BF16), stiff_ref[d], 1, 1)
    smooth_ref[...] = smooth
    jac = column_of(jac_ref[...]) * coef
    step = 16
    for r in range(0, elements, step):
        scale = jnp.broadcast_to(jac[r : r + step], (step, 128))
        for c in range(0, ELEM, 128):
            u = [saved_ref[section, v, r : r + step, c : c + 128].astype(F32) for v in range(5)]
            inv = 1.0 / u[0]
            vel = [u[i] * inv for i in (1, 2, 3)]
            kin = 0.5 * (vel[0] * vel[0] + vel[1] * vel[1] + vel[2] * vel[2])
            enth = gamma_gas * (u[4] * inv) - GM1 * kin
            trace = run = first = None
            g = [None, None, None, None]
            for d in range(3):
                w = [slope_ref[d, v * elements + r : v * elements + r + step, c : c + 128] for v in range(5)]
                q = w[1] * vel[0] + w[2] * vel[1] + w[3] * vel[2]
                term = vel[d] * q
                first = term if first is None else first + term
                trace = w[1 + d] if trace is None else trace + w[1 + d]
                part = vel[d] * w[4]
                run = part if run is None else run + part
                for i in range(3):
                    gi = w[1 + i] * vel[d]
                    if i == d:
                        gi = gi + (w[0] + q + enth * w[4])
                    g[1 + i] = gi if g[1 + i] is None else g[1 + i] + gi
            t = GM1 * (trace + run)
            pulled = [GM1 * kin * trace - first + (GM1 * kin - enth) * run]
            pulled += [g[1 + i] - vel[i] * t for i in range(3)]
            pulled.append(GM1 * trace + gamma_gas * run)
            for v in range(5):
                rows = slice(v * elements + r, v * elements + r + step)
                vol = pulled[v] + smooth_ref[rows, c : c + 128]
                base_ref[v, r : r + step, c : c + 128] = lam_ref[v, r : r + step, c : c + 128] + scale * vol


def spread_children(matrix, stacked):
    return dot(matrix, jnp.concatenate(stacked, axis=0))


def choose(raw, spread, child, keep=None):
    out = []
    for v, value in enumerate(raw):
        width = value.shape[1]
        picked = value
        for c in range(4):
            hit = child[c] if keep is None else child[c] & keep
            picked = jnp.where(hit, spread[c * FACE : (c + 1) * FACE, v * width : (v + 1) * width], picked)
        out.append(picked)
    return out


def read_table(pieces, me_ref, cap, relative):
    slots = pieces[0].shape[1]
    me = me_ref[0]
    lane = lax.broadcasted_iota(jnp.int32, (EXTRA, slots), 1)
    owner_of = lane // cap
    info = jnp.zeros((EXTRA, slots), F32)
    for p, piece in enumerate(pieces):
        owner = me ^ p if relative else p
        shift = lax.rem((owner - me) * cap + slots, slots)
        moved = pltpu.roll(piece[ROWS:].astype(F32), shift, 1)
        info = jnp.where(owner_of == owner, moved, info)
    info = info.astype(jnp.int32)
    source = info[0:1] // cap
    rank = info[0:1] - source * cap
    if relative:
        source = source ^ me
    code = source * slots + owner_of[0:1] * cap + rank
    field = lax.broadcasted_iota(jnp.int32, (EXTRA, slots), 0)
    return jnp.where(field == 0, code, info)


def mortar_update(section, relative, first, last, count, *refs):
    refs = list(refs)
    slots = refs[count].shape[1]
    pieces = [r[...] if len(r.shape) == 3 else r[:, :slots] for r in refs[:count]]
    own_ref = refs[count]
    base_ref, state_ref, hot_ref, table_ref, jac_ref, forward_ref, backward_ref, me_ref = refs[count + 1 : count + 9]
    outs = refs[count + 9 :]
    elements = base_ref.shape[1]
    if len(pieces) == 1 and pieces[0].ndim == 3:
        pieces = [pieces[0][p] for p in range(pieces[0].shape[0])]
    cap = slots // len(pieces)
    if first:
        info = read_table(pieces, me_ref, cap, relative)
        outs[0][...] = info
        outs = outs[1:]
    else:
        info = outs[0][...]
        outs = outs[1:]
    _, child, axis, live, left = (jnp.broadcast_to(info[k : k + 1], (FACE, slots)) for k in range(5))
    row = lax.broadcasted_iota(jnp.int32, (slots, slots), 0)
    partner = None
    for p in range(0, len(pieces), 2):
        both = jnp.concatenate([pieces[p][:ROWS], pieces[p + 1][:ROWS]], axis=1)
        hits = [jnp.where(row + (p + i) * slots == info[0:1], 1.0, 0.0).astype(BF16) for i in range(2)]
        part = dot(both, jnp.concatenate(hits, axis=0))
        partner = part if partner is None else partner + part
    is_left = left == 1
    alive = live == 1
    child = [child == c + 1 for c in range(4)]
    picks = [axis == n for n in range(3)]

    def variables(x):
        return [x[v * FACE : (v + 1) * FACE].astype(F32) for v in range(5)]

    own, partner, state = variables(own_ref[:ROWS]), variables(partner), variables(state_ref[section][:, :slots])
    left_lam = [jnp.where(is_left, a, b) for a, b in zip(own, partner)]
    right_lam = [jnp.where(is_left, b, a) for a, b in zip(own, partner)]
    stacked = jnp.concatenate([x.astype(BF16) for x in left_lam + state], axis=1)
    spread = spread_children(forward_ref[...], [stacked, stacked])
    left_lam = choose(left_lam, spread, child)
    u = choose(state, spread[:, 5 * slots :], child, is_left)
    w = [jnp.where(alive, b - a, 0.0) for a, b in zip(left_lam, right_lam)]
    u = [jnp.where(alive, u[v], REST[v]) for v in range(5)]
    g = flux_pull(u, w, picks)
    side = jnp.where(is_left, 0.5 * penalty, -0.5 * penalty)
    pull = [0.5 * g[v] + side * w[v] for v in range(5)]
    stacked = jnp.concatenate(pull, axis=1)
    high = stacked.astype(BF16)
    rest = (stacked - high.astype(F32)).astype(BF16)
    spread = spread_children(backward_ref[...], [high, rest, high])
    grads = choose(pull, spread, child, is_left)

    table = table_ref[...]
    lifted = lift_slots(grads, hot_ref[:, :slots], table, elements)
    jac = column_of(jac_ref[...]) * (step_size * section_weights[section])
    lam = [base_ref[v] + jac * lifted[v * elements : (v + 1) * elements] for v in range(5)]
    for v in range(5):
        outs[0][v] = lam[v]
    if not last:
        lam_low = jnp.concatenate([x.astype(BF16) for x in lam], axis=0)
        values = slot_values(lam_low, hot_ref[...], table, elements)
        outs[1][...] = values[:, :slots]
        outs[2][...] = values


def call(kernel, outs, args, scratch=(), scalars=(), far=0, last=False):
    def space(i):
        return pltpu.HBM if i < far else pltpu.SMEM if i in scalars else pltpu.VMEM

    args = [a if i in scalars else pltpu.with_memory_space_constraint(a, space(i)) for i, a in enumerate(args)]
    shapes = [jax.ShapeDtypeStruct(o, t) if last else pltpu.VMEM(o, t) for o, t in outs]
    return pl.pallas_call(
        kernel,
        out_shape=shapes,
        in_specs=[pl.BlockSpec(memory_space=space(i)) for i in range(len(args))],
        out_specs=[pl.BlockSpec(memory_space=pltpu.VMEM)] * len(outs),
        scratch_shapes=list(scratch),
        compiler_params=pltpu.CompilerParams(vmem_limit_bytes=VMEM_GRANT),
    )(*args)


def power_of_two(n):
    return n & (n - 1) == 0


def paired():
    ny, nz = lax.axis_size("gy"), lax.axis_size("gz")
    return nz == 2 and power_of_two(ny) and ny <= 8


def swap_pair(x):
    return lax.ppermute(x, "gz", [(0, 1), (1, 0)])


def send_along(x, k):
    ny = lax.axis_size("gy")
    return lax.ppermute(x, "gy", [(i, i ^ k) for i in range(ny)])


def neighbours(payload, slots, faces):
    peers = lax.axis_size("gz")
    up = [(i, (i + 1) % peers) for i in range(peers)]
    down = [(j, i) for i, j in up]
    below = lax.ppermute(payload, "gz", up)
    above = lax.ppermute(payload, "gz", down)
    lane = lax.broadcasted_iota(jnp.int32, payload.shape, 1)
    return jnp.where(lane < slots + faces, above, below)


def per_device(adjoint, saved, inv_jac, stiffness, send_face, mortar_table, conf_faces):
    elements = adjoint.shape[0]
    sections = saved.shape[0]
    slots = send_face.shape[1]
    faces = conf_faces.shape[2]
    shared = -(-2 * faces // 128) * 128
    table = jnp.asarray(restriction_table())
    forward, backward = (jnp.asarray(t) for t in projection_tables())
    jac = inv_jac.reshape(1, elements)
    lam = jnp.transpose(adjoint, (1, 0, 2))
    states = jnp.transpose(saved, (0, 2, 1, 3))
    me = lax.axis_index(("gy", "gz")).astype(jnp.int32).reshape(1)
    rows = ((5, elements, ELEM), F32)
    sent = ((ROWS, slots), BF16)
    pair = ((ROWS, slots + shared), BF16)
    info_shape = ((EXTRA, slots), jnp.int32)

    mortars = jnp.transpose(mortar_table, (1, 0, 2))
    held = lambda x: (x.shape, x.dtype)
    outgoing, both, hot, lam, table = call(
        start_kernel,
        [((ROWS + EXTRA, slots), BF16), ((ROWS + EXTRA, slots + shared), BF16), ((6 * elements, slots + shared), BF16), held(lam), held(table)],
        [lam, send_face, conf_faces, mortars, table, me],
        scratch=(
            pltpu.VMEM(send_face.shape, jnp.int32),
            pltpu.VMEM(conf_faces.shape, jnp.int32),
            pltpu.VMEM(mortars.shape, jnp.int32),
            pltpu.VMEM((8, slots + shared), jnp.int32),
            pltpu.SemaphoreType.DMA((5,)),
        ),
        far=5,
        scalars=(5,),
    )
    values, states, stiffness, forward, backward = call(
        state_kernel,
        [((sections, ROWS, slots + shared), BF16), held(states), held(stiffness), held(forward), held(backward)],
        [states, stiffness, forward, backward, hot, table],
        scratch=(pltpu.SemaphoreType.DMA((4,)),),
        far=4,
    )
    info = None
    for section in (2, 1, 0):
        relative = paired()
        if relative:
            column = [None] * (lax.axis_size("gy") - 1)
            for k in reversed(range(len(column))):
                column[k] = send_along(outgoing, k + 1)
            near = swap_pair(both)
        else:
            near = neighbours(both, slots, faces)
        (base,) = call(
            functools.partial(volume_kernel, section, slots, faces),
            [rows],
            [lam, states, stiffness, jac, both, near, values, hot, table],
            scratch=(pltpu.VMEM((3, 5 * elements, ELEM), F32), pltpu.VMEM((5 * elements, ELEM), F32)),
        )
        if relative:
            pieces = [outgoing, near]
            for here in column:
                pieces += [here, swap_pair(here)]
        else:
            pieces = [lax.all_gather(outgoing, ("gy", "gz"), axis=0, tiled=False)]
        first, last = section == sections - 1, section == 0
        outs = ([info_shape] if first else []) + [rows] + ([] if last else [sent, pair])
        args = pieces + [outgoing, base, values, hot, table, jac, forward, backward, me] + ([] if first else [info])
        out = call(
            functools.partial(mortar_update, section, relative, first, last, len(pieces)),
            outs, args, scalars=(len(pieces) + 8,), last=last,
        )
        if first:
            info, out = out[0], out[1:]
        lam = out[0]
        if not last:
            outgoing, both = out[1:]
    return jnp.transpose(lam, (1, 0, 2))


def solution(mesh):
    return jax.shard_map(
        per_device,
        mesh=mesh,
        in_specs=(
            P(("gx", "gy", "gz"), None, None),
            P(None, ("gx", "gy", "gz"), None, None),
            P(("gx", "gy", "gz")),
            P(),
            P(("gx", "gy", "gz"), None),
            P(("gx", "gy", "gz"), None, None),
            P(("gx", "gy", "gz"), None, None),
        ),
        out_specs=P(("gx", "gy", "gz"), None, None),
        check_vma=False,
    )
```

```python
import functools

import jax
import jax.numpy as jnp
import numpy as np
from jax import lax
from jax.experimental import pallas as pl
from jax.experimental.pallas import tpu as pltpu
from jax.sharding import PartitionSpec as P


ORDER = 7
LINE = ORDER + 1
FACE = LINE * LINE
ELEM = FACE * LINE
PAIRS = 3
TILE = 2 * FACE
ROWS = 5 * FACE
EXTRA = 16

gamma_gas = 1.4
penalty = 1.5
viscosity = 0.5
step_size = 0.2
section_weights = (0.25, 0.25, 0.5)
GM1 = gamma_gas - 1.0
REST = (1.0, 0.0, 0.0, 0.0, 2.5)
F32 = jnp.float32
VMEM_GRANT = 24 << 20
BF16 = jnp.bfloat16


def lagrange_matrix(points, abscissa):
    out = np.ones((LINE, LINE))
    for target in range(LINE):
        for other in range(LINE):
            if other != target:
                out[:, target] *= (points - abscissa[other]) / (abscissa[target] - abscissa[other])
    return out


def split_low(matrix):
    high = matrix.astype(np.float32).astype(BF16)
    low = (matrix - high.astype(np.float64)).astype(np.float32).astype(BF16)
    return high, low


def projection_tables():
    abscissa = -np.cos(np.pi * np.arange(LINE) / ORDER)
    halves = [lagrange_matrix((abscissa + 2.0 * h - 1.0) * 0.5, abscissa) for h in range(2)]
    children = [np.kron(halves[c // 2], halves[c % 2]) for c in range(4)]
    fh, fl = split_low(np.concatenate(children, axis=0))
    bh, bl = split_low(np.concatenate([m.T for m in children], axis=0))
    return np.concatenate([fh, fl], axis=1), np.concatenate([bh, bh, bl], axis=1)


def restriction_table():
    column = np.arange(6 * FACE)
    face, local = column // FACE, column % FACE
    first, second = local // LINE, local % LINE
    axis, fixed = face // 2, face % 2 * (LINE - 1)
    x = np.where(axis == 0, fixed, first)
    y = np.where(axis == 0, first, np.where(axis == 1, fixed, second))
    z = np.where(axis == 2, fixed, second)
    node = x * FACE + y * LINE + z
    return (np.arange(ELEM)[:, None] == node[None, :]).astype(np.float32).astype(BF16)


def dot(a, b, ca=1, cb=0):
    return lax.dot_general(a, b, (((ca,), (cb,)), ((), ())), preferred_element_type=F32)


def low_lanes(rows):
    return lax.broadcasted_iota(jnp.int32, (rows, TILE), 1) < FACE


def swap(x):
    return pltpu.roll(x, FACE, 1)


def exchange(a, b, low):
    return jnp.where(low, a, swap(b)), jnp.where(low, swap(a), b)


def flux_pull(u, w, picks):
    inv = 1.0 / u[0]
    vel = [u[i] * inv for i in (1, 2, 3)]
    kin = 0.5 * (vel[0] * vel[0] + vel[1] * vel[1] + vel[2] * vel[2])
    enth = gamma_gas * (u[4] * inv) - GM1 * kin
    q = w[1] * vel[0] + w[2] * vel[1] + w[3] * vel[2]
    if picks is None:
        vn, wn = vel[2], w[3]
    else:
        vn = jnp.where(picks[0], vel[0], jnp.where(picks[1], vel[1], vel[2]))
        wn = jnp.where(picks[0], w[1], jnp.where(picks[1], w[2], w[3]))
    r = vn * w[4]
    a = w[0] + q + enth * w[4]
    g = [GM1 * kin * wn - vn * q + (GM1 * kin - enth) * r]
    t = GM1 * (wn + r)
    for i in range(3):
        gi = w[1 + i] * vn - vel[i] * t
        if picks is None:
            gi = gi + a if i == 2 else gi
        else:
            gi = gi + jnp.where(picks[i], a, 0.0)
        g.append(gi)
    g.append(GM1 * wn + gamma_gas * r)
    return g


def trace_faces(field_low, table, elements):
    traced = dot(field_low, table)
    low = low_lanes(elements)
    zero = jnp.zeros((elements, TILE), F32)
    rows = [[None] * PAIRS for _ in range(6)]

    def piece(v, k):
        if v >= 5:
            return zero
        return traced[v * elements : (v + 1) * elements, k * TILE : (k + 1) * TILE]

    for j in range(PAIRS):
        for k in range(3):
            rows[2 * k][j], rows[2 * k + 1][j] = exchange(piece(2 * j, k), piece(2 * j + 1, k), low)
    return jnp.concatenate([jnp.concatenate(r, axis=1) for r in rows], axis=0).astype(BF16)


def lift_slots(grads, hot, table, elements):
    padded = jnp.concatenate([g.astype(BF16) for g in grads] + [jnp.zeros(grads[0].shape, BF16)], axis=0)
    face_grad = dot(hot, padded, 1, 1)
    low = low_lanes(elements)
    rows = [[None] * 3 for _ in range(6)]

    def piece(f, j):
        return face_grad[f * elements : (f + 1) * elements, j * TILE : (j + 1) * TILE]

    for j in range(PAIRS):
        for k in range(3):
            rows[2 * j][k], rows[2 * j + 1][k] = exchange(piece(2 * k, j), piece(2 * k + 1, j), low)
    arranged = jnp.concatenate([jnp.concatenate(r, axis=1) for r in rows[:5]], axis=0).astype(BF16)
    return dot(arranged, table, 1, 1)


def column_of(row):
    n = row.shape[1]
    same = lax.broadcasted_iota(jnp.int32, (n, n), 0) == lax.broadcasted_iota(jnp.int32, (n, n), 1)
    return jnp.sum(jnp.where(same, jnp.broadcast_to(row, (n, n)), 0.0), axis=1, keepdims=True)


def slot_values(field_low, hot, table, elements):
    return dot(trace_faces(field_low, table, elements), hot, 0, 0)[:ROWS]


def pack_halves(values):
    low = low_lanes(ROWS // 2)
    out = []
    for tile in range(values.shape[1] // TILE):
        part = values[:, tile * TILE : (tile + 1) * TILE]
        out += [x.astype(BF16) for x in exchange(part[: ROWS // 2], part[ROWS // 2 :], low)]
    return out


def unpack_halves(a, b):
    return jnp.concatenate(exchange(a.astype(F32), b.astype(F32), low_lanes(ROWS // 2)), axis=0).astype(BF16)


def fetch(pairs, sems):
    copies = [pltpu.make_async_copy(a, b, sems.at[i]) for i, (a, b) in enumerate(pairs)]
    for copy in copies:
        copy.start()
    return copies


def start_kernel(lam_hbm, send_hbm, conf_hbm, map_hbm, table_hbm, me_ref, out_ref, pair_ref, hot_ref, lam_ref, table_ref, send_ref, conf_ref, map_ref, ids_ref, sems):
    pairs = ((send_hbm, send_ref), (conf_hbm, conf_ref), (map_hbm, map_ref), (lam_hbm, lam_ref), (table_hbm, table_ref))
    copies = fetch(pairs, sems)
    elements = lam_ref.shape[1]
    slots = send_ref.shape[1]
    faces = conf_ref.shape[2]
    ids_ref[...] = jnp.full(ids_ref.shape, -1, jnp.int32)
    for copy in copies[:3]:
        copy.wait()
    ids_ref[0:1, 0:slots] = send_ref[...]
    ids_ref[0:1, slots : slots + faces] = conf_ref[0, 0:1]
    ids_ref[0:1, slots + faces : slots + 2 * faces] = conf_ref[0, 1:2]
    shape = hot_ref.shape
    row = lax.broadcasted_iota(jnp.int32, shape, 0)
    face = row // elements
    ident = 6 * (row - face * elements) + face
    hot = jnp.where(ident == ids_ref[0:1], 1.0, 0.0).astype(BF16)
    hot_ref[...] = hot
    rows = [map_ref[k] for k in range(5)]
    mortars = rows[0].shape[1]
    slot = lax.broadcasted_iota(jnp.int32, (slots, mortars), 0)
    field = lax.broadcasted_iota(jnp.int32, (EXTRA, mortars), 0)
    known = jnp.where(field == 1, rows[2], jnp.where(field == 2, rows[3], jnp.where(field == 3, rows[4], 0)))
    info = None
    for mine, other, left in ((0, 1, 1), (1, 0, 0)):
        hits = jnp.where(slot == rows[mine], 1.0, 0.0).astype(BF16)
        fields = jnp.where(field == 0, rows[other], jnp.where(field == 4, left, known))
        part = dot(fields.astype(F32).astype(BF16), hits, 1, 1)
        info = part if info is None else info + part
    out_ref[ROWS:] = info.astype(BF16)
    pair_ref[ROWS:, :slots] = info.astype(BF16)
    pair_ref[ROWS:, slots:] = jnp.zeros((EXTRA, pair_ref.shape[1] - slots), BF16)
    for copy in copies[3:]:
        copy.wait()
    lam_low = lam_ref[...].astype(BF16).reshape(5 * elements, ELEM)
    values = slot_values(lam_low, hot, table_ref[...], elements).astype(BF16)
    out_ref[0:ROWS] = values[:, :slots]
    pair_ref[0:ROWS] = values


def state_kernel(saved_hbm, stiff_hbm, forward_hbm, backward_hbm, hot_ref, table_ref, out_ref, stiff_ref, forward_ref, backward_ref, saved_ref, sems):
    pairs = ((saved_hbm, saved_ref), (stiff_hbm.at[0 : stiff_ref.shape[0]], stiff_ref), (forward_hbm, forward_ref), (backward_hbm, backward_ref))
    copies = fetch(pairs, sems)
    copies[0].wait()
    elements = saved_ref.shape[2]
    for s in range(saved_ref.shape[0]):
        values = slot_values(saved_ref[s].reshape(5 * elements, ELEM), hot_ref[...], table_ref[...], elements)
        out_ref[s] = values.astype(BF16)
    for copy in copies[1:]:
        copy.wait()


def volume_kernel(section, slots, faces, saved_hbm, stiff_hbm, lam_ref, held_ref, jac_ref, own_ref, near_ref, state_ref, hot_ref, table_ref, base_ref, slope_ref, smooth_ref, saved_ref, stiff_ref, sems):
    held = held_ref.shape[0]
    copies = fetch(((stiff_hbm.at[held], stiff_ref), (saved_hbm.at[section], saved_ref)), sems)
    elements = lam_ref.shape[1]
    coef = step_size * section_weights[section]
    lam_low = lam_ref[...].astype(BF16).reshape(5 * elements, ELEM)

    width = own_ref.shape[1] - slots
    lane = lax.broadcasted_iota(jnp.int32, (FACE, width), 1)
    used = lane < 2 * faces
    lower = lane < faces
    sign = jnp.where(lower, -1.0, 1.0)
    w, u = [], []
    for v in range(5):
        rows = slice(v * FACE, (v + 1) * FACE)
        near = near_ref[rows, slots:].astype(F32)
        near = jnp.where(lower, pltpu.roll(near, width - faces, 1), pltpu.roll(near, faces, 1))
        w.append(jnp.where(used, sign * (near - own_ref[rows, slots:].astype(F32)), 0.0))
        u.append(jnp.where(used, state_ref[section, rows, slots:].astype(F32), REST[v]))
    g = flux_pull(u, w, None)
    grads = [0.5 * g[v] + (0.5 * penalty) * sign * w[v] for v in range(5)]
    total = viscosity * -1.0
    smooth = lift_slots(grads, hot_ref[:, slots:], table_ref[...], elements)
    for d in range(3):
        if d == held:
            copies[0].wait()
        stiff = held_ref[d] if d < held else stiff_ref[...]
        slopes = dot(lam_low, stiff)
        slope_ref[d] = slopes
        smooth = smooth + total * dot(slopes.astype(BF16), stiff, 1, 1)
    smooth_ref[...] = smooth
    copies[1].wait()
    jac = column_of(jac_ref[...]) * coef
    step = 16
    for r in range(0, elements, step):
        scale = jnp.broadcast_to(jac[r : r + step], (step, 128))
        for c in range(0, ELEM, 128):
            u = [saved_ref[v, r : r + step, c : c + 128].astype(F32) for v in range(5)]
            inv = 1.0 / u[0]
            vel = [u[i] * inv for i in (1, 2, 3)]
            kin = 0.5 * (vel[0] * vel[0] + vel[1] * vel[1] + vel[2] * vel[2])
            enth = gamma_gas * (u[4] * inv) - GM1 * kin
            trace = run = first = None
            g = [None, None, None, None]
            for d in range(3):
                w = [slope_ref[d, v * elements + r : v * elements + r + step, c : c + 128] for v in range(5)]
                q = w[1] * vel[0] + w[2] * vel[1] + w[3] * vel[2]
                term = vel[d] * q
                first = term if first is None else first + term
                trace = w[1 + d] if trace is None else trace + w[1 + d]
                part = vel[d] * w[4]
                run = part if run is None else run + part
                for i in range(3):
                    gi = w[1 + i] * vel[d]
                    if i == d:
                        gi = gi + (w[0] + q + enth * w[4])
                    g[1 + i] = gi if g[1 + i] is None else g[1 + i] + gi
            t = GM1 * (trace + run)
            pulled = [GM1 * kin * trace - first + (GM1 * kin - enth) * run]
            pulled += [g[1 + i] - vel[i] * t for i in range(3)]
            pulled.append(GM1 * trace + gamma_gas * run)
            for v in range(5):
                rows = slice(v * elements + r, v * elements + r + step)
                vol = pulled[v] + smooth_ref[rows, c : c + 128]
                base_ref[v, r : r + step, c : c + 128] = lam_ref[v, r : r + step, c : c + 128] + scale * vol


def spread_children(matrix, stacked):
    return dot(matrix, jnp.concatenate(stacked, axis=0))


def choose(raw, spread, child, keep=None):
    out = []
    for v, value in enumerate(raw):
        width = value.shape[1]
        picked = value
        for c in range(4):
            hit = child[c] if keep is None else child[c] & keep
            picked = jnp.where(hit, spread[c * FACE : (c + 1) * FACE, v * width : (v + 1) * width], picked)
        out.append(picked)
    return out


def read_table(pieces, me_ref, cap, relative):
    slots = pieces[0].shape[1]
    me = me_ref[0]
    lane = lax.broadcasted_iota(jnp.int32, (EXTRA, slots), 1)
    owner_of = lane // cap
    info = jnp.zeros((EXTRA, slots), F32)
    for p, piece in enumerate(pieces):
        owner = me ^ p if relative else p
        shift = lax.rem((owner - me) * cap + slots, slots)
        moved = pltpu.roll(piece[ROWS:].astype(F32), shift, 1)
        info = jnp.where(owner_of == owner, moved, info)
    info = info.astype(jnp.int32)
    source = info[0:1] // cap
    rank = info[0:1] - source * cap
    if relative:
        source = source ^ me
    code = source * slots + owner_of[0:1] * cap + rank
    field = lax.broadcasted_iota(jnp.int32, (EXTRA, slots), 0)
    return jnp.where(field == 0, code, info)


def route(pieces, me, cap):
    slots, devices = pieces[0].shape[1], len(pieces)
    half = slots // 2
    lane = lax.broadcasted_iota(jnp.int32, (devices, slots), 1)
    device = devices - 1 - lax.broadcasted_iota(jnp.int32, (devices, slots), 0)
    partner = jnp.zeros((devices, slots), F32)
    for p, piece in enumerate(pieces):
        owner = me ^ p
        fields = piece[ROWS:].astype(F32)
        mine = jnp.where(fields[3:4] == 1.0, fields[0:1], float(slots))
        turned = pltpu.roll(jnp.broadcast_to(mine, (devices, slots)), lax.rem((owner + 1) * cap, slots), 1)
        moved = pltpu.roll(turned, 0, 1, stride=cap, stride_axis=0)
        partner = jnp.where(lane // cap == owner, moved, partner)
    partner = partner.astype(jnp.int32)
    chip = partner // (2 * cap)
    wanted = [(partner < slots) & (chip == t) & (device // 2 != t) for t in range(devices // 2)]
    wanted = jnp.concatenate([jnp.where(x, 1.0, 0.0) for x in wanted], axis=0)
    before = lax.broadcasted_iota(jnp.int32, (slots, slots), 0) < lax.broadcasted_iota(jnp.int32, (slots, slots), 1)
    rank = dot(wanted.astype(BF16), jnp.where(before, 1.0, 0.0).astype(BF16))
    most = jnp.max(jnp.sum(wanted, axis=1, keepdims=True))
    index = lax.broadcasted_iota(jnp.int32, wanted.shape, 0)

    def row(x, t, q):
        return jnp.sum(jnp.where(index == t * devices + devices - 1 - q, x, 0.0), axis=0, keepdims=True)

    here = me // 2
    place = lax.broadcasted_iota(jnp.int32, (half, slots), 0).astype(F32)
    picks, rests = [], []
    for k in range(1, devices // 2):
        mine = jnp.where(row(wanted, here ^ k, me) > 0.0, row(rank, here ^ k, me), -1.0)
        picks.append(jnp.where(place == mine, 1.0, 0.0))
        rests.append(jnp.where(place + half == mine, 1.0, 0.0))
    picks.append(jnp.zeros_like(picks[0]))
    rests.append(jnp.zeros_like(picks[0]))
    coming = [row(rank, here, me ^ p) for p in range(devices)]
    return jnp.concatenate(picks, axis=0).astype(BF16), jnp.concatenate(rests, axis=0).astype(BF16), coming, most


def gather_lanes(blocks, codes, start=0):
    out = None
    for block in blocks:
        width = block.shape[1]
        place = lax.broadcasted_iota(jnp.int32, (width, codes.shape[1]), 0) + start
        part = dot(block, jnp.where(place == codes, 1.0, 0.0).astype(BF16))
        out = part if out is None else out + part
        start += width
    return out


def flag_kernel(excess_ref, flag_ref):
    flag_ref[0] = (jnp.max(excess_ref[...]) > 0.0).astype(jnp.int32)


def rest_kernel(sent_ref, rests_ref, *outs):
    for out, value in zip(outs, pack_halves(dot(sent_ref[...], rests_ref[...], 1, 1))):
        out[...] = value


def rest_gather_kernel(info_ref, *refs):
    blocks = [unpack_halves(refs[i][...], refs[i + 1][...]) for i in range(0, len(refs) - 1, 2)]
    refs[-1][...] = gather_lanes(blocks, info_ref[6:7]).astype(BF16)


def mortar_update(section, relative, first, last, count, *refs):
    compact = relative and not first
    slots = refs[count].shape[1]
    half = slots // 2
    pieces = [r[...] if len(r.shape) == 3 or r.shape[0] < ROWS else r[:, :slots] for r in refs[:count]]
    own_ref = refs[count]
    base_ref, state_ref, hot_ref, table_ref, jac_ref, forward_ref, backward_ref = refs[count + 1 : count + 8]
    me_ref, *outs = refs[count + 8 :] if first else (None,) + refs[count + 8 :]
    elements = base_ref.shape[1]
    if len(pieces) == 1 and pieces[0].ndim == 3:
        pieces = [pieces[0][p] for p in range(pieces[0].shape[0])]
    cap = slots // len(pieces)
    hot = hot_ref[...]
    if first:
        info = read_table(pieces, me_ref, cap, relative)
    else:
        info = outs[0][...]
        outs = outs[1:]
    if first and relative:
        picks, rests, coming, most = route(pieces, me_ref[0], cap)
        extended = []
        for piece, ranks in zip(pieces, coming):
            extra = jnp.broadcast_to(ranks, (EXTRA, slots)).astype(BF16)
            extended.append(jnp.concatenate([piece[:ROWS], extra], axis=0))
        blocks = [jnp.concatenate(extended[p : p + 2], axis=1) for p in range(0, len(pieces), 2)]
        partner = gather_lanes(blocks, info[0:1])
        rank = partner[ROWS : ROWS + 1].astype(jnp.int32)
        partner = partner[:ROWS]
        piece_of = info[0:1] // slots
        far = (piece_of >= 2) & (info[3:4] == 1)
        packed = (piece_of - 2) * half + rank
        near_code = jnp.where(far & (rank < half), 2 * slots + packed, jnp.where(far, -1, info[0:1]))
        rest_code = jnp.where(far & (rank >= half), packed - half, -1)
        field = lax.broadcasted_iota(jnp.int32, info.shape, 0)
        info = jnp.where(field == 5, near_code, jnp.where(field == 6, rest_code, info))
        chosen = dot(hot[:, :slots], picks, 1, 1).astype(BF16)
        outs[1][...] = chosen
        outs[2][...] = rests
        outs[3][...] = jnp.full(outs[3].shape, most - half, F32)
    elif compact:
        blocks = [jnp.concatenate([pieces[0][:ROWS], pieces[1][:ROWS]], axis=1)]
        blocks += [unpack_halves(pieces[p], pieces[p + 1]) for p in range(2, len(pieces), 2)]
        partner = gather_lanes(blocks, info[5:6])
        partner = partner + outs[0][...].astype(F32)
        outs = outs[1:]
        if not last:
            chosen = outs[0][...]
            outs = outs[1:]
    else:
        blocks = [jnp.concatenate([pieces[p][:ROWS], pieces[p + 1][:ROWS]], axis=1) for p in range(0, len(pieces), 2)]
        partner = gather_lanes(blocks, info[0:1])
    if first:
        outs[0][...] = info
        outs = outs[4:] if relative else outs[1:]
    child, axis, live, left = (jnp.broadcast_to(info[k : k + 1], (FACE, slots)) for k in range(1, 5))
    is_left = left == 1
    alive = live == 1
    child = [child == c + 1 for c in range(4)]
    picks = [axis == n for n in range(3)]

    def variables(x):
        return [x[v * FACE : (v + 1) * FACE].astype(F32) for v in range(5)]

    own, partner, state = variables(own_ref[:ROWS]), variables(partner), variables(state_ref[section][:, :slots])
    left_lam = [jnp.where(is_left, a, b) for a, b in zip(own, partner)]
    right_lam = [jnp.where(is_left, b, a) for a, b in zip(own, partner)]
    stacked = jnp.concatenate([x.astype(BF16) for x in left_lam + state], axis=1)
    spread = spread_children(forward_ref[...], [stacked, stacked])
    left_lam = choose(left_lam, spread, child)
    u = choose(state, spread[:, 5 * slots :], child, is_left)
    w = [jnp.where(alive, b - a, 0.0) for a, b in zip(left_lam, right_lam)]
    u = [jnp.where(alive, u[v], REST[v]) for v in range(5)]
    g = flux_pull(u, w, picks)
    side = jnp.where(is_left, 0.5 * penalty, -0.5 * penalty)
    pull = [0.5 * g[v] + side * w[v] for v in range(5)]
    stacked = jnp.concatenate(pull, axis=1)
    high = stacked.astype(BF16)
    rest = (stacked - high.astype(F32)).astype(BF16)
    spread = spread_children(backward_ref[...], [high, rest, high])
    grads = choose(pull, spread, child, is_left)

    table = table_ref[...]
    lifted = lift_slots(grads, hot[:, :slots], table, elements)
    jac = column_of(jac_ref[...]) * (step_size * section_weights[section])
    lam = [base_ref[v] + jac * lifted[v * elements : (v + 1) * elements] for v in range(5)]
    for v in range(5):
        outs[0][v] = lam[v]
    if not last:
        lam_low = jnp.concatenate([x.astype(BF16) for x in lam], axis=0)
        if relative:
            hot = jnp.concatenate([hot, chosen], axis=1)
        values = slot_values(lam_low, hot, table, elements)
        both = outs[2].shape[1]
        outs[1][...] = values[:, :slots].astype(BF16)
        outs[2][...] = values[:, :both].astype(BF16)
        if relative:
            for out, value in zip(outs[3:], pack_halves(values[:, both:])):
                out[...] = value


def call(kernel, outs, args, scratch=(), scalars=(), far=(), plain=False, final=False):
    def space(i):
        return pltpu.HBM if i in far else pltpu.SMEM if i in scalars else pltpu.VMEM

    if not plain:
        args = [a if i in scalars else pltpu.with_memory_space_constraint(a, space(i)) for i, a in enumerate(args)]
    small = [o == (1,) for o, _ in outs]
    shapes = [jax.ShapeDtypeStruct(o, t) if plain or final or tiny else pltpu.VMEM(o, t) for (o, t), tiny in zip(outs, small)]
    return pl.pallas_call(
        kernel,
        out_shape=shapes,
        in_specs=[pl.BlockSpec(memory_space=space(i)) for i in range(len(args))],
        out_specs=[pl.BlockSpec(memory_space=pltpu.SMEM if tiny else pltpu.VMEM) for tiny in small],
        scratch_shapes=list(scratch),
        compiler_params=pltpu.CompilerParams(vmem_limit_bytes=VMEM_GRANT),
    )(*args)


def power_of_two(n):
    return n & (n - 1) == 0


def paired():
    ny, nz = lax.axis_size("gy"), lax.axis_size("gz")
    return nz == 2 and power_of_two(ny) and ny <= 8


def swap_pair(x):
    return lax.ppermute(x, "gz", [(0, 1), (1, 0)])


def send_along(x, k):
    ny = lax.axis_size("gy")
    return lax.ppermute(x, "gy", [(i, i ^ k) for i in range(ny)])


def send_rest(sent, rests, info):
    count = lax.axis_size("gy")
    parts = call(rest_kernel, [((ROWS // 2, sent.shape[1]), BF16)] * (count - 1), [sent, rests], plain=True)
    pieces = []
    for k in range(1, count):
        here = send_along(parts[k - 1], k)
        pieces += [here, swap_pair(here)]
    return call(rest_gather_kernel, [(sent.shape, BF16)], [info] + pieces, plain=True)[0]


def clear_kernel(out_ref):
    out_ref[...] = jnp.zeros(out_ref.shape, out_ref.dtype)


def no_rest(sent, rests, info):
    return call(clear_kernel, [(sent.shape, sent.dtype)], [], plain=True)[0]


def neighbours(payload, slots, faces):
    peers = lax.axis_size("gz")
    up = [(i, (i + 1) % peers) for i in range(peers)]
    down = [(j, i) for i, j in up]
    below = lax.ppermute(payload, "gz", up)
    above = lax.ppermute(payload, "gz", down)
    lane = lax.broadcasted_iota(jnp.int32, payload.shape, 1)
    return jnp.where(lane < slots + faces, above, below)


def per_device(adjoint, saved, inv_jac, stiffness, send_face, mortar_table, conf_faces):
    elements = adjoint.shape[0]
    sections = saved.shape[0]
    slots = send_face.shape[1]
    faces = conf_faces.shape[2]
    shared = -(-2 * faces // 128) * 128
    table = jnp.asarray(restriction_table())
    forward, backward = (jnp.asarray(t) for t in projection_tables())
    jac = inv_jac.reshape(1, elements)
    lam = jnp.transpose(adjoint, (1, 0, 2))
    states = jnp.transpose(saved, (0, 2, 1, 3))
    me = lax.axis_index(("gy", "gz")).astype(jnp.int32).reshape(1)
    rows = ((5, elements, ELEM), F32)
    sent = ((ROWS, slots), BF16)
    pair = ((ROWS, slots + shared), BF16)
    info_shape = ((EXTRA, slots), jnp.int32)

    mortars = jnp.transpose(mortar_table, (1, 0, 2))
    held = lambda x: (x.shape, x.dtype)
    outgoing, both, hot, lam, table = call(
        start_kernel,
        [((ROWS + EXTRA, slots), BF16), ((ROWS + EXTRA, slots + shared), BF16), ((6 * elements, slots + shared), BF16), held(lam), held(table)],
        [lam, send_face, conf_faces, mortars, table, me],
        scratch=(
            pltpu.VMEM(send_face.shape, jnp.int32),
            pltpu.VMEM(conf_faces.shape, jnp.int32),
            pltpu.VMEM(mortars.shape, jnp.int32),
            pltpu.VMEM((8, slots + shared), jnp.int32),
            pltpu.SemaphoreType.DMA((5,)),
        ),
        far=range(5),
        scalars=(5,),
    )
    values, held_stiff, forward, backward = call(
        state_kernel,
        [((sections, ROWS, slots + shared), BF16), ((2,) + stiffness.shape[1:], BF16), held(forward), held(backward)],
        [states, stiffness, forward, backward, hot, table],
        scratch=(pltpu.VMEM(states.shape, BF16), pltpu.SemaphoreType.DMA((4,))),
        far=range(4),
    )
    count = lax.axis_size("gy")
    parts = [outgoing] * (count - 1)
    packed = ((ROWS // 2, slots), BF16)
    chosen_shape = ((6 * elements, count * slots // 2), BF16)
    rests_shape = ((count * slots // 2, slots), BF16)
    for section in (2, 1, 0):
        relative = paired()
        if relative:
            column = [None] * (count - 1)
            for k in reversed(range(len(column))):
                column[k] = send_along(parts[k], k + 1)
            near = swap_pair(both)
        else:
            near = neighbours(both, slots, faces)
        (base,) = call(
            functools.partial(volume_kernel, section, slots, faces),
            [rows],
            [states, stiffness, lam, held_stiff, jac, both, near, values, hot, table],
            scratch=(
                pltpu.VMEM((3, 5 * elements, ELEM), F32),
                pltpu.VMEM((5 * elements, ELEM), F32),
                pltpu.VMEM(states.shape[1:], BF16),
                pltpu.VMEM(stiffness.shape[1:], BF16),
                pltpu.SemaphoreType.DMA((2,)),
            ),
            far=(0, 1),
        )
        if relative:
            pieces = [outgoing, near]
            for here in column:
                pieces += [here, swap_pair(here)]
        else:
            pieces = [lax.all_gather(outgoing, ("gy", "gz"), axis=0, tiled=False)]
        first, last = section == sections - 1, section == 0
        outs = [rows]
        if not last:
            outs += [sent, pair] + ([packed] * (count - 1) if relative else [])
        if first:
            outs = [info_shape] + ([chosen_shape, rests_shape, ((8, 128), F32)] if relative else []) + outs
        args = pieces + [outgoing, base, values, hot, table, jac, forward, backward]
        scalars = (len(args),) if first else ()
        args.append(me if first else info)
        if relative and not first:
            args.append(lax.cond(flag[0] > 0, send_rest, no_rest, outgoing, rests, info))
            args += [] if last else [chosen]
        out = call(
            functools.partial(mortar_update, section, relative, first, last, len(pieces)),
            outs, args, scalars=scalars, final=last,
        )
        if first:
            info, out = out[0], out[1:]
            if relative:
                (chosen, rests, excess), out = out[:3], out[3:]
                (flag,) = call(flag_kernel, [((1,), jnp.int32)], [excess])
        lam = out[0]
        if not last:
            outgoing, both, parts = out[1], out[2], out[3:]
    return jnp.transpose(lam, (1, 0, 2))


def solution(mesh):
    return jax.shard_map(
        per_device,
        mesh=mesh,
        in_specs=(
            P(("gx", "gy", "gz"), None, None),
            P(None, ("gx", "gy", "gz"), None, None),
            P(("gx", "gy", "gz")),
            P(),
            P(("gx", "gy", "gz"), None),
            P(("gx", "gy", "gz"), None, None),
            P(("gx", "gy", "gz"), None, None),
        ),
        out_specs=P(("gx", "gy", "gz"), None, None),
        check_vma=False,
    )
```

```python
import functools

import jax
import jax.numpy as jnp
import numpy as np
from jax import lax
from jax.experimental import pallas as pl
from jax.experimental.pallas import tpu as pltpu
from jax.sharding import PartitionSpec as P


ORDER = 7
LINE = ORDER + 1
FACE = LINE * LINE
ELEM = FACE * LINE
PAIRS = 3
TILE = 2 * FACE
ROWS = 5 * FACE
EXTRA = 16

gamma_gas = 1.4
penalty = 1.5
viscosity = 0.5
step_size = 0.2
section_weights = (0.25, 0.25, 0.5)
GM1 = gamma_gas - 1.0
REST = (1.0, 0.0, 0.0, 0.0, 2.5)
F32 = jnp.float32
VMEM_GRANT = 24 << 20
BF16 = jnp.bfloat16


def lagrange_matrix(points, abscissa):
    out = np.ones((LINE, LINE))
    for target in range(LINE):
        for other in range(LINE):
            if other != target:
                out[:, target] *= (points - abscissa[other]) / (abscissa[target] - abscissa[other])
    return out


def split_low(matrix):
    high = matrix.astype(np.float32).astype(BF16)
    low = (matrix - high.astype(np.float64)).astype(np.float32).astype(BF16)
    return high, low


def projection_tables():
    abscissa = -np.cos(np.pi * np.arange(LINE) / ORDER)
    halves = [lagrange_matrix((abscissa + 2.0 * h - 1.0) * 0.5, abscissa) for h in range(2)]
    children = [np.kron(halves[c // 2], halves[c % 2]) for c in range(4)]
    fh, fl = split_low(np.concatenate(children, axis=0))
    bh, bl = split_low(np.concatenate([m.T for m in children], axis=0))
    return np.concatenate([fh, fl], axis=1), np.concatenate([bh, bh, bl], axis=1)


def restriction_table():
    column = np.arange(6 * FACE)
    face, local = column // FACE, column % FACE
    first, second = local // LINE, local % LINE
    axis, fixed = face // 2, face % 2 * (LINE - 1)
    x = np.where(axis == 0, fixed, first)
    y = np.where(axis == 0, first, np.where(axis == 1, fixed, second))
    z = np.where(axis == 2, fixed, second)
    node = x * FACE + y * LINE + z
    return (np.arange(ELEM)[:, None] == node[None, :]).astype(np.float32).astype(BF16)


def dot(a, b, ca=1, cb=0):
    return lax.dot_general(a, b, (((ca,), (cb,)), ((), ())), preferred_element_type=F32)


def low_lanes(rows):
    return lax.broadcasted_iota(jnp.int32, (rows, TILE), 1) < FACE


def swap(x):
    return pltpu.roll(x, FACE, 1)


def exchange(a, b, low):
    return jnp.where(low, a, swap(b)), jnp.where(low, swap(a), b)


def flux_pull(u, w, picks):
    inv = 1.0 / u[0]
    vel = [u[i] * inv for i in (1, 2, 3)]
    kin = 0.5 * (vel[0] * vel[0] + vel[1] * vel[1] + vel[2] * vel[2])
    enth = gamma_gas * (u[4] * inv) - GM1 * kin
    q = w[1] * vel[0] + w[2] * vel[1] + w[3] * vel[2]
    if picks is None:
        vn, wn = vel[2], w[3]
    else:
        vn = jnp.where(picks[0], vel[0], jnp.where(picks[1], vel[1], vel[2]))
        wn = jnp.where(picks[0], w[1], jnp.where(picks[1], w[2], w[3]))
    r = vn * w[4]
    a = w[0] + q + enth * w[4]
    g = [GM1 * kin * wn - vn * q + (GM1 * kin - enth) * r]
    t = GM1 * (wn + r)
    for i in range(3):
        gi = w[1 + i] * vn - vel[i] * t
        if picks is None:
            gi = gi + a if i == 2 else gi
        else:
            gi = gi + jnp.where(picks[i], a, 0.0)
        g.append(gi)
    g.append(GM1 * wn + gamma_gas * r)
    return g


def trace_faces(field_low, table, elements):
    traced = dot(field_low, table)
    low = low_lanes(elements)
    zero = jnp.zeros((elements, TILE), F32)
    rows = [[None] * PAIRS for _ in range(6)]

    def piece(v, k):
        if v >= 5:
            return zero
        return traced[v * elements : (v + 1) * elements, k * TILE : (k + 1) * TILE]

    for j in range(PAIRS):
        for k in range(3):
            rows[2 * k][j], rows[2 * k + 1][j] = exchange(piece(2 * j, k), piece(2 * j + 1, k), low)
    return jnp.concatenate([jnp.concatenate(r, axis=1) for r in rows], axis=0).astype(BF16)


def lift_slots(grads, hot, table, elements):
    padded = jnp.concatenate([g.astype(BF16) for g in grads] + [jnp.zeros(grads[0].shape, BF16)], axis=0)
    face_grad = dot(hot, padded, 1, 1)
    low = low_lanes(elements)
    rows = [[None] * 3 for _ in range(6)]

    def piece(f, j):
        return face_grad[f * elements : (f + 1) * elements, j * TILE : (j + 1) * TILE]

    for j in range(PAIRS):
        for k in range(3):
            rows[2 * j][k], rows[2 * j + 1][k] = exchange(piece(2 * k, j), piece(2 * k + 1, j), low)
    arranged = jnp.concatenate([jnp.concatenate(r, axis=1) for r in rows[:5]], axis=0).astype(BF16)
    return dot(arranged, table, 1, 1)


def column_of(row):
    n = row.shape[1]
    same = lax.broadcasted_iota(jnp.int32, (n, n), 0) == lax.broadcasted_iota(jnp.int32, (n, n), 1)
    return jnp.sum(jnp.where(same, jnp.broadcast_to(row, (n, n)), 0.0), axis=1, keepdims=True)


def slot_values(field_low, hot, table, elements):
    return dot(trace_faces(field_low, table, elements), hot, 0, 0)[:ROWS]


def pack_halves(values):
    low = low_lanes(ROWS // 2)
    out = []
    for tile in range(values.shape[1] // TILE):
        part = values[:, tile * TILE : (tile + 1) * TILE]
        out += [x.astype(BF16) for x in exchange(part[: ROWS // 2], part[ROWS // 2 :], low)]
    return out


def unpack_halves(a, b):
    return jnp.concatenate(exchange(a.astype(F32), b.astype(F32), low_lanes(ROWS // 2)), axis=0).astype(BF16)


def fetch(pairs, sems):
    copies = [pltpu.make_async_copy(a, b, sems.at[i]) for i, (a, b) in enumerate(pairs)]
    for copy in copies:
        copy.start()
    return copies


def start_kernel(lam_hbm, send_hbm, conf_hbm, map_hbm, table_hbm, me_ref, out_ref, pair_ref, hot_ref, lam_ref, table_ref, send_ref, conf_ref, map_ref, ids_ref, sems):
    pairs = ((send_hbm, send_ref), (conf_hbm, conf_ref), (map_hbm, map_ref), (lam_hbm, lam_ref), (table_hbm, table_ref))
    copies = fetch(pairs, sems)
    elements = lam_ref.shape[1]
    slots = send_ref.shape[1]
    faces = conf_ref.shape[2]
    ids_ref[...] = jnp.full(ids_ref.shape, -1, jnp.int32)
    for copy in copies[:3]:
        copy.wait()
    ids_ref[0:1, 0:slots] = send_ref[...]
    ids_ref[0:1, slots : slots + faces] = conf_ref[0, 0:1]
    ids_ref[0:1, slots + faces : slots + 2 * faces] = conf_ref[0, 1:2]
    shape = hot_ref.shape
    row = lax.broadcasted_iota(jnp.int32, shape, 0)
    face = row // elements
    ident = 6 * (row - face * elements) + face
    hot = jnp.where(ident == ids_ref[0:1], 1.0, 0.0).astype(BF16)
    hot_ref[...] = hot
    rows = [map_ref[k] for k in range(5)]
    mortars = rows[0].shape[1]
    slot = lax.broadcasted_iota(jnp.int32, (slots, mortars), 0)
    field = lax.broadcasted_iota(jnp.int32, (EXTRA, mortars), 0)
    known = jnp.where(field == 1, rows[2], jnp.where(field == 2, rows[3], jnp.where(field == 3, rows[4], 0)))
    info = None
    for mine, other, left in ((0, 1, 1), (1, 0, 0)):
        hits = jnp.where(slot == rows[mine], 1.0, 0.0).astype(BF16)
        fields = jnp.where(field == 0, rows[other], jnp.where(field == 4, left, known))
        part = dot(fields.astype(F32).astype(BF16), hits, 1, 1)
        info = part if info is None else info + part
    out_ref[ROWS:] = info.astype(BF16)
    pair_ref[ROWS:, :slots] = info.astype(BF16)
    pair_ref[ROWS:, slots:] = jnp.zeros((EXTRA, pair_ref.shape[1] - slots), BF16)
    for copy in copies[3:]:
        copy.wait()
    lam_low = lam_ref[...].astype(BF16).reshape(5 * elements, ELEM)
    values = slot_values(lam_low, hot, table_ref[...], elements).astype(BF16)
    out_ref[0:ROWS] = values[:, :slots]
    pair_ref[0:ROWS] = values


def state_kernel(saved_hbm, stiff_hbm, forward_hbm, backward_hbm, hot_ref, table_ref, out_ref, stiff_ref, forward_ref, backward_ref, saved_ref, sems):
    pairs = ((saved_hbm, saved_ref), (stiff_hbm.at[0 : stiff_ref.shape[0]], stiff_ref), (forward_hbm, forward_ref), (backward_hbm, backward_ref))
    copies = fetch(pairs, sems)
    copies[0].wait()
    elements = saved_ref.shape[2]
    for s in range(saved_ref.shape[0]):
        values = slot_values(saved_ref[s].reshape(5 * elements, ELEM), hot_ref[...], table_ref[...], elements)
        out_ref[s] = values.astype(BF16)
    for copy in copies[1:]:
        copy.wait()


def volume_kernel(section, slots, faces, saved_hbm, stiff_hbm, lam_ref, held_ref, jac_ref, own_ref, near_ref, state_ref, hot_ref, table_ref, base_ref, slope_ref, smooth_ref, saved_ref, stiff_ref, sems):
    held = held_ref.shape[0]
    copies = fetch(((stiff_hbm.at[held], stiff_ref), (saved_hbm.at[section], saved_ref)), sems)
    elements = lam_ref.shape[1]
    coef = step_size * section_weights[section]
    lam_low = lam_ref[...].astype(BF16).reshape(5 * elements, ELEM)

    width = own_ref.shape[1] - slots
    lane = lax.broadcasted_iota(jnp.int32, (FACE, width), 1)
    used = lane < 2 * faces
    lower = lane < faces
    sign = jnp.where(lower, -1.0, 1.0)
    w, u = [], []
    for v in range(5):
        rows = slice(v * FACE, (v + 1) * FACE)
        near = near_ref[rows, slots:].astype(F32)
        near = jnp.where(lower, pltpu.roll(near, width - faces, 1), pltpu.roll(near, faces, 1))
        w.append(jnp.where(used, sign * (near - own_ref[rows, slots:].astype(F32)), 0.0))
        u.append(jnp.where(used, state_ref[section, rows, slots:].astype(F32), REST[v]))
    g = flux_pull(u, w, None)
    grads = [0.5 * g[v] + (0.5 * penalty) * sign * w[v] for v in range(5)]
    total = viscosity * -1.0
    smooth = lift_slots(grads, hot_ref[:, slots:], table_ref[...], elements)
    for d in range(3):
        if d == held:
            copies[0].wait()
        stiff = held_ref[d] if d < held else stiff_ref[...]
        slopes = dot(lam_low, stiff)
        slope_ref[d] = slopes
        smooth = smooth + total * dot(slopes.astype(BF16), stiff, 1, 1)
    smooth_ref[...] = smooth
    copies[1].wait()
    jac = column_of(jac_ref[...]) * coef
    step = 16
    for r in range(0, elements, step):
        scale = jnp.broadcast_to(jac[r : r + step], (step, 128))
        for c in range(0, ELEM, 128):
            u = [saved_ref[v, r : r + step, c : c + 128].astype(F32) for v in range(5)]
            inv = 1.0 / u[0]
            vel = [u[i] * inv for i in (1, 2, 3)]
            kin = 0.5 * (vel[0] * vel[0] + vel[1] * vel[1] + vel[2] * vel[2])
            enth = gamma_gas * (u[4] * inv) - GM1 * kin
            trace = run = first = None
            g = [None, None, None, None]
            for d in range(3):
                w = [slope_ref[d, v * elements + r : v * elements + r + step, c : c + 128] for v in range(5)]
                q = w[1] * vel[0] + w[2] * vel[1] + w[3] * vel[2]
                term = vel[d] * q
                first = term if first is None else first + term
                trace = w[1 + d] if trace is None else trace + w[1 + d]
                part = vel[d] * w[4]
                run = part if run is None else run + part
                for i in range(3):
                    gi = w[1 + i] * vel[d]
                    if i == d:
                        gi = gi + (w[0] + q + enth * w[4])
                    g[1 + i] = gi if g[1 + i] is None else g[1 + i] + gi
            t = GM1 * (trace + run)
            pulled = [GM1 * kin * trace - first + (GM1 * kin - enth) * run]
            pulled += [g[1 + i] - vel[i] * t for i in range(3)]
            pulled.append(GM1 * trace + gamma_gas * run)
            for v in range(5):
                rows = slice(v * elements + r, v * elements + r + step)
                vol = pulled[v] + smooth_ref[rows, c : c + 128]
                base_ref[v, r : r + step, c : c + 128] = lam_ref[v, r : r + step, c : c + 128] + scale * vol


def spread_children(matrix, stacked):
    return dot(matrix, jnp.concatenate(stacked, axis=0))


def choose(raw, spread, child, keep=None):
    out = []
    for v, value in enumerate(raw):
        width = value.shape[1]
        picked = value
        for c in range(4):
            hit = child[c] if keep is None else child[c] & keep
            picked = jnp.where(hit, spread[c * FACE : (c + 1) * FACE, v * width : (v + 1) * width], picked)
        out.append(picked)
    return out


def read_table(pieces, me_ref, cap, relative):
    slots = pieces[0].shape[1]
    me = me_ref[0]
    lane = lax.broadcasted_iota(jnp.int32, (EXTRA, slots), 1)
    owner_of = lane // cap
    info = jnp.zeros((EXTRA, slots), F32)
    for p, piece in enumerate(pieces):
        owner = me ^ p if relative else p
        shift = lax.rem((owner - me) * cap + slots, slots)
        moved = pltpu.roll(piece[ROWS:].astype(F32), shift, 1)
        info = jnp.where(owner_of == owner, moved, info)
    info = info.astype(jnp.int32)
    source = info[0:1] // cap
    rank = info[0:1] - source * cap
    if relative:
        source = source ^ me
    code = source * slots + owner_of[0:1] * cap + rank
    field = lax.broadcasted_iota(jnp.int32, (EXTRA, slots), 0)
    return jnp.where(field == 0, code, info)


def route(pieces, me, cap):
    slots, devices = pieces[0].shape[1], len(pieces)
    half = slots // 2
    lane = lax.broadcasted_iota(jnp.int32, (devices, slots), 1)
    device = devices - 1 - lax.broadcasted_iota(jnp.int32, (devices, slots), 0)
    partner = jnp.zeros((devices, slots), F32)
    for p, piece in enumerate(pieces):
        owner = me ^ p
        fields = piece[ROWS:].astype(F32)
        mine = jnp.where(fields[3:4] == 1.0, fields[0:1], float(slots))
        turned = pltpu.roll(jnp.broadcast_to(mine, (devices, slots)), lax.rem((owner + 1) * cap, slots), 1)
        moved = pltpu.roll(turned, 0, 1, stride=cap, stride_axis=0)
        partner = jnp.where(lane // cap == owner, moved, partner)
    partner = partner.astype(jnp.int32)
    chip = partner // (2 * cap)
    wanted = [(partner < slots) & (chip == t) & (device // 2 != t) for t in range(devices // 2)]
    wanted = jnp.concatenate([jnp.where(x, 1.0, 0.0) for x in wanted], axis=0)
    before = lax.broadcasted_iota(jnp.int32, (slots, slots), 0) < lax.broadcasted_iota(jnp.int32, (slots, slots), 1)
    rank = dot(wanted.astype(BF16), jnp.where(before, 1.0, 0.0).astype(BF16))
    most = jnp.max(jnp.sum(wanted, axis=1, keepdims=True))
    index = lax.broadcasted_iota(jnp.int32, wanted.shape, 0)

    def row(x, t, q):
        return jnp.sum(jnp.where(index == t * devices + devices - 1 - q, x, 0.0), axis=0, keepdims=True)

    here = me // 2
    place = lax.broadcasted_iota(jnp.int32, (half, slots), 0).astype(F32)
    picks, rests = [], []
    for k in range(1, devices // 2):
        mine = jnp.where(row(wanted, here ^ k, me) > 0.0, row(rank, here ^ k, me), -1.0)
        picks.append(jnp.where(place == mine, 1.0, 0.0))
        rests.append(jnp.where(place + half == mine, 1.0, 0.0))
    picks.append(jnp.zeros_like(picks[0]))
    rests.append(jnp.zeros_like(picks[0]))
    coming = [row(rank, here, me ^ p) for p in range(devices)]
    return jnp.concatenate(picks, axis=0).astype(BF16), jnp.concatenate(rests, axis=0).astype(BF16), coming, most


def gather_lanes(blocks, codes, start=0):
    out = None
    for block in blocks:
        width = block.shape[1]
        place = lax.broadcasted_iota(jnp.int32, (width, codes.shape[1]), 0) + start
        part = dot(block, jnp.where(place == codes, 1.0, 0.0).astype(BF16))
        out = part if out is None else out + part
        start += width
    return out


def flag_kernel(excess_ref, flag_ref):
    flag_ref[0] = (jnp.max(excess_ref[...]) > 0.0).astype(jnp.int32)


def rest_kernel(sent_ref, rests_ref, *outs):
    for out, value in zip(outs, pack_halves(dot(sent_ref[...], rests_ref[...], 1, 1))):
        out[...] = value


def rest_gather_kernel(info_ref, *refs):
    blocks = [unpack_halves(refs[i][...], refs[i + 1][...]) for i in range(0, len(refs) - 1, 2)]
    refs[-1][...] = gather_lanes(blocks, info_ref[6:7]).astype(BF16)


def unpack_all(pieces):
    pieces = pieces + pieces[-1:] * (len(pieces) % 2)
    return [unpack_halves(pieces[p], pieces[p + 1]) for p in range(0, len(pieces), 2)]


def early_kernel(section, own_ref, near_ref, info_ref, state_ref, forward_ref, *refs):
    slots = own_ref.shape[1]
    part_ref, left_ref, here_ref = refs[-3:]
    info = info_ref[...]
    pieces = [r[...] for r in refs[:-3]]
    blocks = [jnp.concatenate([own_ref[...], near_ref[:, :slots]], axis=1)] + unpack_all(pieces)
    part_ref[...] = gather_lanes(blocks, info[5:6]).astype(BF16)
    child, left = (jnp.broadcast_to(info[k : k + 1], (FACE, slots)) for k in (1, 4))
    child = [child == c + 1 for c in range(4)]
    raw = [own_ref[v * FACE : (v + 1) * FACE] for v in range(5)]
    raw += [state_ref[section, v * FACE : (v + 1) * FACE, :slots] for v in range(5)]
    stacked = jnp.concatenate(raw, axis=1)
    spread = spread_children(forward_ref[...], [stacked, stacked])
    values = [x.astype(F32) for x in raw]
    for v, x in enumerate(choose(values[:5], spread, child)):
        left_ref[v * FACE : (v + 1) * FACE] = x
    for v, x in enumerate(choose(values[5:], spread[:, 5 * slots :], child, left == 1)):
        here_ref[v * FACE : (v + 1) * FACE] = x


def mortar_update(section, relative, first, last, count, *refs):
    compact = relative and not first
    slots = refs[count].shape[1]
    half = slots // 2
    pieces = [r[...] if len(r.shape) == 3 or r.shape[0] < ROWS else r[:, :slots] for r in refs[:count]]
    own_ref = refs[count]
    base_ref, state_ref, hot_ref, table_ref, jac_ref, forward_ref, backward_ref = refs[count + 1 : count + 8]
    me_ref, *outs = refs[count + 8 :] if first else (None,) + refs[count + 8 :]
    elements = base_ref.shape[1]
    if len(pieces) == 1 and pieces[0].ndim == 3:
        pieces = [pieces[0][p] for p in range(pieces[0].shape[0])]
    hot = hot_ref[...]
    if first:
        cap = slots // len(pieces)
        info = read_table(pieces, me_ref, cap, relative)
    else:
        info = outs[0][...]
        outs = outs[1:]
    if first and relative:
        picks, rests, coming, most = route(pieces, me_ref[0], cap)
        extended = []
        for piece, ranks in zip(pieces, coming):
            extra = jnp.broadcast_to(ranks, (EXTRA, slots)).astype(BF16)
            extended.append(jnp.concatenate([piece[:ROWS], extra], axis=0))
        blocks = [jnp.concatenate(extended[p : p + 2], axis=1) for p in range(0, len(pieces), 2)]
        partner = gather_lanes(blocks, info[0:1])
        rank = partner[ROWS : ROWS + 1].astype(jnp.int32)
        partner = partner[:ROWS]
        piece_of = info[0:1] // slots
        far = (piece_of >= 2) & (info[3:4] == 1)
        passed = piece_of % 2
        packed = 2 * slots + (passed * (len(pieces) // 2) + piece_of // 2 - 1) * half + rank
        near_code = jnp.where(far & (rank < half), packed, jnp.where(far, -1, info[0:1]))
        rest_code = jnp.where(far & (rank >= half), (piece_of - 3) * half + rank, -1)
        field = lax.broadcasted_iota(jnp.int32, info.shape, 0)
        info = jnp.where(field == 5, near_code, jnp.where(field == 6, rest_code, info))
        chosen = dot(hot[:, :slots], picks, 1, 1).astype(BF16)
        outs[1][...] = chosen
        outs[2][...] = rests
        outs[3][...] = jnp.full(outs[3].shape, most - half, F32)
    elif compact:
        start = 2 * slots + (len(pieces) + 1) * half
        partner = gather_lanes(unpack_all(pieces), info[5:6], start)
        more_ref, part_ref, left_ref, state_here_ref, *outs = outs
        partner = partner + part_ref[...].astype(F32) + more_ref[...].astype(F32)
        if not last:
            chosen = outs[0][...]
            outs = outs[1:]
    else:
        blocks = [jnp.concatenate([pieces[p][:ROWS], pieces[p + 1][:ROWS]], axis=1) for p in range(0, len(pieces), 2)]
        partner = gather_lanes(blocks, info[0:1])
    if first:
        outs[0][...] = info
        outs = outs[4:] if relative else outs[1:]
    child, axis, live, left = (jnp.broadcast_to(info[k : k + 1], (FACE, slots)) for k in range(1, 5))
    is_left = left == 1
    alive = live == 1
    child = [child == c + 1 for c in range(4)]
    picks = [axis == n for n in range(3)]

    def variables(x):
        return [x[v * FACE : (v + 1) * FACE].astype(F32) for v in range(5)]

    own, partner = variables(own_ref[:ROWS]), variables(partner)
    right_lam = [jnp.where(is_left, b, a) for a, b in zip(own, partner)]
    if compact:
        stacked = jnp.concatenate([x.astype(BF16) for x in partner], axis=1)
        projected = choose(partner, spread_children(forward_ref[...], [stacked, stacked]), child)
        left_lam = [jnp.where(is_left, a, b) for a, b in zip(variables(left_ref[...]), projected)]
        u = variables(state_here_ref[...])
    else:
        state = variables(state_ref[section][:, :slots])
        left_lam = [jnp.where(is_left, a, b) for a, b in zip(own, partner)]
        stacked = jnp.concatenate([x.astype(BF16) for x in left_lam + state], axis=1)
        spread = spread_children(forward_ref[...], [stacked, stacked])
        left_lam = choose(left_lam, spread, child)
        u = choose(state, spread[:, 5 * slots :], child, is_left)
    w = [jnp.where(alive, b - a, 0.0) for a, b in zip(left_lam, right_lam)]
    u = [jnp.where(alive, u[v], REST[v]) for v in range(5)]
    g = flux_pull(u, w, picks)
    side = jnp.where(is_left, 0.5 * penalty, -0.5 * penalty)
    pull = [0.5 * g[v] + side * w[v] for v in range(5)]
    stacked = jnp.concatenate(pull, axis=1)
    high = stacked.astype(BF16)
    rest = (stacked - high.astype(F32)).astype(BF16)
    spread = spread_children(backward_ref[...], [high, rest, high])
    grads = choose(pull, spread, child, is_left)

    table = table_ref[...]
    lifted = lift_slots(grads, hot[:, :slots], table, elements)
    jac = column_of(jac_ref[...]) * (step_size * section_weights[section])
    lam = [base_ref[v] + jac * lifted[v * elements : (v + 1) * elements] for v in range(5)]
    for v in range(5):
        outs[0][v] = lam[v]
    if not last:
        lam_low = jnp.concatenate([x.astype(BF16) for x in lam], axis=0)
        if relative:
            hot = jnp.concatenate([hot, chosen], axis=1)
        values = slot_values(lam_low, hot, table, elements)
        both = outs[2].shape[1]
        outs[1][...] = values[:, :slots].astype(BF16)
        outs[2][...] = values[:, :both].astype(BF16)
        if relative:
            for out, value in zip(outs[3:], pack_halves(values[:, both:])):
                out[...] = value


def call(kernel, outs, args, scratch=(), scalars=(), far=(), plain=False, final=False):
    def space(i):
        return pltpu.HBM if i in far else pltpu.SMEM if i in scalars else pltpu.VMEM

    if not plain:
        args = [a if i in scalars else pltpu.with_memory_space_constraint(a, space(i)) for i, a in enumerate(args)]
    small = [o == (1,) for o, _ in outs]
    shapes = [jax.ShapeDtypeStruct(o, t) if plain or final or tiny else pltpu.VMEM(o, t) for (o, t), tiny in zip(outs, small)]
    return pl.pallas_call(
        kernel,
        out_shape=shapes,
        in_specs=[pl.BlockSpec(memory_space=space(i)) for i in range(len(args))],
        out_specs=[pl.BlockSpec(memory_space=pltpu.SMEM if tiny else pltpu.VMEM) for tiny in small],
        scratch_shapes=list(scratch),
        compiler_params=pltpu.CompilerParams(vmem_limit_bytes=VMEM_GRANT),
    )(*args)


def power_of_two(n):
    return n & (n - 1) == 0


def paired():
    ny, nz = lax.axis_size("gy"), lax.axis_size("gz")
    return nz == 2 and power_of_two(ny) and ny <= 8


def swap_pair(x):
    return lax.ppermute(x, "gz", [(0, 1), (1, 0)])


def send_along(x, k):
    ny = lax.axis_size("gy")
    return lax.ppermute(x, "gy", [(i, i ^ k) for i in range(ny)])


def send_rest(sent, rests, info):
    count = lax.axis_size("gy")
    parts = call(rest_kernel, [((ROWS // 2, sent.shape[1]), BF16)] * (count - 1), [sent, rests], plain=True)
    pieces = []
    for k in range(1, count):
        here = send_along(parts[k - 1], k)
        pieces += [here, swap_pair(here)]
    return call(rest_gather_kernel, [(sent.shape, BF16)], [info] + pieces, plain=True)[0]


def clear_kernel(out_ref):
    out_ref[...] = jnp.zeros(out_ref.shape, out_ref.dtype)


def no_rest(sent, rests, info):
    return call(clear_kernel, [(sent.shape, sent.dtype)], [], plain=True)[0]


def neighbours(payload, slots, faces):
    peers = lax.axis_size("gz")
    up = [(i, (i + 1) % peers) for i in range(peers)]
    down = [(j, i) for i, j in up]
    below = lax.ppermute(payload, "gz", up)
    above = lax.ppermute(payload, "gz", down)
    lane = lax.broadcasted_iota(jnp.int32, payload.shape, 1)
    return jnp.where(lane < slots + faces, above, below)


def per_device(adjoint, saved, inv_jac, stiffness, send_face, mortar_table, conf_faces):
    elements = adjoint.shape[0]
    sections = saved.shape[0]
    slots = send_face.shape[1]
    faces = conf_faces.shape[2]
    shared = -(-2 * faces // 128) * 128
    table = jnp.asarray(restriction_table())
    forward, backward = (jnp.asarray(t) for t in projection_tables())
    jac = inv_jac.reshape(1, elements)
    lam = jnp.transpose(adjoint, (1, 0, 2))
    states = jnp.transpose(saved, (0, 2, 1, 3))
    me = lax.axis_index(("gy", "gz")).astype(jnp.int32).reshape(1)
    rows = ((5, elements, ELEM), F32)
    sent = ((ROWS, slots), BF16)
    pair = ((ROWS, slots + shared), BF16)
    info_shape = ((EXTRA, slots), jnp.int32)

    mortars = jnp.transpose(mortar_table, (1, 0, 2))
    held = lambda x: (x.shape, x.dtype)
    outgoing, both, hot, lam, table = call(
        start_kernel,
        [((ROWS + EXTRA, slots), BF16), ((ROWS + EXTRA, slots + shared), BF16), ((6 * elements, slots + shared), BF16), held(lam), held(table)],
        [lam, send_face, conf_faces, mortars, table, me],
        scratch=(
            pltpu.VMEM(send_face.shape, jnp.int32),
            pltpu.VMEM(conf_faces.shape, jnp.int32),
            pltpu.VMEM(mortars.shape, jnp.int32),
            pltpu.VMEM((8, slots + shared), jnp.int32),
            pltpu.SemaphoreType.DMA((5,)),
        ),
        far=range(5),
        scalars=(5,),
    )
    values, held_stiff, forward, backward = call(
        state_kernel,
        [((sections, ROWS, slots + shared), BF16), ((2,) + stiffness.shape[1:], BF16), held(forward), held(backward)],
        [states, stiffness, forward, backward, hot, table],
        scratch=(pltpu.VMEM(states.shape, BF16), pltpu.SemaphoreType.DMA((4,))),
        far=range(4),
    )
    count = lax.axis_size("gy")
    parts = [outgoing] * (count - 1)
    packed = ((ROWS // 2, slots), BF16)
    chosen_shape = ((6 * elements, count * slots // 2), BF16)
    rests_shape = ((count * slots // 2, slots), BF16)
    for section in (2, 1, 0):
        relative = paired()
        if relative:
            column = [None] * (count - 1)
            for k in reversed(range(len(column))):
                column[k] = send_along(parts[k], k + 1)
            near = swap_pair(both)
        else:
            near = neighbours(both, slots, faces)
        (base,) = call(
            functools.partial(volume_kernel, section, slots, faces),
            [rows],
            [states, stiffness, lam, held_stiff, jac, both, near, values, hot, table],
            scratch=(
                pltpu.VMEM((3, 5 * elements, ELEM), F32),
                pltpu.VMEM((5 * elements, ELEM), F32),
                pltpu.VMEM(states.shape[1:], BF16),
                pltpu.VMEM(stiffness.shape[1:], BF16),
                pltpu.SemaphoreType.DMA((2,)),
            ),
            far=(0, 1),
        )
        if relative:
            pieces = [outgoing, near]
            for here in column:
                pieces += [here, swap_pair(here)]
        else:
            pieces = [lax.all_gather(outgoing, ("gy", "gz"), axis=0, tiled=False)]
        first, last = section == sections - 1, section == 0
        outs = [rows]
        if not last:
            outs += [sent, pair] + ([packed] * (count - 1) if relative else [])
        if first:
            outs = [info_shape] + ([chosen_shape, rests_shape, ((8, 128), F32)] if relative else []) + outs
        compact = relative and not first
        if compact:
            wide = ((ROWS, slots), F32)
            early = call(
                functools.partial(early_kernel, section),
                [sent, wide, wide],
                [outgoing, near, info, values, forward] + column,
            )
            pieces = pieces[3::2]
        args = pieces + [outgoing, base, values, hot, table, jac, forward, backward]
        scalars = (len(args),) if first else ()
        args.append(me if first else info)
        if compact:
            args.append(lax.cond(flag[0] > 0, send_rest, no_rest, outgoing, rests, info))
            args += list(early) + ([] if last else [chosen])
        out = call(
            functools.partial(mortar_update, section, relative, first, last, len(pieces)),
            outs, args, scalars=scalars, final=last,
        )
        if first:
            info, out = out[0], out[1:]
            if relative:
                (chosen, rests, excess), out = out[:3], out[3:]
                (flag,) = call(flag_kernel, [((1,), jnp.int32)], [excess])
        lam = out[0]
        if not last:
            outgoing, both, parts = out[1], out[2], out[3:]
    return jnp.transpose(lam, (1, 0, 2))


def solution(mesh):
    return jax.shard_map(
        per_device,
        mesh=mesh,
        in_specs=(
            P(("gx", "gy", "gz"), None, None),
            P(None, ("gx", "gy", "gz"), None, None),
            P(("gx", "gy", "gz")),
            P(),
            P(("gx", "gy", "gz"), None),
            P(("gx", "gy", "gz"), None, None),
            P(("gx", "gy", "gz"), None, None),
        ),
        out_specs=P(("gx", "gy", "gz"), None, None),
        check_vma=False,
    )
```

```python
import functools

import jax
import jax.numpy as jnp
import numpy as np
from jax import lax
from jax.experimental import pallas as pl
from jax.experimental.pallas import tpu as pltpu
from jax.sharding import PartitionSpec as P


ORDER = 7
LINE = ORDER + 1
FACE = LINE * LINE
ELEM = FACE * LINE
PAIRS = 3
TILE = 2 * FACE
ROWS = 5 * FACE
EXTRA = 16

gamma_gas = 1.4
penalty = 1.5
viscosity = 0.5
step_size = 0.2
section_weights = (0.25, 0.25, 0.5)
GM1 = gamma_gas - 1.0
REST = (1.0, 0.0, 0.0, 0.0, 2.5)
F32 = jnp.float32
VMEM_GRANT = 24 << 20
BF16 = jnp.bfloat16


def lagrange_matrix(points, abscissa):
    out = np.ones((LINE, LINE))
    for target in range(LINE):
        for other in range(LINE):
            if other != target:
                out[:, target] *= (points - abscissa[other]) / (abscissa[target] - abscissa[other])
    return out


def split_low(matrix):
    high = matrix.astype(np.float32).astype(BF16)
    low = (matrix - high.astype(np.float64)).astype(np.float32).astype(BF16)
    return high, low


def projection_tables():
    abscissa = -np.cos(np.pi * np.arange(LINE) / ORDER)
    halves = [lagrange_matrix((abscissa + 2.0 * h - 1.0) * 0.5, abscissa) for h in range(2)]
    children = [np.kron(halves[c // 2], halves[c % 2]) for c in range(4)]
    fh, fl = split_low(np.concatenate(children, axis=0))
    bh, bl = split_low(np.concatenate([m.T for m in children], axis=0))
    return np.concatenate([fh, fl], axis=1), np.concatenate([bh, bl], axis=1)


def restriction_table():
    column = np.arange(6 * FACE)
    face, local = column // FACE, column % FACE
    first, second = local // LINE, local % LINE
    axis, fixed = face // 2, face % 2 * (LINE - 1)
    x = np.where(axis == 0, fixed, first)
    y = np.where(axis == 0, first, np.where(axis == 1, fixed, second))
    z = np.where(axis == 2, fixed, second)
    node = x * FACE + y * LINE + z
    return (np.arange(ELEM)[:, None] == node[None, :]).astype(np.float32).astype(BF16)


def dot(a, b, ca=1, cb=0):
    return lax.dot_general(a, b, (((ca,), (cb,)), ((), ())), preferred_element_type=F32)


def low_lanes(rows):
    return lax.broadcasted_iota(jnp.int32, (rows, TILE), 1) < FACE


def swap(x):
    return pltpu.roll(x, FACE, 1)


def exchange(a, b, low):
    return jnp.where(low, a, swap(b)), jnp.where(low, swap(a), b)


def flux_pull(u, w, picks):
    inv = 1.0 / u[0]
    vel = [u[i] * inv for i in (1, 2, 3)]
    kin = 0.5 * (vel[0] * vel[0] + vel[1] * vel[1] + vel[2] * vel[2])
    enth = gamma_gas * (u[4] * inv) - GM1 * kin
    q = w[1] * vel[0] + w[2] * vel[1] + w[3] * vel[2]
    if picks is None:
        vn, wn = vel[2], w[3]
    else:
        vn = jnp.where(picks[0], vel[0], jnp.where(picks[1], vel[1], vel[2]))
        wn = jnp.where(picks[0], w[1], jnp.where(picks[1], w[2], w[3]))
    r = vn * w[4]
    a = w[0] + q + enth * w[4]
    g = [GM1 * kin * wn - vn * q + (GM1 * kin - enth) * r]
    t = GM1 * (wn + r)
    for i in range(3):
        gi = w[1 + i] * vn - vel[i] * t
        if picks is None:
            gi = gi + a if i == 2 else gi
        else:
            gi = gi + jnp.where(picks[i], a, 0.0)
        g.append(gi)
    g.append(GM1 * wn + gamma_gas * r)
    return g


def trace_faces(field_low, table, elements):
    traced = dot(field_low, table)
    low = low_lanes(elements)
    zero = jnp.zeros((elements, TILE), F32)
    rows = [[None] * PAIRS for _ in range(6)]

    def piece(v, k):
        if v >= 5:
            return zero
        return traced[v * elements : (v + 1) * elements, k * TILE : (k + 1) * TILE]

    for j in range(PAIRS):
        for k in range(3):
            rows[2 * k][j], rows[2 * k + 1][j] = exchange(piece(2 * j, k), piece(2 * j + 1, k), low)
    return jnp.concatenate([jnp.concatenate(r, axis=1) for r in rows], axis=0).astype(BF16)


def lift_slots(grads, hot, table, elements):
    padded = jnp.concatenate([g.astype(BF16) for g in grads] + [jnp.zeros(grads[0].shape, BF16)], axis=0)
    face_grad = dot(hot, padded, 1, 1)
    low = low_lanes(elements)
    rows = [[None] * 3 for _ in range(6)]

    def piece(f, j):
        return face_grad[f * elements : (f + 1) * elements, j * TILE : (j + 1) * TILE]

    for j in range(PAIRS):
        for k in range(3):
            rows[2 * j][k], rows[2 * j + 1][k] = exchange(piece(2 * k, j), piece(2 * k + 1, j), low)
    arranged = jnp.concatenate([jnp.concatenate(r, axis=1) for r in rows[:5]], axis=0).astype(BF16)
    return dot(arranged, table, 1, 1)


def column_of(row):
    n = row.shape[1]
    same = lax.broadcasted_iota(jnp.int32, (n, n), 0) == lax.broadcasted_iota(jnp.int32, (n, n), 1)
    return jnp.sum(jnp.where(same, jnp.broadcast_to(row, (n, n)), 0.0), axis=1, keepdims=True)


def slot_values(field_low, hot, table, elements):
    return dot(trace_faces(field_low, table, elements), hot, 0, 0)[:ROWS]


def pack_halves(values):
    low = low_lanes(ROWS // 2)
    out = []
    for tile in range(values.shape[1] // TILE):
        part = values[:, tile * TILE : (tile + 1) * TILE]
        out += [x.astype(BF16) for x in exchange(part[: ROWS // 2], part[ROWS // 2 :], low)]
    return out


def unpack_halves(a, b):
    return jnp.concatenate(exchange(a.astype(F32), b.astype(F32), low_lanes(ROWS // 2)), axis=0).astype(BF16)


def fetch(pairs, sems):
    copies = [pltpu.make_async_copy(a, b, sems.at[i]) for i, (a, b) in enumerate(pairs)]
    for copy in copies:
        copy.start()
    return copies


def start_kernel(lam_hbm, send_hbm, conf_hbm, map_hbm, table_hbm, me_ref, out_ref, pair_ref, hot_ref, lam_ref, table_ref, send_ref, conf_ref, map_ref, ids_ref, sems):
    pairs = ((send_hbm, send_ref), (conf_hbm, conf_ref), (map_hbm, map_ref), (lam_hbm, lam_ref), (table_hbm, table_ref))
    copies = fetch(pairs, sems)
    elements = lam_ref.shape[1]
    slots = send_ref.shape[1]
    faces = conf_ref.shape[2]
    ids_ref[...] = jnp.full(ids_ref.shape, -1, jnp.int32)
    for copy in copies[:3]:
        copy.wait()
    ids_ref[0:1, 0:slots] = send_ref[...]
    ids_ref[0:1, slots : slots + faces] = conf_ref[0, 0:1]
    ids_ref[0:1, slots + faces : slots + 2 * faces] = conf_ref[0, 1:2]
    shape = hot_ref.shape
    row = lax.broadcasted_iota(jnp.int32, shape, 0)
    face = row // elements
    ident = 6 * (row - face * elements) + face
    hot = jnp.where(ident == ids_ref[0:1], 1.0, 0.0).astype(BF16)
    hot_ref[...] = hot
    rows = [map_ref[k] for k in range(5)]
    mortars = rows[0].shape[1]
    slot = lax.broadcasted_iota(jnp.int32, (slots, mortars), 0)
    field = lax.broadcasted_iota(jnp.int32, (EXTRA, mortars), 0)
    known = jnp.where(field == 1, rows[2], jnp.where(field == 2, rows[3], jnp.where(field == 3, rows[4], 0)))
    info = None
    for mine, other, left in ((0, 1, 1), (1, 0, 0)):
        hits = jnp.where(slot == rows[mine], 1.0, 0.0).astype(BF16)
        fields = jnp.where(field == 0, rows[other], jnp.where(field == 4, left, known))
        part = dot(fields.astype(F32).astype(BF16), hits, 1, 1)
        info = part if info is None else info + part
    out_ref[ROWS:] = info.astype(BF16)
    pair_ref[ROWS:, :slots] = info.astype(BF16)
    pair_ref[ROWS:, slots:] = jnp.zeros((EXTRA, pair_ref.shape[1] - slots), BF16)
    for copy in copies[3:]:
        copy.wait()
    lam_low = lam_ref[...].astype(BF16).reshape(5 * elements, ELEM)
    values = slot_values(lam_low, hot, table_ref[...], elements).astype(BF16)
    out_ref[0:ROWS] = values[:, :slots]
    pair_ref[0:ROWS] = values


def state_kernel(saved_hbm, stiff_hbm, forward_hbm, backward_hbm, hot_ref, table_ref, out_ref, stiff_ref, forward_ref, backward_ref, saved_ref, sems):
    pairs = ((saved_hbm, saved_ref), (stiff_hbm.at[0 : stiff_ref.shape[0]], stiff_ref), (forward_hbm, forward_ref), (backward_hbm, backward_ref))
    copies = fetch(pairs, sems)
    copies[0].wait()
    elements = saved_ref.shape[2]
    for s in range(saved_ref.shape[0]):
        values = slot_values(saved_ref[s].reshape(5 * elements, ELEM), hot_ref[...], table_ref[...], elements)
        out_ref[s] = values.astype(BF16)
    for copy in copies[1:]:
        copy.wait()


def volume_kernel(section, slots, faces, saved_hbm, stiff_hbm, lam_ref, held_ref, jac_ref, own_ref, near_ref, state_ref, hot_ref, table_ref, base_ref, slope_ref, smooth_ref, saved_ref, stiff_ref, sems):
    held = held_ref.shape[0]
    copies = fetch(((stiff_hbm.at[held], stiff_ref), (saved_hbm.at[section], saved_ref)), sems)
    elements = lam_ref.shape[1]
    coef = step_size * section_weights[section]
    lam_low = lam_ref[...].astype(BF16).reshape(5 * elements, ELEM)

    width = own_ref.shape[1] - slots
    lane = lax.broadcasted_iota(jnp.int32, (FACE, width), 1)
    used = lane < 2 * faces
    lower = lane < faces
    sign = jnp.where(lower, -1.0, 1.0)
    w, u = [], []
    for v in range(5):
        rows = slice(v * FACE, (v + 1) * FACE)
        near = near_ref[rows, slots:].astype(F32)
        near = jnp.where(lower, pltpu.roll(near, width - faces, 1), pltpu.roll(near, faces, 1))
        w.append(jnp.where(used, sign * (near - own_ref[rows, slots:].astype(F32)), 0.0))
        u.append(jnp.where(used, state_ref[section, rows, slots:].astype(F32), REST[v]))
    g = flux_pull(u, w, None)
    grads = [0.5 * g[v] + (0.5 * penalty) * sign * w[v] for v in range(5)]
    total = viscosity * -1.0
    smooth = lift_slots(grads, hot_ref[:, slots:], table_ref[...], elements)
    for d in range(3):
        if d == held:
            copies[0].wait()
        stiff = held_ref[d] if d < held else stiff_ref[...]
        slopes = dot(lam_low, stiff)
        slope_ref[d] = slopes
        smooth = smooth + total * dot(slopes.astype(BF16), stiff, 1, 1)
    smooth_ref[...] = smooth
    copies[1].wait()
    jac = column_of(jac_ref[...]) * coef
    step = 16
    for r in range(0, elements, step):
        scale = jnp.broadcast_to(jac[r : r + step], (step, 128))
        for c in range(0, ELEM, 128):
            u = [saved_ref[v, r : r + step, c : c + 128].astype(F32) for v in range(5)]
            inv = 1.0 / u[0]
            vel = [u[i] * inv for i in (1, 2, 3)]
            kin = 0.5 * (vel[0] * vel[0] + vel[1] * vel[1] + vel[2] * vel[2])
            enth = gamma_gas * (u[4] * inv) - GM1 * kin
            trace = run = first = None
            g = [None, None, None, None]
            for d in range(3):
                w = [slope_ref[d, v * elements + r : v * elements + r + step, c : c + 128] for v in range(5)]
                q = w[1] * vel[0] + w[2] * vel[1] + w[3] * vel[2]
                term = vel[d] * q
                first = term if first is None else first + term
                trace = w[1 + d] if trace is None else trace + w[1 + d]
                part = vel[d] * w[4]
                run = part if run is None else run + part
                for i in range(3):
                    gi = w[1 + i] * vel[d]
                    if i == d:
                        gi = gi + (w[0] + q + enth * w[4])
                    g[1 + i] = gi if g[1 + i] is None else g[1 + i] + gi
            t = GM1 * (trace + run)
            pulled = [GM1 * kin * trace - first + (GM1 * kin - enth) * run]
            pulled += [g[1 + i] - vel[i] * t for i in range(3)]
            pulled.append(GM1 * trace + gamma_gas * run)
            for v in range(5):
                rows = slice(v * elements + r, v * elements + r + step)
                vol = pulled[v] + smooth_ref[rows, c : c + 128]
                base_ref[v, r : r + step, c : c + 128] = lam_ref[v, r : r + step, c : c + 128] + scale * vol


def spread_children(matrix, stacked):
    return dot(matrix, jnp.concatenate(stacked, axis=0))


def choose(raw, spread, child, keep=None):
    out = []
    for v, value in enumerate(raw):
        width = value.shape[1]
        picked = value
        for c in range(4):
            hit = child[c] if keep is None else child[c] & keep
            picked = jnp.where(hit, spread[c * FACE : (c + 1) * FACE, v * width : (v + 1) * width], picked)
        out.append(picked)
    return out


def read_table(pieces, me_ref, cap, relative):
    slots = pieces[0].shape[1]
    me = me_ref[0]
    lane = lax.broadcasted_iota(jnp.int32, (EXTRA, slots), 1)
    owner_of = lane // cap
    info = jnp.zeros((EXTRA, slots), F32)
    for p, piece in enumerate(pieces):
        owner = me ^ p if relative else p
        shift = lax.rem((owner - me) * cap + slots, slots)
        moved = pltpu.roll(piece[ROWS:].astype(F32), shift, 1)
        info = jnp.where(owner_of == owner, moved, info)
    info = info.astype(jnp.int32)
    source = info[0:1] // cap
    rank = info[0:1] - source * cap
    if relative:
        source = source ^ me
    code = source * slots + owner_of[0:1] * cap + rank
    field = lax.broadcasted_iota(jnp.int32, (EXTRA, slots), 0)
    return jnp.where(field == 0, code, info)


def route(pieces, me, cap):
    slots, devices = pieces[0].shape[1], len(pieces)
    half = slots // 2
    lane = lax.broadcasted_iota(jnp.int32, (devices, slots), 1)
    device = devices - 1 - lax.broadcasted_iota(jnp.int32, (devices, slots), 0)
    partner = jnp.zeros((devices, slots), F32)
    for p, piece in enumerate(pieces):
        owner = me ^ p
        fields = piece[ROWS:].astype(F32)
        mine = jnp.where(fields[3:4] == 1.0, fields[0:1], float(slots))
        turned = pltpu.roll(jnp.broadcast_to(mine, (devices, slots)), lax.rem((owner + 1) * cap, slots), 1)
        moved = pltpu.roll(turned, 0, 1, stride=cap, stride_axis=0)
        partner = jnp.where(lane // cap == owner, moved, partner)
    partner = partner.astype(jnp.int32)
    chip = partner // (2 * cap)
    wanted = [(partner < slots) & (chip == t) & (device // 2 != t) for t in range(devices // 2)]
    wanted = jnp.concatenate([jnp.where(x, 1.0, 0.0) for x in wanted], axis=0)
    before = lax.broadcasted_iota(jnp.int32, (slots, slots), 0) < lax.broadcasted_iota(jnp.int32, (slots, slots), 1)
    rank = dot(wanted.astype(BF16), jnp.where(before, 1.0, 0.0).astype(BF16))
    most = jnp.max(jnp.sum(wanted, axis=1, keepdims=True))
    index = lax.broadcasted_iota(jnp.int32, wanted.shape, 0)

    def row(x, t, q):
        return jnp.sum(jnp.where(index == t * devices + devices - 1 - q, x, 0.0), axis=0, keepdims=True)

    here = me // 2
    place = lax.broadcasted_iota(jnp.int32, (half, slots), 0).astype(F32)
    picks, rests = [], []
    for k in range(1, devices // 2):
        mine = jnp.where(row(wanted, here ^ k, me) > 0.0, row(rank, here ^ k, me), -1.0)
        picks.append(jnp.where(place == mine, 1.0, 0.0))
        rests.append(jnp.where(place + half == mine, 1.0, 0.0))
    picks.append(jnp.zeros_like(picks[0]))
    rests.append(jnp.zeros_like(picks[0]))
    coming = [row(rank, here, me ^ p) for p in range(devices)]
    return jnp.concatenate(picks, axis=0).astype(BF16), jnp.concatenate(rests, axis=0).astype(BF16), coming, most


def gather_lanes(blocks, codes, start=0):
    out = None
    for block in blocks:
        width = block.shape[1]
        place = lax.broadcasted_iota(jnp.int32, (width, codes.shape[1]), 0) + start
        part = dot(block, jnp.where(place == codes, 1.0, 0.0).astype(BF16))
        out = part if out is None else out + part
        start += width
    return out


def flag_kernel(excess_ref, flag_ref):
    flag_ref[0] = (jnp.max(excess_ref[...]) > 0.0).astype(jnp.int32)


def rest_kernel(sent_ref, rests_ref, *outs):
    for out, value in zip(outs, pack_halves(dot(sent_ref[...], rests_ref[...], 1, 1))):
        out[...] = value


def rest_gather_kernel(info_ref, *refs):
    blocks = [unpack_halves(refs[i][...], refs[i + 1][...]) for i in range(0, len(refs) - 1, 2)]
    refs[-1][...] = gather_lanes(blocks, info_ref[6:7]).astype(BF16)


def unpack_all(pieces):
    pieces = pieces + pieces[-1:] * (len(pieces) % 2)
    return [unpack_halves(pieces[p], pieces[p + 1]) for p in range(0, len(pieces), 2)]


def early_kernel(section, own_ref, near_ref, info_ref, state_ref, forward_ref, *refs):
    slots = own_ref.shape[1]
    part_ref, left_ref, here_ref = refs[-3:]
    info = info_ref[...]
    pieces = [r[...] for r in refs[:-3]]
    blocks = [jnp.concatenate([own_ref[...], near_ref[:, :slots]], axis=1)] + unpack_all(pieces)
    part_ref[...] = gather_lanes(blocks, info[5:6]).astype(BF16)
    child, left = (jnp.broadcast_to(info[k : k + 1], (FACE, slots)) for k in (1, 4))
    child = [child == c + 1 for c in range(4)]
    raw = [own_ref[v * FACE : (v + 1) * FACE] for v in range(5)]
    raw += [state_ref[section, v * FACE : (v + 1) * FACE, :slots] for v in range(5)]
    stacked = jnp.concatenate(raw, axis=1)
    spread = spread_children(forward_ref[...], [stacked, stacked])
    values = [x.astype(F32) for x in raw]
    for v, x in enumerate(choose(values[:5], spread, child)):
        left_ref[v * FACE : (v + 1) * FACE] = x
    for v, x in enumerate(choose(values[5:], spread[:, 5 * slots :], child, left == 1)):
        here_ref[v * FACE : (v + 1) * FACE] = x


def mortar_update(section, relative, first, last, count, *refs):
    compact = relative and not first
    slots = refs[count].shape[1]
    half = slots // 2
    pieces = [r[...] if len(r.shape) == 3 or r.shape[0] < ROWS else r[:, :slots] for r in refs[:count]]
    own_ref = refs[count]
    base_ref, state_ref, hot_ref, table_ref, jac_ref, forward_ref, backward_ref = refs[count + 1 : count + 8]
    me_ref, *outs = refs[count + 8 :] if first else (None,) + refs[count + 8 :]
    elements = base_ref.shape[1]
    if len(pieces) == 1 and pieces[0].ndim == 3:
        pieces = [pieces[0][p] for p in range(pieces[0].shape[0])]
    hot = hot_ref[...]
    if first:
        cap = slots // len(pieces)
        info = read_table(pieces, me_ref, cap, relative)
    else:
        info = outs[0][...]
        outs = outs[1:]
    if first and relative:
        picks, rests, coming, most = route(pieces, me_ref[0], cap)
        extended = []
        for piece, ranks in zip(pieces, coming):
            extra = jnp.broadcast_to(ranks, (EXTRA, slots)).astype(BF16)
            extended.append(jnp.concatenate([piece[:ROWS], extra], axis=0))
        blocks = [jnp.concatenate(extended[p : p + 2], axis=1) for p in range(0, len(pieces), 2)]
        partner = gather_lanes(blocks, info[0:1])
        rank = partner[ROWS : ROWS + 1].astype(jnp.int32)
        partner = partner[:ROWS]
        piece_of = info[0:1] // slots
        far = (piece_of >= 2) & (info[3:4] == 1)
        passed = piece_of % 2
        packed = 2 * slots + (passed * (len(pieces) // 2) + piece_of // 2 - 1) * half + rank
        near_code = jnp.where(far & (rank < half), packed, jnp.where(far, -1, info[0:1]))
        rest_code = jnp.where(far & (rank >= half), (piece_of - 3) * half + rank, -1)
        field = lax.broadcasted_iota(jnp.int32, info.shape, 0)
        info = jnp.where(field == 5, near_code, jnp.where(field == 6, rest_code, info))
        chosen = dot(hot[:, :slots], picks, 1, 1).astype(BF16)
        outs[1][...] = chosen
        outs[2][...] = rests
        outs[3][...] = jnp.full(outs[3].shape, most - half, F32)
    elif compact:
        start = 2 * slots + (len(pieces) + 1) * half
        partner = gather_lanes(unpack_all(pieces), info[5:6], start)
        more_ref, part_ref, left_ref, state_here_ref, *outs = outs
        partner = partner + part_ref[...].astype(F32) + more_ref[...].astype(F32)
        if not last:
            chosen = outs[0][...]
            outs = outs[1:]
    else:
        blocks = [jnp.concatenate([pieces[p][:ROWS], pieces[p + 1][:ROWS]], axis=1) for p in range(0, len(pieces), 2)]
        partner = gather_lanes(blocks, info[0:1])
    if first:
        outs[0][...] = info
        outs = outs[4:] if relative else outs[1:]
    step = FACE // 4
    child, axis, live, left = (jnp.broadcast_to(info[k : k + 1], (step, slots)) for k in range(1, 5))
    is_left = left == 1
    alive = live == 1
    child = [child == c + 1 for c in range(4)]
    picks = [axis == n for n in range(3)]
    side = jnp.where(is_left, 0.5 * penalty, -0.5 * penalty)
    partner = partner.astype(BF16)
    if compact:
        projecting = [partner[v * FACE : (v + 1) * FACE] for v in range(5)]
    else:
        whole = jnp.broadcast_to(info[4:5], (FACE, slots)) == 1
        mixed = [jnp.where(whole, own_ref[v * FACE : (v + 1) * FACE].astype(F32), partner[v * FACE : (v + 1) * FACE].astype(F32)).astype(BF16) for v in range(5)]
        projecting = mixed + [state_ref[section, v * FACE : (v + 1) * FACE, :slots] for v in range(5)]
    stacked = jnp.concatenate(projecting, axis=1)
    spread = spread_children(forward_ref[...], [stacked, stacked])

    def project(raw, v, r, keep=None):
        picked = raw
        for c in range(4):
            hit = child[c] if keep is None else child[c] & keep
            picked = jnp.where(hit, spread[c * FACE + r : c * FACE + r + step, v * slots : (v + 1) * slots], picked)
        return picked

    chunks = [[] for _ in range(5)]
    for r in range(0, FACE, step):
        w, u = [], []
        for v in range(5):
            rows = slice(v * FACE + r, v * FACE + r + step)
            mine, other = own_ref[rows].astype(F32), partner[rows].astype(F32)
            right = jnp.where(is_left, other, mine)
            if compact:
                near_left = jnp.where(is_left, left_ref[rows], project(other, v, r))
                here = state_here_ref[rows]
            else:
                near_left = project(jnp.where(is_left, mine, other), v, r)
                here = project(state_ref[section, rows, :slots].astype(F32), 5 + v, r, is_left)
            w.append(jnp.where(alive, right - near_left, 0.0))
            u.append(jnp.where(alive, here, REST[v]))
        g = flux_pull(u, w, picks)
        for v in range(5):
            chunks[v].append(0.5 * g[v] + side * w[v])
    pull = [jnp.concatenate(parts, axis=0) for parts in chunks]
    child, left = (jnp.broadcast_to(info[k : k + 1], (FACE, slots)) for k in (1, 4))
    is_left = left == 1
    child = [child == c + 1 for c in range(4)]
    stacked = jnp.concatenate(pull, axis=1)
    high = stacked.astype(BF16)
    spread = spread_children(backward_ref[...], [high, high])
    grads = choose(pull, spread, child, is_left)

    table = table_ref[...]
    lifted = lift_slots(grads, hot[:, :slots], table, elements)
    jac = column_of(jac_ref[...]) * (step_size * section_weights[section])
    lam = [base_ref[v] + jac * lifted[v * elements : (v + 1) * elements] for v in range(5)]
    for v in range(5):
        outs[0][v] = lam[v]
    if not last:
        lam_low = jnp.concatenate([x.astype(BF16) for x in lam], axis=0)
        if relative:
            hot = jnp.concatenate([hot, chosen], axis=1)
        values = slot_values(lam_low, hot, table, elements)
        both = outs[2].shape[1]
        outs[1][...] = values[:, :slots].astype(BF16)
        outs[2][...] = values[:, :both].astype(BF16)
        if relative:
            for out, value in zip(outs[3:], pack_halves(values[:, both:])):
                out[...] = value


def call(kernel, outs, args, scratch=(), scalars=(), far=(), plain=False, final=False):
    def space(i):
        return pltpu.HBM if i in far else pltpu.SMEM if i in scalars else pltpu.VMEM

    if not plain:
        args = [a if i in scalars else pltpu.with_memory_space_constraint(a, space(i)) for i, a in enumerate(args)]
    small = [o == (1,) for o, _ in outs]
    shapes = [jax.ShapeDtypeStruct(o, t) if plain or final or tiny else pltpu.VMEM(o, t) for (o, t), tiny in zip(outs, small)]
    return pl.pallas_call(
        kernel,
        out_shape=shapes,
        in_specs=[pl.BlockSpec(memory_space=space(i)) for i in range(len(args))],
        out_specs=[pl.BlockSpec(memory_space=pltpu.SMEM if tiny else pltpu.VMEM) for tiny in small],
        scratch_shapes=list(scratch),
        compiler_params=pltpu.CompilerParams(vmem_limit_bytes=VMEM_GRANT),
    )(*args)


def power_of_two(n):
    return n & (n - 1) == 0


def paired():
    ny, nz = lax.axis_size("gy"), lax.axis_size("gz")
    return nz == 2 and power_of_two(ny) and ny <= 8


def swap_pair(x):
    return lax.ppermute(x, "gz", [(0, 1), (1, 0)])


def send_along(x, k):
    ny = lax.axis_size("gy")
    return lax.ppermute(x, "gy", [(i, i ^ k) for i in range(ny)])


def send_rest(sent, rests, info):
    count = lax.axis_size("gy")
    parts = call(rest_kernel, [((ROWS // 2, sent.shape[1]), BF16)] * (count - 1), [sent, rests], plain=True)
    pieces = []
    for k in range(1, count):
        here = send_along(parts[k - 1], k)
        pieces += [here, swap_pair(here)]
    return call(rest_gather_kernel, [(sent.shape, BF16)], [info] + pieces, plain=True)[0]


def clear_kernel(out_ref):
    out_ref[...] = jnp.zeros(out_ref.shape, out_ref.dtype)


def no_rest(sent, rests, info):
    return call(clear_kernel, [(sent.shape, sent.dtype)], [], plain=True)[0]


def neighbours(payload, slots, faces):
    peers = lax.axis_size("gz")
    up = [(i, (i + 1) % peers) for i in range(peers)]
    down = [(j, i) for i, j in up]
    below = lax.ppermute(payload, "gz", up)
    above = lax.ppermute(payload, "gz", down)
    lane = lax.broadcasted_iota(jnp.int32, payload.shape, 1)
    return jnp.where(lane < slots + faces, above, below)


def per_device(adjoint, saved, inv_jac, stiffness, send_face, mortar_table, conf_faces):
    elements = adjoint.shape[0]
    sections = saved.shape[0]
    slots = send_face.shape[1]
    faces = conf_faces.shape[2]
    shared = -(-2 * faces // 128) * 128
    table = jnp.asarray(restriction_table())
    forward, backward = (jnp.asarray(t) for t in projection_tables())
    jac = inv_jac.reshape(1, elements)
    lam = jnp.transpose(adjoint, (1, 0, 2))
    states = jnp.transpose(saved, (0, 2, 1, 3))
    me = lax.axis_index(("gy", "gz")).astype(jnp.int32).reshape(1)
    rows = ((5, elements, ELEM), F32)
    sent = ((ROWS, slots), BF16)
    pair = ((ROWS, slots + shared), BF16)
    info_shape = ((EXTRA, slots), jnp.int32)

    mortars = jnp.transpose(mortar_table, (1, 0, 2))
    held = lambda x: (x.shape, x.dtype)
    outgoing, both, hot, lam, table = call(
        start_kernel,
        [((ROWS + EXTRA, slots), BF16), ((ROWS + EXTRA, slots + shared), BF16), ((6 * elements, slots + shared), BF16), held(lam), held(table)],
        [lam, send_face, conf_faces, mortars, table, me],
        scratch=(
            pltpu.VMEM(send_face.shape, jnp.int32),
            pltpu.VMEM(conf_faces.shape, jnp.int32),
            pltpu.VMEM(mortars.shape, jnp.int32),
            pltpu.VMEM((8, slots + shared), jnp.int32),
            pltpu.SemaphoreType.DMA((5,)),
        ),
        far=range(5),
        scalars=(5,),
    )
    values, held_stiff, forward, backward = call(
        state_kernel,
        [((sections, ROWS, slots + shared), BF16), ((2,) + stiffness.shape[1:], BF16), held(forward), held(backward)],
        [states, stiffness, forward, backward, hot, table],
        scratch=(pltpu.VMEM(states.shape, BF16), pltpu.SemaphoreType.DMA((4,))),
        far=range(4),
    )
    count = lax.axis_size("gy")
    parts = [outgoing] * (count - 1)
    packed = ((ROWS // 2, slots), BF16)
    chosen_shape = ((6 * elements, count * slots // 2), BF16)
    rests_shape = ((count * slots // 2, slots), BF16)
    for section in (2, 1, 0):
        relative = paired()
        if relative:
            column = [None] * (count - 1)
            for k in reversed(range(len(column))):
                column[k] = send_along(parts[k], k + 1)
            near = swap_pair(both)
        else:
            near = neighbours(both, slots, faces)
        (base,) = call(
            functools.partial(volume_kernel, section, slots, faces),
            [rows],
            [states, stiffness, lam, held_stiff, jac, both, near, values, hot, table],
            scratch=(
                pltpu.VMEM((3, 5 * elements, ELEM), F32),
                pltpu.VMEM((5 * elements, ELEM), F32),
                pltpu.VMEM(states.shape[1:], BF16),
                pltpu.VMEM(stiffness.shape[1:], BF16),
                pltpu.SemaphoreType.DMA((2,)),
            ),
            far=(0, 1),
        )
        if relative:
            pieces = [outgoing, near]
            for here in column:
                pieces += [here, swap_pair(here)]
        else:
            pieces = [lax.all_gather(outgoing, ("gy", "gz"), axis=0, tiled=False)]
        first, last = section == sections - 1, section == 0
        outs = [rows]
        if not last:
            outs += [sent, pair] + ([packed] * (count - 1) if relative else [])
        if first:
            outs = [info_shape] + ([chosen_shape, rests_shape, ((8, 128), F32)] if relative else []) + outs
        compact = relative and not first
        if compact:
            wide = ((ROWS, slots), F32)
            early = call(
                functools.partial(early_kernel, section),
                [sent, wide, wide],
                [outgoing, near, info, values, forward] + column,
            )
            pieces = pieces[3::2]
        args = pieces + [outgoing, base, values, hot, table, jac, forward, backward]
        scalars = (len(args),) if first else ()
        args.append(me if first else info)
        if compact:
            args.append(lax.cond(flag[0] > 0, send_rest, no_rest, outgoing, rests, info))
            args += list(early) + ([] if last else [chosen])
        out = call(
            functools.partial(mortar_update, section, relative, first, last, len(pieces)),
            outs, args, scalars=scalars, final=last,
        )
        if first:
            info, out = out[0], out[1:]
            if relative:
                (chosen, rests, excess), out = out[:3], out[3:]
                (flag,) = call(flag_kernel, [((1,), jnp.int32)], [excess])
        lam = out[0]
        if not last:
            outgoing, both, parts = out[1], out[2], out[3:]
    return jnp.transpose(lam, (1, 0, 2))


def solution(mesh):
    return jax.shard_map(
        per_device,
        mesh=mesh,
        in_specs=(
            P(("gx", "gy", "gz"), None, None),
            P(None, ("gx", "gy", "gz"), None, None),
            P(("gx", "gy", "gz")),
            P(),
            P(("gx", "gy", "gz"), None),
            P(("gx", "gy", "gz"), None, None),
            P(("gx", "gy", "gz"), None, None),
        ),
        out_specs=P(("gx", "gy", "gz"), None, None),
        check_vma=False,
    )
```

```python
import functools

import jax
import jax.numpy as jnp
import numpy as np
from jax import lax
from jax.experimental import pallas as pl
from jax.experimental.pallas import tpu as pltpu
from jax.sharding import PartitionSpec as P


ORDER = 7
LINE = ORDER + 1
FACE = LINE * LINE
ELEM = FACE * LINE
PAIRS = 3
TILE = 2 * FACE
ROWS = 5 * FACE
EXTRA = 16

gamma_gas = 1.4
penalty = 1.5
viscosity = 0.5
step_size = 0.2
section_weights = (0.25, 0.25, 0.5)
GM1 = gamma_gas - 1.0
REST = (1.0, 0.0, 0.0, 0.0, 2.5)
F32 = jnp.float32
VMEM_GRANT = 24 << 20
BF16 = jnp.bfloat16


def lagrange_matrix(points, abscissa):
    out = np.ones((LINE, LINE))
    for target in range(LINE):
        for other in range(LINE):
            if other != target:
                out[:, target] *= (points - abscissa[other]) / (abscissa[target] - abscissa[other])
    return out


def split_low(matrix):
    high = matrix.astype(np.float32).astype(BF16)
    low = (matrix - high.astype(np.float64)).astype(np.float32).astype(BF16)
    return high, low


def projection_tables():
    abscissa = -np.cos(np.pi * np.arange(LINE) / ORDER)
    halves = [lagrange_matrix((abscissa + 2.0 * h - 1.0) * 0.5, abscissa) for h in range(2)]
    children = [np.kron(halves[c // 2], halves[c % 2]) for c in range(4)]
    fh, fl = split_low(np.concatenate(children, axis=0))
    bh, bl = split_low(np.concatenate([m.T for m in children], axis=0))
    return np.concatenate([fh, fl], axis=1), np.concatenate([bh, bl], axis=1)


def restriction_table():
    column = np.arange(6 * FACE)
    face, local = column // FACE, column % FACE
    first, second = local // LINE, local % LINE
    axis, fixed = face // 2, face % 2 * (LINE - 1)
    x = np.where(axis == 0, fixed, first)
    y = np.where(axis == 0, first, np.where(axis == 1, fixed, second))
    z = np.where(axis == 2, fixed, second)
    node = x * FACE + y * LINE + z
    return (np.arange(ELEM)[:, None] == node[None, :]).astype(np.float32).astype(BF16)


def dot(a, b, ca=1, cb=0):
    return lax.dot_general(a, b, (((ca,), (cb,)), ((), ())), preferred_element_type=F32)


def low_lanes(rows):
    return lax.broadcasted_iota(jnp.int32, (rows, TILE), 1) < FACE


def swap(x):
    return pltpu.roll(x, FACE, 1)


def exchange(a, b, low):
    return jnp.where(low, a, swap(b)), jnp.where(low, swap(a), b)


def flux_pull(u, w, picks):
    inv = 1.0 / u[0]
    vel = [u[i] * inv for i in (1, 2, 3)]
    kin = 0.5 * (vel[0] * vel[0] + vel[1] * vel[1] + vel[2] * vel[2])
    enth = gamma_gas * (u[4] * inv) - GM1 * kin
    q = w[1] * vel[0] + w[2] * vel[1] + w[3] * vel[2]
    if picks is None:
        vn, wn = vel[2], w[3]
    else:
        vn = jnp.where(picks[0], vel[0], jnp.where(picks[1], vel[1], vel[2]))
        wn = jnp.where(picks[0], w[1], jnp.where(picks[1], w[2], w[3]))
    r = vn * w[4]
    a = w[0] + q + enth * w[4]
    g = [GM1 * kin * wn - vn * q + (GM1 * kin - enth) * r]
    t = GM1 * (wn + r)
    for i in range(3):
        gi = w[1 + i] * vn - vel[i] * t
        if picks is None:
            gi = gi + a if i == 2 else gi
        else:
            gi = gi + jnp.where(picks[i], a, 0.0)
        g.append(gi)
    g.append(GM1 * wn + gamma_gas * r)
    return g


def trace_faces(field_low, table, elements):
    traced = dot(field_low, table)
    low = low_lanes(elements)
    zero = jnp.zeros((elements, TILE), F32)
    rows = [[None] * PAIRS for _ in range(6)]

    def piece(v, k):
        if v >= 5:
            return zero
        return traced[v * elements : (v + 1) * elements, k * TILE : (k + 1) * TILE]

    for j in range(PAIRS):
        for k in range(3):
            rows[2 * k][j], rows[2 * k + 1][j] = exchange(piece(2 * j, k), piece(2 * j + 1, k), low)
    return jnp.concatenate([jnp.concatenate(r, axis=1) for r in rows], axis=0).astype(BF16)


def lift_slots(grads, hot, table, elements):
    padded = jnp.concatenate([g.astype(BF16) for g in grads] + [jnp.zeros(grads[0].shape, BF16)], axis=0)
    face_grad = dot(hot, padded, 1, 1)
    low = low_lanes(elements)
    rows = [[None] * 3 for _ in range(6)]

    def piece(f, j):
        return face_grad[f * elements : (f + 1) * elements, j * TILE : (j + 1) * TILE]

    for j in range(PAIRS):
        for k in range(3):
            rows[2 * j][k], rows[2 * j + 1][k] = exchange(piece(2 * k, j), piece(2 * k + 1, j), low)
    arranged = jnp.concatenate([jnp.concatenate(r, axis=1) for r in rows[:5]], axis=0).astype(BF16)
    return dot(arranged, table, 1, 1)


def column_of(row):
    n = row.shape[1]
    same = lax.broadcasted_iota(jnp.int32, (n, n), 0) == lax.broadcasted_iota(jnp.int32, (n, n), 1)
    return jnp.sum(jnp.where(same, jnp.broadcast_to(row, (n, n)), 0.0), axis=1, keepdims=True)


def slot_values(field_low, hot, table, elements):
    return dot(trace_faces(field_low, table, elements), hot, 0, 0)[:ROWS]


def pack_halves(values):
    low = low_lanes(ROWS // 2)
    out = []
    for tile in range(values.shape[1] // TILE):
        part = values[:, tile * TILE : (tile + 1) * TILE]
        out += [x.astype(BF16) for x in exchange(part[: ROWS // 2], part[ROWS // 2 :], low)]
    return out


def unpack_halves(a, b):
    return jnp.concatenate(exchange(a.astype(F32), b.astype(F32), low_lanes(ROWS // 2)), axis=0).astype(BF16)


def fetch(pairs, sems):
    copies = [pltpu.make_async_copy(a, b, sems.at[i]) for i, (a, b) in enumerate(pairs)]
    for copy in copies:
        copy.start()
    return copies


def start_kernel(lam_hbm, send_hbm, conf_hbm, map_hbm, table_hbm, me_ref, out_ref, pair_ref, hot_ref, lam_ref, table_ref, send_ref, conf_ref, map_ref, ids_ref, sems):
    pairs = ((lam_hbm, lam_ref), (table_hbm, table_ref), (send_hbm, send_ref), (conf_hbm, conf_ref), (map_hbm, map_ref))
    copies = fetch(pairs, sems)
    elements = lam_ref.shape[1]
    slots = send_ref.shape[1]
    faces = conf_ref.shape[2]
    ids_ref[...] = jnp.full(ids_ref.shape, -1, jnp.int32)
    for copy in copies[2:]:
        copy.wait()
    ids_ref[0:1, 0:slots] = send_ref[...]
    ids_ref[0:1, slots : slots + faces] = conf_ref[0, 0:1]
    ids_ref[0:1, slots + faces : slots + 2 * faces] = conf_ref[0, 1:2]
    shape = hot_ref.shape
    row = lax.broadcasted_iota(jnp.int32, shape, 0)
    face = row // elements
    ident = 6 * (row - face * elements) + face
    hot = jnp.where(ident == ids_ref[0:1], 1.0, 0.0).astype(BF16)
    hot_ref[...] = hot
    rows = [map_ref[k] for k in range(5)]
    mortars = rows[0].shape[1]
    slot = lax.broadcasted_iota(jnp.int32, (slots, mortars), 0)
    field = lax.broadcasted_iota(jnp.int32, (EXTRA, mortars), 0)
    known = jnp.where(field == 1, rows[2], jnp.where(field == 2, rows[3], jnp.where(field == 3, rows[4], 0)))
    info = None
    for mine, other, left in ((0, 1, 1), (1, 0, 0)):
        hits = jnp.where(slot == rows[mine], 1.0, 0.0).astype(BF16)
        fields = jnp.where(field == 0, rows[other], jnp.where(field == 4, left, known))
        part = dot(fields.astype(F32).astype(BF16), hits, 1, 1)
        info = part if info is None else info + part
    out_ref[ROWS:] = info.astype(BF16)
    pair_ref[ROWS:, :slots] = info.astype(BF16)
    pair_ref[ROWS:, slots:] = jnp.zeros((EXTRA, pair_ref.shape[1] - slots), BF16)
    for copy in copies[:2]:
        copy.wait()
    lam_low = lam_ref[...].astype(BF16).reshape(5 * elements, ELEM)
    values = slot_values(lam_low, hot, table_ref[...], elements).astype(BF16)
    out_ref[0:ROWS] = values[:, :slots]
    pair_ref[0:ROWS] = values


def state_kernel(saved_hbm, stiff_hbm, forward_hbm, backward_hbm, hot_ref, table_ref, out_ref, stiff_ref, forward_ref, backward_ref, saved_ref, sems):
    pairs = ((saved_hbm, saved_ref), (stiff_hbm.at[0 : stiff_ref.shape[0]], stiff_ref), (forward_hbm, forward_ref), (backward_hbm, backward_ref))
    copies = fetch(pairs, sems)
    copies[0].wait()
    elements = saved_ref.shape[2]
    for s in range(saved_ref.shape[0]):
        values = slot_values(saved_ref[s].reshape(5 * elements, ELEM), hot_ref[...], table_ref[...], elements)
        out_ref[s] = values.astype(BF16)
    for copy in copies[1:]:
        copy.wait()


def volume_kernel(section, slots, faces, saved_hbm, stiff_hbm, lam_ref, held_ref, jac_ref, own_ref, near_ref, state_ref, hot_ref, table_ref, base_ref, slope_ref, smooth_ref, saved_ref, stiff_ref, sems):
    held = held_ref.shape[0]
    copies = fetch(((stiff_hbm.at[held], stiff_ref), (saved_hbm.at[section], saved_ref)), sems)
    elements = lam_ref.shape[1]
    coef = step_size * section_weights[section]
    lam_low = lam_ref[...].astype(BF16).reshape(5 * elements, ELEM)

    width = own_ref.shape[1] - slots
    lane = lax.broadcasted_iota(jnp.int32, (FACE, width), 1)
    used = lane < 2 * faces
    lower = lane < faces
    sign = jnp.where(lower, -1.0, 1.0)
    w, u = [], []
    for v in range(5):
        rows = slice(v * FACE, (v + 1) * FACE)
        near = near_ref[rows, slots:].astype(F32)
        near = jnp.where(lower, pltpu.roll(near, width - faces, 1), pltpu.roll(near, faces, 1))
        w.append(jnp.where(used, sign * (near - own_ref[rows, slots:].astype(F32)), 0.0))
        u.append(jnp.where(used, state_ref[section, rows, slots:].astype(F32), REST[v]))
    g = flux_pull(u, w, None)
    grads = [0.5 * g[v] + (0.5 * penalty) * sign * w[v] for v in range(5)]
    total = viscosity * -1.0
    smooth = lift_slots(grads, hot_ref[:, slots:], table_ref[...], elements)
    for d in range(3):
        if d == held:
            copies[0].wait()
        stiff = held_ref[d] if d < held else stiff_ref[...]
        slopes = dot(lam_low, stiff)
        slope_ref[d] = slopes
        smooth = smooth + total * dot(slopes.astype(BF16), stiff, 1, 1)
    smooth_ref[...] = smooth
    copies[1].wait()
    jac = column_of(jac_ref[...]) * coef
    step = 16
    for r in range(0, elements, step):
        scale = jnp.broadcast_to(jac[r : r + step], (step, 128))
        for c in range(0, ELEM, 128):
            u = [saved_ref[v, r : r + step, c : c + 128].astype(F32) for v in range(5)]
            inv = 1.0 / u[0]
            vel = [u[i] * inv for i in (1, 2, 3)]
            kin = 0.5 * (vel[0] * vel[0] + vel[1] * vel[1] + vel[2] * vel[2])
            enth = gamma_gas * (u[4] * inv) - GM1 * kin
            trace = run = first = None
            g = [None, None, None, None]
            for d in range(3):
                w = [slope_ref[d, v * elements + r : v * elements + r + step, c : c + 128] for v in range(5)]
                q = w[1] * vel[0] + w[2] * vel[1] + w[3] * vel[2]
                term = vel[d] * q
                first = term if first is None else first + term
                trace = w[1 + d] if trace is None else trace + w[1 + d]
                part = vel[d] * w[4]
                run = part if run is None else run + part
                for i in range(3):
                    gi = w[1 + i] * vel[d]
                    if i == d:
                        gi = gi + (w[0] + q + enth * w[4])
                    g[1 + i] = gi if g[1 + i] is None else g[1 + i] + gi
            t = GM1 * (trace + run)
            pulled = [GM1 * kin * trace - first + (GM1 * kin - enth) * run]
            pulled += [g[1 + i] - vel[i] * t for i in range(3)]
            pulled.append(GM1 * trace + gamma_gas * run)
            for v in range(5):
                rows = slice(v * elements + r, v * elements + r + step)
                vol = pulled[v] + smooth_ref[rows, c : c + 128]
                base_ref[v, r : r + step, c : c + 128] = lam_ref[v, r : r + step, c : c + 128] + scale * vol


def spread_children(matrix, stacked):
    return dot(matrix, jnp.concatenate(stacked, axis=0))


def choose(raw, spread, child, keep=None):
    out = []
    for v, value in enumerate(raw):
        width = value.shape[1]
        picked = value
        for c in range(4):
            hit = child[c] if keep is None else child[c] & keep
            picked = jnp.where(hit, spread[c * FACE : (c + 1) * FACE, v * width : (v + 1) * width], picked)
        out.append(picked)
    return out


def read_table(pieces, me_ref, cap, relative):
    slots = pieces[0].shape[1]
    me = me_ref[0]
    lane = lax.broadcasted_iota(jnp.int32, (EXTRA, slots), 1)
    owner_of = lane // cap
    info = jnp.zeros((EXTRA, slots), F32)
    for p, piece in enumerate(pieces):
        owner = me ^ p if relative else p
        shift = lax.rem((owner - me) * cap + slots, slots)
        moved = pltpu.roll(piece[ROWS:].astype(F32), shift, 1)
        info = jnp.where(owner_of == owner, moved, info)
    info = info.astype(jnp.int32)
    source = info[0:1] // cap
    rank = info[0:1] - source * cap
    if relative:
        source = source ^ me
    code = source * slots + owner_of[0:1] * cap + rank
    field = lax.broadcasted_iota(jnp.int32, (EXTRA, slots), 0)
    return jnp.where(field == 0, code, info)


def route(pieces, me, cap):
    slots, devices = pieces[0].shape[1], len(pieces)
    half = slots // 2
    lane = lax.broadcasted_iota(jnp.int32, (devices, slots), 1)
    device = devices - 1 - lax.broadcasted_iota(jnp.int32, (devices, slots), 0)
    partner = jnp.zeros((devices, slots), F32)
    for p, piece in enumerate(pieces):
        owner = me ^ p
        fields = piece[ROWS:].astype(F32)
        mine = jnp.where(fields[3:4] == 1.0, fields[0:1], float(slots))
        turned = pltpu.roll(jnp.broadcast_to(mine, (devices, slots)), lax.rem((owner + 1) * cap, slots), 1)
        moved = pltpu.roll(turned, 0, 1, stride=cap, stride_axis=0)
        partner = jnp.where(lane // cap == owner, moved, partner)
    partner = partner.astype(jnp.int32)
    chip = partner // (2 * cap)
    wanted = [(partner < slots) & (chip == t) & (device // 2 != t) for t in range(devices // 2)]
    wanted = jnp.concatenate([jnp.where(x, 1.0, 0.0) for x in wanted], axis=0)
    before = lax.broadcasted_iota(jnp.int32, (slots, slots), 0) < lax.broadcasted_iota(jnp.int32, (slots, slots), 1)
    rank = dot(wanted.astype(BF16), jnp.where(before, 1.0, 0.0).astype(BF16))
    most = jnp.max(jnp.sum(wanted, axis=1, keepdims=True))
    index = lax.broadcasted_iota(jnp.int32, wanted.shape, 0)

    def row(x, t, q):
        return jnp.sum(jnp.where(index == t * devices + devices - 1 - q, x, 0.0), axis=0, keepdims=True)

    here = me // 2
    place = lax.broadcasted_iota(jnp.int32, (half, slots), 0).astype(F32)
    picks, rests = [], []
    for k in range(1, devices // 2):
        mine = jnp.where(row(wanted, here ^ k, me) > 0.0, row(rank, here ^ k, me), -1.0)
        picks.append(jnp.where(place == mine, 1.0, 0.0))
        rests.append(jnp.where(place + half == mine, 1.0, 0.0))
    picks.append(jnp.zeros_like(picks[0]))
    rests.append(jnp.zeros_like(picks[0]))
    coming = [row(rank, here, me ^ p) for p in range(devices)]
    return jnp.concatenate(picks, axis=0).astype(BF16), jnp.concatenate(rests, axis=0).astype(BF16), coming, most


def gather_lanes(blocks, codes, start=0):
    out = None
    for block in blocks:
        width = block.shape[1]
        place = lax.broadcasted_iota(jnp.int32, (width, codes.shape[1]), 0) + start
        part = dot(block, jnp.where(place == codes, 1.0, 0.0).astype(BF16))
        out = part if out is None else out + part
        start += width
    return out


def flag_kernel(excess_ref, flag_ref):
    flag_ref[0] = (jnp.max(excess_ref[...]) > 0.0).astype(jnp.int32)


def rest_kernel(sent_ref, rests_ref, *outs):
    for out, value in zip(outs, pack_halves(dot(sent_ref[...], rests_ref[...], 1, 1))):
        out[...] = value


def rest_gather_kernel(info_ref, *refs):
    blocks = [unpack_halves(refs[i][...], refs[i + 1][...]) for i in range(0, len(refs) - 1, 2)]
    refs[-1][...] = gather_lanes(blocks, info_ref[6:7]).astype(BF16)


def unpack_all(pieces):
    pieces = pieces + pieces[-1:] * (len(pieces) % 2)
    return [unpack_halves(pieces[p], pieces[p + 1]) for p in range(0, len(pieces), 2)]


def early_kernel(section, own_ref, near_ref, info_ref, state_ref, forward_ref, *refs):
    slots = own_ref.shape[1]
    part_ref, left_ref, here_ref = refs[-3:]
    info = info_ref[...]
    pieces = [r[...] for r in refs[:-3]]
    blocks = [jnp.concatenate([own_ref[...], near_ref[:, :slots]], axis=1)] + unpack_all(pieces)
    part_ref[...] = gather_lanes(blocks, info[5:6]).astype(BF16)
    child, left = (jnp.broadcast_to(info[k : k + 1], (FACE, slots)) for k in (1, 4))
    child = [child == c + 1 for c in range(4)]
    raw = [own_ref[v * FACE : (v + 1) * FACE] for v in range(5)]
    raw += [state_ref[section, v * FACE : (v + 1) * FACE, :slots] for v in range(5)]
    stacked = jnp.concatenate(raw, axis=1)
    spread = spread_children(forward_ref[...], [stacked, stacked])
    values = [x.astype(F32) for x in raw]
    for v, x in enumerate(choose(values[:5], spread, child)):
        left_ref[v * FACE : (v + 1) * FACE] = x
    for v, x in enumerate(choose(values[5:], spread[:, 5 * slots :], child, left == 1)):
        here_ref[v * FACE : (v + 1) * FACE] = x


def mortar_update(section, relative, first, last, count, *refs):
    compact = relative and not first
    slots = refs[count].shape[1]
    half = slots // 2
    pieces = [r[...] if len(r.shape) == 3 or r.shape[0] < ROWS else r[:, :slots] for r in refs[:count]]
    own_ref = refs[count]
    base_ref, state_ref, hot_ref, table_ref, jac_ref, forward_ref, backward_ref = refs[count + 1 : count + 8]
    me_ref, *outs = refs[count + 8 :] if first else (None,) + refs[count + 8 :]
    elements = base_ref.shape[1]
    if len(pieces) == 1 and pieces[0].ndim == 3:
        pieces = [pieces[0][p] for p in range(pieces[0].shape[0])]
    hot = hot_ref[...]
    if first:
        cap = slots // len(pieces)
        info = read_table(pieces, me_ref, cap, relative)
    else:
        info = outs[0][...]
        outs = outs[1:]
    if first and relative:
        picks, rests, coming, most = route(pieces, me_ref[0], cap)
        extended = []
        for piece, ranks in zip(pieces, coming):
            extra = jnp.broadcast_to(ranks, (EXTRA, slots)).astype(BF16)
            extended.append(jnp.concatenate([piece[:ROWS], extra], axis=0))
        blocks = [jnp.concatenate(extended[p : p + 2], axis=1) for p in range(0, len(pieces), 2)]
        partner = gather_lanes(blocks, info[0:1])
        rank = partner[ROWS : ROWS + 1].astype(jnp.int32)
        partner = partner[:ROWS]
        piece_of = info[0:1] // slots
        far = (piece_of >= 2) & (info[3:4] == 1)
        passed = piece_of % 2
        packed = 2 * slots + (passed * (len(pieces) // 2) + piece_of // 2 - 1) * half + rank
        near_code = jnp.where(far & (rank < half), packed, jnp.where(far, -1, info[0:1]))
        rest_code = jnp.where(far & (rank >= half), (piece_of - 3) * half + rank, -1)
        field = lax.broadcasted_iota(jnp.int32, info.shape, 0)
        info = jnp.where(field == 5, near_code, jnp.where(field == 6, rest_code, info))
        chosen = dot(hot[:, :slots], picks, 1, 1).astype(BF16)
        outs[1][...] = chosen
        outs[2][...] = rests
        outs[3][...] = jnp.full(outs[3].shape, most - half, F32)
    elif compact:
        start = 2 * slots + (len(pieces) + 1) * half
        partner = gather_lanes(unpack_all(pieces), info[5:6], start)
        more_ref, part_ref, left_ref, state_here_ref, *outs = outs
        partner = partner + part_ref[...].astype(F32) + more_ref[...].astype(F32)
        if not last:
            chosen = outs[0][...]
            outs = outs[1:]
    else:
        blocks = [jnp.concatenate([pieces[p][:ROWS], pieces[p + 1][:ROWS]], axis=1) for p in range(0, len(pieces), 2)]
        partner = gather_lanes(blocks, info[0:1])
    if first:
        outs[0][...] = info
        outs = outs[4:] if relative else outs[1:]
    step = FACE // 4
    child, axis, live, left = (jnp.broadcast_to(info[k : k + 1], (step, slots)) for k in range(1, 5))
    is_left = left == 1
    alive = live == 1
    child = [child == c + 1 for c in range(4)]
    picks = [axis == n for n in range(3)]
    side = jnp.where(is_left, 0.5 * penalty, -0.5 * penalty)
    partner = partner.astype(BF16)
    if compact:
        projecting = [partner[v * FACE : (v + 1) * FACE] for v in range(5)]
    else:
        whole = jnp.broadcast_to(info[4:5], (FACE, slots)) == 1
        mixed = [jnp.where(whole, own_ref[v * FACE : (v + 1) * FACE].astype(F32), partner[v * FACE : (v + 1) * FACE].astype(F32)).astype(BF16) for v in range(5)]
        projecting = mixed + [state_ref[section, v * FACE : (v + 1) * FACE, :slots] for v in range(5)]
    stacked = jnp.concatenate(projecting, axis=1)
    spread = spread_children(forward_ref[...], [stacked, stacked])

    def project(raw, v, r, keep=None):
        picked = raw
        for c in range(4):
            hit = child[c] if keep is None else child[c] & keep
            picked = jnp.where(hit, spread[c * FACE + r : c * FACE + r + step, v * slots : (v + 1) * slots], picked)
        return picked

    chunks = [[] for _ in range(5)]
    for r in range(0, FACE, step):
        w, u = [], []
        for v in range(5):
            rows = slice(v * FACE + r, v * FACE + r + step)
            mine, other = own_ref[rows].astype(F32), partner[rows].astype(F32)
            right = jnp.where(is_left, other, mine)
            if compact:
                near_left = jnp.where(is_left, left_ref[rows], project(other, v, r))
                here = state_here_ref[rows]
            else:
                near_left = project(jnp.where(is_left, mine, other), v, r)
                here = project(state_ref[section, rows, :slots].astype(F32), 5 + v, r, is_left)
            w.append(jnp.where(alive, right - near_left, 0.0))
            u.append(jnp.where(alive, here, REST[v]))
        g = flux_pull(u, w, picks)
        for v in range(5):
            chunks[v].append(0.5 * g[v] + side * w[v])
    pull = [jnp.concatenate(parts, axis=0) for parts in chunks]
    child, left = (jnp.broadcast_to(info[k : k + 1], (FACE, slots)) for k in (1, 4))
    is_left = left == 1
    child = [child == c + 1 for c in range(4)]
    stacked = jnp.concatenate(pull, axis=1)
    high = stacked.astype(BF16)
    spread = spread_children(backward_ref[...], [high, high])
    grads = choose(pull, spread, child, is_left)

    table = table_ref[...]
    lifted = lift_slots(grads, hot[:, :slots], table, elements)
    jac = column_of(jac_ref[...]) * (step_size * section_weights[section])
    lam = [base_ref[v] + jac * lifted[v * elements : (v + 1) * elements] for v in range(5)]
    for v in range(5):
        outs[0][v] = lam[v]
    if not last:
        lam_low = jnp.concatenate([x.astype(BF16) for x in lam], axis=0)
        if relative:
            hot = jnp.concatenate([hot, chosen], axis=1)
        values = slot_values(lam_low, hot, table, elements)
        both = outs[2].shape[1]
        outs[1][...] = values[:, :slots].astype(BF16)
        outs[2][...] = values[:, :both].astype(BF16)
        if relative:
            for out, value in zip(outs[3:], pack_halves(values[:, both:])):
                out[...] = value


def call(kernel, outs, args, scratch=(), scalars=(), far=(), plain=False, final=False):
    def space(i):
        return pltpu.HBM if i in far else pltpu.SMEM if i in scalars else pltpu.VMEM

    if not plain:
        args = [a if i in scalars else pltpu.with_memory_space_constraint(a, space(i)) for i, a in enumerate(args)]
    small = [o == (1,) for o, _ in outs]
    shapes = [jax.ShapeDtypeStruct(o, t) if plain or final or tiny else pltpu.VMEM(o, t) for (o, t), tiny in zip(outs, small)]
    return pl.pallas_call(
        kernel,
        out_shape=shapes,
        in_specs=[pl.BlockSpec(memory_space=space(i)) for i in range(len(args))],
        out_specs=[pl.BlockSpec(memory_space=pltpu.SMEM if tiny else pltpu.VMEM) for tiny in small],
        scratch_shapes=list(scratch),
        compiler_params=pltpu.CompilerParams(vmem_limit_bytes=VMEM_GRANT),
    )(*args)


def power_of_two(n):
    return n & (n - 1) == 0


def paired():
    ny, nz = lax.axis_size("gy"), lax.axis_size("gz")
    return nz == 2 and power_of_two(ny) and ny <= 8


def swap_pair(x):
    return lax.ppermute(x, "gz", [(0, 1), (1, 0)])


def send_along(x, k):
    ny = lax.axis_size("gy")
    return lax.ppermute(x, "gy", [(i, i ^ k) for i in range(ny)])


def send_rest(sent, rests, info):
    count = lax.axis_size("gy")
    parts = call(rest_kernel, [((ROWS // 2, sent.shape[1]), BF16)] * (count - 1), [sent, rests], plain=True)
    pieces = []
    for k in range(1, count):
        here = send_along(parts[k - 1], k)
        pieces += [here, swap_pair(here)]
    return call(rest_gather_kernel, [(sent.shape, BF16)], [info] + pieces, plain=True)[0]


def clear_kernel(out_ref):
    out_ref[...] = jnp.zeros(out_ref.shape, out_ref.dtype)


def no_rest(sent, rests, info):
    return call(clear_kernel, [(sent.shape, sent.dtype)], [], plain=True)[0]


def neighbours(payload, slots, faces):
    peers = lax.axis_size("gz")
    up = [(i, (i + 1) % peers) for i in range(peers)]
    down = [(j, i) for i, j in up]
    below = lax.ppermute(payload, "gz", up)
    above = lax.ppermute(payload, "gz", down)
    lane = lax.broadcasted_iota(jnp.int32, payload.shape, 1)
    return jnp.where(lane < slots + faces, above, below)


def per_device(adjoint, saved, inv_jac, stiffness, send_face, mortar_table, conf_faces):
    elements = adjoint.shape[0]
    sections = saved.shape[0]
    slots = send_face.shape[1]
    faces = conf_faces.shape[2]
    shared = -(-2 * faces // 128) * 128
    table = jnp.asarray(restriction_table())
    forward, backward = (jnp.asarray(t) for t in projection_tables())
    jac = inv_jac.reshape(1, elements)
    lam = jnp.transpose(adjoint, (1, 0, 2))
    states = jnp.transpose(saved, (0, 2, 1, 3))
    me = lax.axis_index(("gy", "gz")).astype(jnp.int32).reshape(1)
    rows = ((5, elements, ELEM), F32)
    sent = ((ROWS, slots), BF16)
    pair = ((ROWS, slots + shared), BF16)
    info_shape = ((EXTRA, slots), jnp.int32)

    mortars = jnp.transpose(mortar_table, (1, 0, 2))
    held = lambda x: (x.shape, x.dtype)
    outgoing, both, hot, lam, table = call(
        start_kernel,
        [((ROWS + EXTRA, slots), BF16), ((ROWS + EXTRA, slots + shared), BF16), ((6 * elements, slots + shared), BF16), held(lam), held(table)],
        [lam, send_face, conf_faces, mortars, table, me],
        scratch=(
            pltpu.VMEM(send_face.shape, jnp.int32),
            pltpu.VMEM(conf_faces.shape, jnp.int32),
            pltpu.VMEM(mortars.shape, jnp.int32),
            pltpu.VMEM((8, slots + shared), jnp.int32),
            pltpu.SemaphoreType.DMA((5,)),
        ),
        far=range(5),
        scalars=(5,),
    )
    values, held_stiff, forward, backward = call(
        state_kernel,
        [((sections, ROWS, slots + shared), BF16), ((2,) + stiffness.shape[1:], BF16), held(forward), held(backward)],
        [states, stiffness, forward, backward, hot, table],
        scratch=(pltpu.VMEM(states.shape, BF16), pltpu.SemaphoreType.DMA((4,))),
        far=range(4),
    )
    count = lax.axis_size("gy")
    parts = [outgoing] * (count - 1)
    packed = ((ROWS // 2, slots), BF16)
    chosen_shape = ((6 * elements, count * slots // 2), BF16)
    rests_shape = ((count * slots // 2, slots), BF16)
    for section in (2, 1, 0):
        relative = paired()
        if relative:
            column = [None] * (count - 1)
            for k in reversed(range(len(column))):
                column[k] = send_along(parts[k], k + 1)
            near = swap_pair(both)
        else:
            near = neighbours(both, slots, faces)
        (base,) = call(
            functools.partial(volume_kernel, section, slots, faces),
            [rows],
            [states, stiffness, lam, held_stiff, jac, both, near, values, hot, table],
            scratch=(
                pltpu.VMEM((3, 5 * elements, ELEM), F32),
                pltpu.VMEM((5 * elements, ELEM), F32),
                pltpu.VMEM(states.shape[1:], BF16),
                pltpu.VMEM(stiffness.shape[1:], BF16),
                pltpu.SemaphoreType.DMA((2,)),
            ),
            far=(0, 1),
        )
        if relative:
            pieces = [outgoing, near]
            for here in column:
                pieces += [here, swap_pair(here)]
        else:
            pieces = [lax.all_gather(outgoing, ("gy", "gz"), axis=0, tiled=False)]
        first, last = section == sections - 1, section == 0
        outs = [rows]
        if not last:
            outs += [sent, pair] + ([packed] * (count - 1) if relative else [])
        if first:
            outs = [info_shape] + ([chosen_shape, rests_shape, ((8, 128), F32)] if relative else []) + outs
        compact = relative and not first
        if compact:
            wide = ((ROWS, slots), F32)
            early = call(
                functools.partial(early_kernel, section),
                [sent, wide, wide],
                [outgoing, near, info, values, forward] + column,
            )
            pieces = pieces[3::2]
        args = pieces + [outgoing, base, values, hot, table, jac, forward, backward]
        scalars = (len(args),) if first else ()
        args.append(me if first else info)
        if compact:
            args.append(lax.cond(flag[0] > 0, send_rest, no_rest, outgoing, rests, info))
            args += list(early) + ([] if last else [chosen])
        out = call(
            functools.partial(mortar_update, section, relative, first, last, len(pieces)),
            outs, args, scalars=scalars, final=last,
        )
        if first:
            info, out = out[0], out[1:]
            if relative:
                (chosen, rests, excess), out = out[:3], out[3:]
                (flag,) = call(flag_kernel, [((1,), jnp.int32)], [excess])
        lam = out[0]
        if not last:
            outgoing, both, parts = out[1], out[2], out[3:]
    return jnp.transpose(lam, (1, 0, 2))


def solution(mesh):
    return jax.shard_map(
        per_device,
        mesh=mesh,
        in_specs=(
            P(("gx", "gy", "gz"), None, None),
            P(None, ("gx", "gy", "gz"), None, None),
            P(("gx", "gy", "gz")),
            P(),
            P(("gx", "gy", "gz"), None),
            P(("gx", "gy", "gz"), None, None),
            P(("gx", "gy", "gz"), None, None),
        ),
        out_specs=P(("gx", "gy", "gz"), None, None),
        check_vma=False,
    )
```
